32 devices in a mesh: fsdp: 4 (over z), seq: 8 (over y, x, core).
Axes of the slice: x: 2, y: 2, z: 4, core: 2. Of those that a mesh axis runs over, the one named last changes fastest.
Arguments:
- layer_input: bfloat16 [8192, 2048], P(('fsdp', 'seq')), may hold values from -6 to 6
- lengths: int32 [4, 4], P('fsdp'), may hold values from 32 to 2048, as said below
- norm1_gain: bfloat16 [2048], P(('fsdp', 'seq')), may hold values from 0.5 to 1.5
- w_x: bfloat16 [2048, 2560], P(('fsdp', 'seq')), may hold values from -0.125 to 0.125
- w_y: bfloat16 [2048, 2560], P(('fsdp', 'seq')), may hold values from -0.125 to 0.125
- conv_w: bfloat16 [2560, 4], P(('fsdp', 'seq')), may hold values from -3 to 3
- conv_b: bfloat16 [2560], P(('fsdp', 'seq')), may hold values from -2 to 2
- w_rgate: bfloat16 [2560, 160], P(('fsdp', 'seq')), may hold values from -0.5 to 0.5
- b_rgate: bfloat16 [2560], P(('fsdp', 'seq')), may hold values from -3 to 3
- w_igate: bfloat16 [2560, 160], P(('fsdp', 'seq')), may hold values from -0.5 to 0.5
- b_igate: bfloat16 [2560], P(('fsdp', 'seq')), may hold values from -3 to 3
- lam: bfloat16 [2560], P(('fsdp', 'seq')), may hold values from 3 to 14
- w_out: bfloat16 [2560, 2048], P(('fsdp', 'seq')), may hold values from -0.25 to 0.25
- norm2_gain: bfloat16 [2048], P(('fsdp', 'seq')), may hold values from 0.5 to 1.5
- w_gate: bfloat16 [2048, 6144], P(('fsdp', 'seq')), may hold values from -0.125 to 0.125
- w_up: bfloat16 [2048, 6144], P(('fsdp', 'seq')), may hold values from -0.125 to 0.125
- w_down: bfloat16 [6144, 2048], P(('fsdp', 'seq')), may hold values from -0.15625 to 0.15625
- cot: bfloat16 [8192, 2048], P(('fsdp', 'seq')), may hold values from -6 to 6
Outputs:
- layer_output: bfloat16 [8192, 2048], P(('fsdp', 'seq'))
- d_x: bfloat16 [8192, 2048], P(('fsdp', 'seq'))
- d_norm1_gain: float32 [2048], P(('fsdp', 'seq'))
- d_w_x: float32 [2048, 2560], P(('fsdp', 'seq'))
- d_w_y: float32 [2048, 2560], P(('fsdp', 'seq'))
- d_conv_w: float32 [2560, 4], P(('fsdp', 'seq'))
- d_conv_b: float32 [2560], P(('fsdp', 'seq'))
- d_w_rgate: float32 [2560, 160], P(('fsdp', 'seq'))
- d_b_rgate: float32 [2560], P(('fsdp', 'seq'))
- d_w_igate: float32 [2560, 160], P(('fsdp', 'seq'))
- d_b_igate: float32 [2560], P(('fsdp', 'seq'))
- d_lam: float32 [2560], P(('fsdp', 'seq'))
- d_w_out: float32 [2560, 2048], P(('fsdp', 'seq'))
- d_norm2_gain: float32 [2048], P(('fsdp', 'seq'))
- d_w_gate: float32 [2048, 6144], P(('fsdp', 'seq'))
- d_w_up: float32 [2048, 6144], P(('fsdp', 'seq'))
- d_w_down: float32 [6144, 2048], P(('fsdp', 'seq'))
The draws below stay inside these ranges and needn't reach their ends.
Inputs may be any that keep to these rules, and one draw needn't show every extreme that they name: `lengths`: each row sums to 2048. One entry, at a place drawn from the seed, exceeds 2048 - 256; the others are at most (255) // 3, and the first of them equals 32.
All inputs are finite; a program needn't handle non-finite values.
Results may differ from the reference program's by a relative error of at most 0.013.
Values may be sent and summed in bfloat16 or wider, within the bound.
No kernel may reach another device: no remote copies, remote signals or barrier semaphores. Data moves between devices by JAX's collectives and lax.ppermute only.
A program may use at most 448 MiB of HBM per device.

```python
import jax
import jax.numpy as jnp
from jax import lax

D = 2048
BLOCK = 160
FF = 6144
CONV = 4
SEQS = 4
MIN_LEN = 32
TOK_DEV = 256
RW = 2560
GROUP = 2048
TOKENS = 8192
N_FSDP = 4


def draw_lengths(key, part):
    key_short = jax.random.fold_in(key, 11)
    key_place = jax.random.fold_in(key, 12)
    most_short = (TOK_DEV - 1) // (SEQS - 1)
    shorts = jax.random.randint(key_short, (N_FSDP, SEQS - 1), MIN_LEN, most_short + 1, dtype=jnp.int32)
    shorts = shorts.at[:, 0].set(MIN_LEN)
    longest = GROUP - jnp.sum(shorts, axis=1, keepdims=True)
    place = jax.random.randint(key_place, (N_FSDP, 1), 0, SEQS, dtype=jnp.int32)
    column = jnp.arange(SEQS, dtype=jnp.int32)[None, :]
    source = jnp.clip(column - (column > place).astype(jnp.int32), 0, SEQS - 2)
    picked = jnp.take_along_axis(shorts, source, axis=1)
    return jnp.where(column == place, longest, picked).astype(jnp.int32)


def draw_lam(key, part):
    key_kind = jax.random.fold_in(key, 21)
    key_slow = jax.random.fold_in(key, 22)
    key_fast = jax.random.fold_in(key, 23)
    share = 0.5
    kind = jax.random.uniform(key_kind, (RW,), jnp.float32)
    slow_low = jnp.log(0.05 / GROUP)
    slow_high = jnp.log(0.5 / GROUP)
    slow = jnp.exp(jax.random.uniform(key_slow, (RW,), jnp.float32, slow_low, slow_high))
    fast = jnp.exp(jax.random.uniform(key_fast, (RW,), jnp.float32, jnp.log(0.005), jnp.log(0.02)))
    rate = jnp.where(kind < share, slow, fast)
    return (-jnp.log(jnp.expm1(rate))).astype(jnp.bfloat16)


def raised(drawn, rng, source, target, shards_of, factor):
    def block_of(position):
        return (jnp.arange(drawn.shape[position]) // (drawn.shape[position] // shards_of)).reshape((-1,) + (1,) * (drawn.ndim - 1 - position))

    one_side = jax.random.permutation(rng, shards_of)[block_of(target)]
    second = (block_of(target) + shards_of // 2) % shards_of
    return jnp.where((block_of(source) == one_side) | (block_of(source) == second), factor * drawn, drawn)


def block_levels(stream_key, extent, shards, smallest, high):
    def one(position, parts):
        heights = jax.random.uniform(jax.random.fold_in(jax.random.fold_in(stream_key, 6), position), (parts,), jnp.float32, smallest / len(shards), high / len(shards))
        return jnp.repeat(jnp.exp(heights), extent[position] // parts).reshape((-1,) + (1,) * (len(extent) - position - 1))

    factor_of = one(*shards[0])
    for cut in shards[1:]:
        factor_of = factor_of * one(*cut)
    return factor_of


def centred(stream_key, dims, scale, most, split=(), kind=jnp.bfloat16):
    level = block_levels(stream_key, dims, split, -0.22, 0.18) if split else 1.0
    entries = jax.random.normal(stream_key, dims, jnp.float32) * scale * level
    return jnp.minimum(jnp.maximum(entries, -most), most).astype(kind)


def noise_with(rng, extent, spread, most, pieces, heavy, kind=jnp.bfloat16):
    entries = spread * jax.random.normal(rng, extent, jnp.float32)
    if pieces:
        entries = entries * block_levels(rng, extent, pieces, -0.22, 0.18)
    return jnp.clip(raised(entries, jax.random.fold_in(rng, 3), *heavy), -most, most).astype(kind)


def setup_inputs(seed: int = 0) -> dict:
    streams_of = jax.random.split(jax.random.key(seed), 19)
    return {
        "layer_input": centred(streams_of[0], (TOKENS, D), 1.0, 6.0, ((0, 32),)),
        "lengths": draw_lengths(jax.random.fold_in(streams_of[18], 71), 0),
        "norm1_gain": jnp.clip(1.0 + 0.1 * jax.random.normal(streams_of[2], (D,), jnp.float32), 0.5, 1.5).astype(jnp.bfloat16),
        "w_x": centred(streams_of[3], (D, RW), D ** -0.5, 0.125, ((0, 32),)),
        "w_y": centred(streams_of[4], (D, RW), D ** -0.5, 0.125, ((0, 32),)),
        "conv_w": centred(streams_of[5], (RW, CONV), 0.5, 3.0, ((0, 32),)),
        "conv_b": centred(streams_of[6], (RW,), 0.3, 2.0, ((0, 32),)),
        "w_rgate": centred(streams_of[7], (RW, BLOCK), BLOCK ** -0.5, 0.5, ((0, 32),)),
        "b_rgate": centred(streams_of[8], (RW,), 0.5, 3.0, ((0, 32),)),
        "w_igate": centred(streams_of[9], (RW, BLOCK), BLOCK ** -0.5, 0.5, ((0, 32),)),
        "b_igate": centred(streams_of[10], (RW,), 0.5, 3.0, ((0, 32),)),
        "lam": draw_lam(jax.random.fold_in(streams_of[18], 71), 0),
        "w_out": centred(streams_of[12], (RW, D), (RW // 4) ** -0.5, 0.25, ((0, 32),)),
        "norm2_gain": jnp.clip(1.0 + 0.1 * jax.random.normal(streams_of[13], (D,), jnp.float32), 0.5, 1.5).astype(jnp.bfloat16),
        "w_gate": centred(streams_of[14], (D, FF), D ** -0.5, 0.125, ((0, 32),)),
        "w_up": centred(streams_of[15], (D, FF), D ** -0.5, 0.125, ((0, 32),)),
        "w_down": centred(streams_of[16], (FF, D), (FF // 4) ** -0.5, 0.15625, ((0, 32),)),
        "cot": noise_with(streams_of[17], (TOKENS, D), 1.0, 6.0, ((0, 32),), (0, 1, 32, 2.75)),
    }


DECAY_C = 8.0
NORM_EPS = 1e-06

@jax.custom_vjp
def low(v):
    return lax.optimization_barrier(v.astype(jnp.bfloat16)).astype(jnp.float32)

@jax.custom_vjp
def low_back(v):
    return v

def low_keep(v):
    return (low(v), None)

def low_pass(kept, grad):
    return (grad,)

def back_keep(v):
    return (v, None)

def back_low(kept, grad):
    return (low(grad),)
low.defvjp(low_keep, low_pass)
low_back.defvjp(back_keep, back_low)

def matmul(left, right):
    return jnp.dot(left, right, precision=lax.Precision.HIGHEST, preferred_element_type=jnp.float32)

def rms_apply(value, gain):
    scale = lax.rsqrt(lax.optimization_barrier(jnp.mean(value * value, axis=-1, keepdims=True)) + NORM_EPS)
    return value * scale * gain

def combine(earlier, later):
    return (earlier[0] * later[0], later[0] * earlier[1] + later[1])

def lru_terms(pre_r, pre_i, lam_vec, conv_out, start):
    rate = jax.nn.softplus(-lam_vec)
    log_a = -DECAY_C * jax.nn.sigmoid(pre_r) * rate
    decay = jnp.where(start[:, None], 0.0, jnp.exp(log_a))
    scale = jnp.sqrt(jnp.maximum(-jnp.expm1(2.0 * log_a), 0.2 * DECAY_C * rate))
    scale = jnp.where(start[:, None], 1.0, scale)
    return (decay, scale * jax.nn.sigmoid(pre_i) * conv_out)

def block_product(value, weight):
    blocks = weight.shape[0] // weight.shape[1]
    width = weight.shape[1]
    vals = value.reshape(value.shape[0], blocks, width)
    mats = weight.reshape(blocks, width, width)
    return jnp.einsum('nhi,hij->nhj', vals, mats, precision=lax.Precision.HIGHEST).reshape(value.shape[0], -1)

def group_masks(lens_row):
    ends = jnp.cumsum(lens_row)
    starts = ends - lens_row
    place = jnp.arange(GROUP, dtype=jnp.int32)

    def segment(p):
        return lax.optimization_barrier(jnp.sum((p[:, None] >= starts[None, :]).astype(jnp.int32), axis=1))
    seg_now = segment(place)
    start = jnp.any(place[:, None] == starts[None, :], axis=1)
    same = jnp.stack([((segment(place - k) == seg_now) & (place - k >= 0)).astype(jnp.float32) for k in range(CONV)], 0)
    return (start, same)

def reference(layer_input, lengths, norm1_gain, w_x, w_y, conv_w, conv_b, w_rgate, b_rgate, w_igate, b_igate, lam, w_out, norm2_gain, w_gate, w_up, w_down, cot):
    starts_all, same_all = jax.vmap(group_masks)(lengths)
    params = tuple((v.astype(jnp.float32) for v in (norm1_gain, w_x, w_y, conv_w, conv_b, w_rgate, b_rgate, w_igate, b_igate, lam, w_out, norm2_gain, w_gate, w_up, w_down)))

    def forward(xin, g1, wx, wy, cw, cb, wr, br, wi, bi, lamv, wo, g2, wg, wu, wd):

        def one_group(item):
            xg, start, same = item
            un = low(rms_apply(xg, g1))
            xb = low(low_back(matmul(un, wx)))
            yb = low_back(matmul(un, wy))
            gy = jax.nn.gelu(yb)
            padded = jnp.pad(xb, ((CONV - 1, 0), (0, 0)))
            conv = cb[None, :]
            for k in range(CONV):
                conv = conv + cw[:, k][None, :] * padded[CONV - 1 - k:CONV - 1 - k + GROUP] * same[k][:, None]
            xc = low(conv)
            pre_r = low_back(block_product(xc, wr) + br[None, :])
            pre_i = low_back(block_product(xc, wi) + bi[None, :])
            decay, drive = lru_terms(pre_r, pre_i, lamv, xc, start)
            state = lax.associative_scan(combine, (decay, drive), axis=0)[1]
            mixed = low(state * gy)
            resid = xg + low_back(matmul(mixed, wo))
            un2 = low(rms_apply(resid, g2))
            gate_pre = low_back(matmul(un2, wg))
            up_pre = low_back(matmul(un2, wu))
            hidden = low(jax.nn.gelu(gate_pre) * up_pre)
            return resid + low_back(matmul(hidden, wd))
        groups = xin.reshape(N_FSDP, GROUP, D)
        result = lax.map(jax.checkpoint(one_group), (groups, starts_all, same_all))
        return result.reshape(TOKENS, D)
    out, back = jax.vjp(forward, layer_input.astype(jnp.float32), *params)
    grads = back(cot.astype(jnp.float32))
    return (out.astype(jnp.bfloat16), grads[0].astype(jnp.bfloat16), grads[1], grads[2], grads[3], grads[4], grads[5], grads[6], grads[7], grads[8], grads[9], grads[10], grads[11], grads[12], grads[13], grads[14], grads[15])
```

```python
import functools

import jax
import jax.numpy as jnp
import numpy as np
from jax import lax
from jax.experimental import pallas as pl
from jax.experimental.pallas import tpu as pltpu
from jax.sharding import Mesh
from jax.sharding import PartitionSpec as P

DECAY_C = 8.0
NORM_EPS = 1e-06


def from_behind(x, axis, by):
    size = lax.axis_size(axis)
    pairs = [(i, i + by) for i in range(size) if 0 <= i + by < size]
    return lax.ppermute(x, axis, pairs)


def carried_in(value, axis, join, neutral, backward):
    count, mine = (lax.axis_size(axis), lax.axis_index(axis))
    pieces = jax.tree.map(lambda part: lax.all_gather(part, axis), value)
    if backward:
        pieces = jax.tree.map(lambda part: part[::-1], pieces)
        mine = count - 1 - mine
    subtotal = jax.tree.map(
        lambda part, zero: jnp.full_like(part, 0) + jnp.asarray(zero, part.dtype), value, neutral
    )

    def step(position, subtotal):
        longer = join(subtotal, jax.tree.map(lambda part: part[position], pieces))
        return jax.tree.map(lambda new, old: jnp.where(position < mine, new, old), longer, subtotal)

    return lax.fori_loop(0, count - 1, step, subtotal)


def rms_apply(value, gain):
    scale = lax.rsqrt(jnp.mean(value * value, axis=-1, keepdims=True) + NORM_EPS)
    return value * scale * gain


def combine(earlier, later):
    return (earlier[0] * later[0], later[0] * earlier[1] + later[1])


def lru_terms(pre_r, pre_i, lam_vec, conv_out, start):
    rate = jax.nn.softplus(-lam_vec)
    log_a = -DECAY_C * jax.nn.sigmoid(pre_r) * rate
    decay = jnp.where(start[:, None], 0.0, jnp.exp(log_a))
    scale = jnp.sqrt(jnp.maximum(-jnp.expm1(2.0 * log_a), 0.2 * DECAY_C * rate))
    scale = jnp.where(start[:, None], 1.0, scale)
    return (decay, scale * jax.nn.sigmoid(pre_i) * conv_out)


def row_contract(left, right):
    return lax.dot_general(
        left, right, (((0,), (0,)), ((), ())), preferred_element_type=jnp.float32
    )


def back_product(grad, weight):
    return lax.dot_general(
        grad, weight, (((1,), (1,)), ((), ())), preferred_element_type=jnp.float32
    )


def split_blocks(value, width):
    return value.reshape(value.shape[0], value.shape[1] // width, width)


def block_product(value, weight):
    width = weight.shape[1]
    mats = weight.reshape(weight.shape[0] // width, width, width)
    result = jnp.einsum(
        "nhi,hij->nhj", split_blocks(value, width), mats, preferred_element_type=jnp.float32
    )
    return result.reshape(value.shape[0], -1)


def block_back(grad, weight):
    width = weight.shape[1]
    mats = weight.reshape(weight.shape[0] // width, width, width)
    result = jnp.einsum(
        "nhj,hij->nhi", split_blocks(grad, width), mats, preferred_element_type=jnp.float32
    )
    return result.reshape(grad.shape[0], -1)


def gate_grad(value, grad, width):
    result = jnp.einsum(
        "nhi,nhj->hij",
        split_blocks(value, width),
        split_blocks(grad, width),
        preferred_element_type=jnp.float32,
    )
    return result.reshape(value.shape[1], width)


def seq_starts(lens_row):
    count = lens_row.shape[0]
    before = jnp.arange(count)[None, :] < jnp.arange(count)[:, None]
    return jnp.sum(jnp.where(before, lens_row[None, :], 0), axis=1)


def seq_masks(lens_row, first, rows, taps):
    starts = seq_starts(lens_row)
    place = first + jnp.arange(rows, dtype=jnp.int32)

    def segment(p):
        return jnp.sum((p[:, None] >= starts[None, :]).astype(jnp.int32), axis=1)

    seg_now = segment(place)
    start = jnp.any(place[:, None] == starts[None, :], axis=1)
    same = jnp.stack(
        [
            ((segment(place - k) == seg_now) & (place - k >= 0)).astype(jnp.float32)
            for k in range(taps)
        ],
        0,
    )
    return (start, same)


def on_device(
    layer_input,
    lengths,
    norm1_gain,
    w_x,
    w_y,
    conv_w,
    conv_b,
    w_rgate,
    b_rgate,
    w_igate,
    b_igate,
    lam,
    w_out,
    norm2_gain,
    w_gate,
    w_up,
    w_down,
    cot,
):
    rows = layer_input.shape[0]
    taps = conv_w.shape[1]
    width = w_rgate.shape[1]
    rim = taps - 1
    index = lax.axis_index("seq")
    start, same = seq_masks(lengths[0], index * rows, rows, taps)
    gain_one, wx, wy, cw, cb, wr, br, wi, bi, lam_all, wo = (
        lax.all_gather(norm1_gain, ("fsdp", "seq"), axis=0, tiled=True),
        lax.all_gather(w_x, ("fsdp", "seq"), axis=0, tiled=True),
        lax.all_gather(w_y, ("fsdp", "seq"), axis=0, tiled=True),
        lax.all_gather(conv_w, ("fsdp", "seq"), axis=0, tiled=True),
        lax.all_gather(conv_b, ("fsdp", "seq"), axis=0, tiled=True),
        lax.all_gather(w_rgate, ("fsdp", "seq"), axis=0, tiled=True),
        lax.all_gather(b_rgate, ("fsdp", "seq"), axis=0, tiled=True),
        lax.all_gather(w_igate, ("fsdp", "seq"), axis=0, tiled=True),
        lax.all_gather(b_igate, ("fsdp", "seq"), axis=0, tiled=True),
        lax.all_gather(lam, ("fsdp", "seq"), axis=0, tiled=True),
        lax.all_gather(w_out, ("fsdp", "seq"), axis=0, tiled=True),
    )
    xf = layer_input.astype(jnp.float32)
    gain1 = gain_one.astype(jnp.float32)
    un = rms_apply(xf, gain1).astype(jnp.bfloat16)
    xb = jnp.dot(un, wx, preferred_element_type=jnp.float32).astype(jnp.bfloat16)
    yb = jnp.dot(un, wy, preferred_element_type=jnp.float32)
    gy = jax.nn.gelu(yb)
    rim_in = from_behind(xb[rows - rim :], "seq", 1)
    extended = jnp.concatenate([rim_in, xb], axis=0).astype(jnp.float32)
    cwf = cw.astype(jnp.float32)
    conv = jnp.broadcast_to(cb.astype(jnp.float32)[None, :], (rows, cwf.shape[0]))
    for k in range(taps):
        conv = conv + cwf[:, k][None, :] * extended[rim - k : rim - k + rows] * same[k][:, None]
    xc = conv.astype(jnp.bfloat16)
    xcf = xc.astype(jnp.float32)
    pre_r = block_product(xc, wr) + br.astype(jnp.float32)[None, :]
    pre_i = block_product(xc, wi) + bi.astype(jnp.float32)[None, :]
    lamf = lam_all.astype(jnp.float32)
    decay, drive = lru_terms(pre_r, pre_i, lamf, xcf, start)
    decay_cum, state_loc = lax.associative_scan(combine, (decay, drive), axis=0)
    zero_vec = jnp.zeros((decay.shape[1],), jnp.float32)
    one_vec = jnp.ones((decay.shape[1],), jnp.float32)
    state_in = carried_in(
        (decay_cum[-1], state_loc[-1]), "seq", combine, (one_vec, zero_vec), False
    )[1]
    state = state_loc + decay_cum * state_in[None, :]
    state_prev = jnp.concatenate([state_in[None, :], state[:-1]], axis=0)
    mixed = (state * gy).astype(jnp.bfloat16)
    resid = xf + jnp.dot(mixed, wo, preferred_element_type=jnp.float32)
    gain_two, wg, wu, wd = (
        lax.all_gather(norm2_gain, ("fsdp", "seq"), axis=0, tiled=True),
        lax.all_gather(w_gate, ("fsdp", "seq"), axis=0, tiled=True),
        lax.all_gather(w_up, ("fsdp", "seq"), axis=0, tiled=True),
        lax.all_gather(w_down, ("fsdp", "seq"), axis=0, tiled=True),
    )
    gain2 = gain_two.astype(jnp.float32)
    un2 = rms_apply(resid, gain2).astype(jnp.bfloat16)
    gate_pre = jnp.dot(un2, wg, preferred_element_type=jnp.float32)
    up_pre = jnp.dot(un2, wu, preferred_element_type=jnp.float32)
    gate_act, gelu_back = jax.vjp(jax.nn.gelu, gate_pre)
    hidden = (gate_act * up_pre).astype(jnp.bfloat16)
    output = (resid + jnp.dot(hidden, wd, preferred_element_type=jnp.float32)).astype(jnp.bfloat16)
    grad = cot.astype(jnp.float32)
    gain_two, wg, wu, wd = (
        lax.all_gather(norm2_gain, ("fsdp", "seq"), axis=0, tiled=True),
        lax.all_gather(w_gate, ("fsdp", "seq"), axis=0, tiled=True),
        lax.all_gather(w_up, ("fsdp", "seq"), axis=0, tiled=True),
        lax.all_gather(w_down, ("fsdp", "seq"), axis=0, tiled=True),
    )
    gain2 = gain_two.astype(jnp.float32)
    d_wd = row_contract(hidden, cot)
    d_hidden = back_product(cot, wd)
    d_gate = gelu_back(d_hidden * up_pre)[0].astype(jnp.bfloat16)
    d_up = (d_hidden * gate_act).astype(jnp.bfloat16)
    d_wg = row_contract(un2, d_gate)
    d_wu = row_contract(un2, d_up)
    d_un2 = back_product(d_gate, wg) + back_product(d_up, wu)
    norm_two_back = jax.vjp(rms_apply, resid, gain2)[1]
    d_resid_norm, d_gain2 = norm_two_back(d_un2)
    mlp_grads = (
        lax.psum_scatter(d_gain2, ("fsdp", "seq"), scatter_dimension=0, tiled=True),
        lax.psum_scatter(d_wg, ("fsdp", "seq"), scatter_dimension=0, tiled=True),
        lax.psum_scatter(d_wu, ("fsdp", "seq"), scatter_dimension=0, tiled=True),
        lax.psum_scatter(d_wd, ("fsdp", "seq"), scatter_dimension=0, tiled=True),
    )
    d_resid = grad + d_resid_norm
    gain_one, wx, wy, cw, cb, wr, br, wi, bi, lam_all, wo = (
        lax.all_gather(norm1_gain, ("fsdp", "seq"), axis=0, tiled=True),
        lax.all_gather(w_x, ("fsdp", "seq"), axis=0, tiled=True),
        lax.all_gather(w_y, ("fsdp", "seq"), axis=0, tiled=True),
        lax.all_gather(conv_w, ("fsdp", "seq"), axis=0, tiled=True),
        lax.all_gather(conv_b, ("fsdp", "seq"), axis=0, tiled=True),
        lax.all_gather(w_rgate, ("fsdp", "seq"), axis=0, tiled=True),
        lax.all_gather(b_rgate, ("fsdp", "seq"), axis=0, tiled=True),
        lax.all_gather(w_igate, ("fsdp", "seq"), axis=0, tiled=True),
        lax.all_gather(b_igate, ("fsdp", "seq"), axis=0, tiled=True),
        lax.all_gather(lam, ("fsdp", "seq"), axis=0, tiled=True),
        lax.all_gather(w_out, ("fsdp", "seq"), axis=0, tiled=True),
    )
    gain1 = gain_one.astype(jnp.float32)
    cwf = cw.astype(jnp.float32)
    lamf = lam_all.astype(jnp.float32)
    d_mix = d_resid.astype(jnp.bfloat16)
    d_wo = row_contract(mixed, d_mix)
    d_mixed = back_product(d_mix, wo)
    d_state = d_mixed * gy
    gelu_y_back = jax.vjp(jax.nn.gelu, yb)[1]
    d_yb = gelu_y_back(d_mixed * state)[0].astype(jnp.bfloat16)
    next_decay = jnp.concatenate([decay[1:], one_vec[None, :]], axis=0)
    decay_after, adjoint_loc = lax.associative_scan(
        combine, (next_decay, d_state), reverse=True, axis=0
    )
    send_decay = decay[0] * decay_after[0]
    send_adjoint = decay[0] * adjoint_loc[0]
    adjoint_in = carried_in((send_decay, send_adjoint), "seq", combine, (one_vec, zero_vec), True)[
        1
    ]
    adjoint = adjoint_loc + decay_after * adjoint_in[None, :]

    def local_lru(pr, pi, lv, cv):
        return lru_terms(pr, pi, lv, cv, start)

    lru_back = jax.vjp(local_lru, pre_r, pre_i, lamf, xcf)[1]
    d_pre_r, d_pre_i, d_lam, d_xc_local = lru_back((adjoint * state_prev, adjoint))
    d_pr = d_pre_r.astype(jnp.bfloat16)
    d_pi = d_pre_i.astype(jnp.bfloat16)
    d_wr = gate_grad(xc, d_pr, width)
    d_wi = gate_grad(xc, d_pi, width)
    d_br = jnp.sum(d_pr.astype(jnp.float32), axis=0)
    d_bi = jnp.sum(d_pi.astype(jnp.float32), axis=0)
    d_xc = d_xc_local + block_back(d_pr, wr) + block_back(d_pi, wi)
    d_cb = jnp.sum(d_xc, axis=0)
    d_cw = jnp.stack(
        [
            jnp.sum(d_xc * extended[rim - k : rim - k + rows] * same[k][:, None], axis=0)
            for k in range(taps)
        ],
        axis=1,
    )
    d_extended = jnp.zeros((rows + rim, d_xc.shape[1]), jnp.float32)
    for k in range(taps):
        d_extended = d_extended + jnp.pad(
            d_xc * cwf[:, k][None, :] * same[k][:, None], ((rim - k, k), (0, 0))
        )
    rim_back = from_behind(d_extended[:rim], "seq", -1)
    d_xb = (d_extended[rim:] + jnp.pad(rim_back, ((rows - rim, 0), (0, 0)))).astype(jnp.bfloat16)
    d_wx = row_contract(un, d_xb)
    d_wy = row_contract(un, d_yb)
    d_un = back_product(d_xb, wx) + back_product(d_yb, wy)
    norm_one_back = jax.vjp(rms_apply, xf, gain1)[1]
    d_x_norm, d_gain1 = norm_one_back(d_un)
    d_input = (d_resid + d_x_norm).astype(jnp.bfloat16)
    block_grads = (
        lax.psum_scatter(d_gain1, ("fsdp", "seq"), scatter_dimension=0, tiled=True),
        lax.psum_scatter(d_wx, ("fsdp", "seq"), scatter_dimension=0, tiled=True),
        lax.psum_scatter(d_wy, ("fsdp", "seq"), scatter_dimension=0, tiled=True),
        lax.psum_scatter(d_cw, ("fsdp", "seq"), scatter_dimension=0, tiled=True),
        lax.psum_scatter(d_cb, ("fsdp", "seq"), scatter_dimension=0, tiled=True),
        lax.psum_scatter(d_wr, ("fsdp", "seq"), scatter_dimension=0, tiled=True),
        lax.psum_scatter(d_br, ("fsdp", "seq"), scatter_dimension=0, tiled=True),
        lax.psum_scatter(d_wi, ("fsdp", "seq"), scatter_dimension=0, tiled=True),
        lax.psum_scatter(d_bi, ("fsdp", "seq"), scatter_dimension=0, tiled=True),
        lax.psum_scatter(d_lam, ("fsdp", "seq"), scatter_dimension=0, tiled=True),
        lax.psum_scatter(d_wo, ("fsdp", "seq"), scatter_dimension=0, tiled=True),
    )
    return (
        output,
        d_input,
        block_grads[0],
        block_grads[1],
        block_grads[2],
        block_grads[3],
        block_grads[4],
        block_grads[5],
        block_grads[6],
        block_grads[7],
        block_grads[8],
        block_grads[9],
        block_grads[10],
        mlp_grads[0],
        mlp_grads[1],
        mlp_grads[2],
        mlp_grads[3],
    )


NAMES = ("zh", "zl", "y", "x", "c")
F32 = jnp.float32
BF16 = jnp.bfloat16
GELU_C = 0.7978845608
GELU_K = 0.044715


def swap(v, name):
    return lax.ppermute(v, name, [(0, 1), (1, 0)])


def add16(one, two):
    return (one.astype(F32) + two.astype(F32)).astype(BF16)


def act_gather(v, a, b):
    h = v.shape[0] // 2
    near, from_a, from_b = swap(v, "c"), swap(v, a), swap(v, b)
    far0, far1 = swap(from_a[:h], b), swap(from_b[h:], a)
    near_a, near_b = swap(from_a, "c"), swap(from_b, "c")
    far = jnp.concatenate([far0, far1], axis=0)
    return [v, near, from_a, near_a, from_b, near_b, far, swap(far, "c")]


def act_scatter(get, a, b):
    far, to_a, to_b = [add16(get(k), swap(get(k + 1), "c")) for k in (6, 2, 4)]
    own = get(0).astype(F32) + swap(get(1), "c").astype(F32)
    h = far.shape[0] // 2
    in_b, in_a = swap(far[:h], b), swap(far[h:], a)
    to_a = jnp.concatenate([add16(to_a[:h], in_b), to_a[h:]], axis=0)
    to_b = jnp.concatenate([to_b[:h], add16(to_b[h:], in_a)], axis=0)
    return own + swap(to_a, a).astype(F32) + swap(to_b, b).astype(F32)


def w_gather(v, w1, w2):
    i1, i2 = lax.axis_index(w1), lax.axis_index(w2)
    p1, p2 = swap(v, w1), swap(v, w2)
    p12 = swap(p1, w2)
    out = jnp.zeros((2, 2) + v.shape, v.dtype)
    tail = (0,) * v.ndim
    for part, j1, j2 in ((v, i1, i2), (p1, 1 - i1, i2), (p2, i1, 1 - i2), (p12, 1 - i1, 1 - i2)):
        out = lax.dynamic_update_slice(out, part[None, None], (j1, j2) + tail)
    return out


def w_scatter(v, w1, w2):
    i1, i2 = lax.axis_index(w1), lax.axis_index(w2)

    def get(j1, j2):
        return lax.dynamic_slice(v, (j1, j2) + (0,) * (v.ndim - 2), (1, 1) + v.shape[2:])[0, 0]

    other = add16(get(1 - i1, i2), swap(get(1 - i1, 1 - i2), w2))
    own = get(i1, i2).astype(F32) + swap(get(i1, 1 - i2), w2).astype(F32)
    return own + swap(other, w1).astype(F32)


def to_columns(w, tp, rest):
    rows, cols = w.shape
    dims = {n: i + 1 for i, n in enumerate(NAMES)}
    v = w.reshape((rows,) + (2,) * 5 + (cols // 32,))
    v = v.transpose([dims[n] for n in tp] + [0] + [dims[n] for n in rest] + [6])
    return v.reshape(8, rows, cols // 8)


def from_columns(v, tp, rest):
    _, rows, cols = v.shape
    order = list(tp) + ["rows"] + list(rest)
    v = v.reshape((2, 2, 2, rows, 2, 2, cols // 4))
    v = v.transpose([order.index("rows")] + [order.index(n) for n in NAMES] + [6])
    return v.reshape(rows, cols * 8)


def exchange(v, tp):
    return lax.all_to_all(v, tp, split_axis=0, concat_axis=0, tiled=True)


def neg_expm1(v):
    series = 1.0 + v * (1.0 / 10.0)
    for n in range(9, 1, -1):
        series = 1.0 + v * (1.0 / n) * series
    return jnp.where(v > -0.5, -v * series, 1.0 - jnp.exp(v))


def gate_terms(pa, px, rate, start):
    sr = jax.nn.sigmoid(pa)
    si = jax.nn.sigmoid(px)
    la = -DECAY_C * sr * rate
    decay = jnp.where(start, 0.0, jnp.exp(la))
    e2 = neg_expm1(2.0 * la)
    floor = 0.2 * DECAY_C * rate
    scale = jnp.where(start, 1.0, jnp.sqrt(jnp.maximum(e2, floor)))
    return sr, si, decay, e2, floor, scale


def gelu(v):
    return 0.5 * v * (1.0 + jnp.tanh(GELU_C * (v + GELU_K * v * v * v)))


def gelu_both(v):
    t = jnp.tanh(GELU_C * (v + GELU_K * v * v * v))
    half = 0.5 * (1.0 + t)
    return v * half, half + 0.5 * v * (1.0 - t * t) * GELU_C * (1.0 + 3.0 * GELU_K * v * v)


def scan_tile(decay, drive, into):
    row = lax.broadcasted_iota(jnp.int32, decay.shape, 0)
    for by in (1, 2, 4):
        keep = row >= by
        drive = jnp.where(keep, decay * pltpu.roll(drive, by, 0) + drive, drive)
        decay = jnp.where(keep, decay * pltpu.roll(decay, by, 0), decay)
    return decay * into + drive


def scan_tile_back(decay, drive, into):
    row = lax.broadcasted_iota(jnp.int32, decay.shape, 0)
    for by in (1, 2, 4):
        keep = row < 8 - by
        drive = jnp.where(keep, decay * pltpu.roll(drive, 8 - by, 0) + drive, drive)
        decay = jnp.where(keep, decay * pltpu.roll(decay, 8 - by, 0), decay)
    return decay * into + drive


STEP = 16


def rec_fwd_kernel(xb_ref, yb_ref, mask_ref, vec_ref, w_ref, xc_ref, pa_ref, px_ref, sp_ref, mixed_ref, ext, carry):
    rows, width = xb_ref.shape

    @pl.when(pl.program_id(0) == 0)
    def _():
        ext[0:8, :] = jnp.zeros((8, width), F32)
        carry[...] = jnp.zeros_like(carry)

    ext[8 : 8 + rows, :] = xb_ref[...].astype(F32)

    def conv_step(r, _):
        at = pl.multiple_of(r * STEP, STEP)
        window = ext[pl.ds(at, STEP + 8), :]
        mask = mask_ref[pl.ds(at, STEP), :]
        total = vec_ref[4:5, :] + vec_ref[0:1, :] * window[8:, :]
        for k in range(1, 4):
            total = total + vec_ref[k : k + 1, :] * window[8 - k : 8 - k + STEP, :] * mask[:, k : k + 1]
        xc_ref[pl.ds(at, STEP), :] = total.astype(BF16)
        return 0

    lax.fori_loop(0, rows // STEP, conv_step, 0, unroll=2)
    ext[0:8, :] = ext[rows : rows + 8, :]
    xc = xc_ref[...]
    pa_ref[...] = jnp.dot(xc, w_ref[:, :width], preferred_element_type=F32) + vec_ref[6:7, :]
    px_ref[...] = jnp.dot(xc, w_ref[:, width:], preferred_element_type=F32) + vec_ref[7:8, :]
    top = lax.broadcasted_iota(jnp.int32, (8, width), 0) == 0

    def scan_step(r, held):
        here = pl.ds(pl.multiple_of(r * STEP, STEP), STEP)
        start = jnp.broadcast_to(mask_ref[here, 0:1], (STEP, width)) > 0.5
        _, si, decay, _, _, scale = gate_terms(pa_ref[here, :], px_ref[here, :], vec_ref[5:6, :], start)
        drive = scale * si * xc_ref[here, :].astype(F32)
        states, before = [], []
        for part in range(0, STEP, 8):
            now = scan_tile(decay[part : part + 8], drive[part : part + 8], held)
            states.append(now)
            before.append(jnp.where(top, held, pltpu.roll(now, 1, 0)))
            held = jnp.broadcast_to(now[7:8, :], (8, width))
        sp_ref[here, :] = jnp.concatenate(before, axis=0)
        mixed_ref[here, :] = (jnp.concatenate(states, axis=0) * gelu(yb_ref[here, :])).astype(BF16)
        return held

    carry[...] = lax.fori_loop(0, rows // STEP, scan_step, carry[...], unroll=2)


def rec_bwd_kernel(
    dm_ref, yb_ref, sp_ref, pa_ref, px_ref, xc_ref, xb_ref, mask_ref, vec_ref, wt_ref,
    dxb_ref, dyb_ref, dw_ref, sum_ref, ext, dp, carry,
):
    rows, width = xb_ref.shape

    @pl.when(pl.program_id(0) == 0)
    def _():
        ext[rows : rows + 8, :] = jnp.zeros((8, width), F32)
        carry[...] = jnp.zeros_like(carry)
        dw_ref[...] = jnp.zeros_like(dw_ref)
        sum_ref[...] = jnp.zeros_like(sum_ref)

    row = lax.broadcasted_iota(jnp.int32, (8, width), 0)
    steps = rows // STEP

    def fold(v):
        return v[0:8, :] + v[8:16, :]

    def scan_step(i, state):
        held, s_rate, s_r, s_i = state
        here = pl.ds(pl.multiple_of((steps - 1 - i) * STEP, STEP), STEP)
        start = jnp.broadcast_to(mask_ref[here, 0:1], (STEP, width)) > 0.5
        rate = vec_ref[5:6, :]
        sr, si, decay, e2, floor, scale = gate_terms(pa_ref[here, :], px_ref[here, :], rate, start)
        xc = xc_ref[here, :].astype(F32)
        before = sp_ref[here, :]
        gate = si * xc
        now = decay * before + scale * gate
        dm = dm_ref[here, :]
        act, slope = gelu_both(yb_ref[here, :])
        dyb_ref[here, :] = (dm * now * slope).astype(BF16)
        dstate = dm * act
        parts = []
        for part in range(STEP - 8, -1, -8):
            here_decay = decay[part : part + 8]
            coef = jnp.where(row == 7, 1.0, pltpu.roll(here_decay, 7, 0))
            adj = scan_tile_back(coef, dstate[part : part + 8], held)
            held = jnp.broadcast_to((here_decay * adj)[0:1, :], (8, width))
            parts.append(adj)
        adj = jnp.concatenate(parts[::-1], axis=0)
        d_scale = adj * gate
        d_half = jnp.where(start, 0.0, d_scale * 0.5 / scale)
        share = jnp.where(e2 > floor, 1.0, jnp.where(e2 == floor, 0.5, 0.0))
        kept = adj * scale
        d_la = decay * (adj * before - 2.0 * decay * d_half * share)
        d_rate = -DECAY_C * sr * d_la + (0.2 * DECAY_C) * d_half * (1.0 - share)
        d_pa = (-DECAY_C * rate * d_la * sr * (1.0 - sr)).astype(BF16)
        d_px = (kept * xc * si * (1.0 - si)).astype(BF16)
        dp[here, :width] = d_pa
        dp[here, width:] = d_px
        ext[here, :] = kept * si
        return held, s_rate + fold(d_rate), s_r + fold(d_pa.astype(F32)), s_i + fold(d_px.astype(F32))

    held, s_rate, s_r, s_i = lax.fori_loop(
        0, steps, scan_step, (carry[...], sum_ref[40:48, :], sum_ref[48:56, :], sum_ref[56:64, :]), unroll=2
    )
    carry[...] = held
    sum_ref[40:48, :] = s_rate
    sum_ref[48:56, :] = s_r
    sum_ref[56:64, :] = s_i
    ext[0:rows, :] += jnp.dot(dp[...], wt_ref[...], preferred_element_type=F32)
    dw_ref[...] += row_contract(xc_ref[...], dp[...])

    def conv_step(r, sums):
        at = pl.multiple_of(r * STEP, STEP)
        window = ext[pl.ds(at, STEP + 8), :]
        mask = mask_ref[pl.ds(at, STEP), :]
        xb = xb_ref[pl.ds(at, STEP), :].astype(F32)
        total = jnp.zeros((STEP, width), F32)
        new = []
        for k in range(4):
            moved = window[k : k + STEP, :]
            if k:
                moved = moved * mask[:, 3 + k : 4 + k]
            total = total + vec_ref[k : k + 1, :] * moved
            new.append(sums[k] + fold(moved * xb))
        new.append(sums[4] + fold(window[:STEP, :]))
        dxb_ref[pl.ds(at, STEP), :] = total.astype(BF16)
        return tuple(new)

    sums = lax.fori_loop(0, steps, conv_step, tuple(sum_ref[8 * q : 8 * q + 8, :] for q in range(5)), unroll=2)
    for q in range(5):
        sum_ref[8 * q : 8 * q + 8, :] = sums[q]
    ext[rows : rows + 8, :] = ext[0:8, :]


def time_tile(total):
    return 256 if total % 256 == 0 else total


def rec_forward(xb, yb, mask, vec, w):
    total, width = xb.shape
    tile = time_tile(total)
    block = pl.BlockSpec((tile, width), lambda i: (i, 0))
    whole = lambda v: pl.BlockSpec(v.shape, lambda i: (0, 0))
    return pl.pallas_call(
        rec_fwd_kernel,
        grid=(total // tile,),
        in_specs=[block, block, pl.BlockSpec((tile, 8), lambda i: (i, 0)), whole(vec), whole(w)],
        out_specs=[block] * 5,
        out_shape=[jax.ShapeDtypeStruct((total, width), t) for t in (BF16, F32, F32, F32, BF16)],
        scratch_shapes=[pltpu.VMEM((tile + 8, width), F32), pltpu.VMEM((8, width), F32)],
        compiler_params=pltpu.CompilerParams(vmem_limit_bytes=32 << 20),
        cost_estimate=pl.CostEstimate(
            flops=100 * total * width + 4 * total * width * width,
            transcendentals=6 * total * width,
            bytes_accessed=22 * total * width,
        ),
        name="recurrence_forward",
    )(xb, yb, mask, vec, w)


def rec_backward(dm, yb, sp, pa, px, xc, xb, mask, vec, wt):
    total, width = xb.shape
    tile = time_tile(total)
    steps = total // tile
    block = pl.BlockSpec((tile, width), lambda i: (steps - 1 - i, 0))
    whole = lambda v: pl.BlockSpec(v.shape, lambda i: (0, 0))
    return pl.pallas_call(
        rec_bwd_kernel,
        grid=(steps,),
        in_specs=[block] * 7 + [pl.BlockSpec((tile, 8), lambda i: (steps - 1 - i, 0)), whole(vec), whole(wt)],
        out_specs=[
            block,
            block,
            pl.BlockSpec((width, 2 * width), lambda i: (0, 0)),
            pl.BlockSpec((64, width), lambda i: (0, 0)),
        ],
        out_shape=[
            jax.ShapeDtypeStruct((total, width), BF16),
            jax.ShapeDtypeStruct((total, width), BF16),
            jax.ShapeDtypeStruct((width, 2 * width), F32),
            jax.ShapeDtypeStruct((64, width), F32),
        ],
        scratch_shapes=[
            pltpu.VMEM((tile + 8, width), F32),
            pltpu.VMEM((tile, 2 * width), BF16),
            pltpu.VMEM((8, width), F32),
        ],
        compiler_params=pltpu.CompilerParams(vmem_limit_bytes=32 << 20),
        cost_estimate=pl.CostEstimate(
            flops=180 * total * width + 8 * total * width * width,
            transcendentals=6 * total * width,
            bytes_accessed=28 * total * width,
        ),
        name="recurrence_backward",
    )(dm, yb, sp, pa, px, xc, xb, mask, vec, wt)


def place_masks(lens_row, total, taps):
    start, same = seq_masks(lens_row, 0, total, taps)
    cols = [start.astype(F32)] + [same[k] for k in range(1, taps)]
    cols += [jnp.pad(same[k][k:], (0, k)) for k in range(1, taps)]
    return jnp.pad(jnp.stack(cols, axis=1), ((0, 0), (0, 8 - len(cols))))


def dot32(one, two):
    return jnp.dot(one, two, preferred_element_type=F32)


def norm_back(dv, v, scale):
    return scale * dv - scale * scale * scale * v * jnp.mean(dv * v, axis=-1, keepdims=True)


REC_TP = ("y", "x", "c")
REC_COLS = (("y", "x", "zh"), ("zl", "c"))
REC_W = ("zh", "zl")
FF_A, FF_B = "x", "y"
FF_TP = ("y", "x", "c")
FF_W = ("zh", "zl")


def tensor_parallel(
    layer_input, lengths, norm1_gain, w_x, w_y, conv_w, conv_b, w_rgate, b_rgate, w_igate, b_igate, lam,
    w_out, norm2_gain, w_gate, w_up, w_down, cot,
):
    rows, model = layer_input.shape
    total = 8 * rows
    taps = conv_w.shape[1]
    width = w_rgate.shape[1]
    part = w_out.shape[0]
    channels = 4 * part
    padded = -(-channels // 128) * 128
    extra = padded - channels
    blocks = channels // width
    core = lax.axis_index("c")
    me = (lax.axis_index("y") * 2 + lax.axis_index("x")) * 2 + core

    def in_order(pieces):
        out = jnp.zeros((8,) + pieces[0].shape, pieces[0].dtype)
        for k, piece in enumerate(pieces):
            out = lax.dynamic_update_slice(out, piece[None], (me ^ k, 0, 0))
        return out.reshape(total, -1)

    def rows_of(v, k):
        return lax.dynamic_slice(v, ((me ^ k) * rows, 0), (rows, v.shape[1]))

    gain1 = norm1_gain.astype(F32)[:, None]
    gain2 = norm2_gain.astype(F32)[:, None]

    xf = layer_input.astype(F32)
    scale1 = lax.rsqrt(jnp.mean(xf * xf, axis=-1, keepdims=True) + NORM_EPS)
    xs = (xf * scale1).astype(BF16)

    def columns_in(w, gain, cols, tp, over):
        scaled = (w.astype(F32) * gain).astype(BF16)
        mine = exchange(to_columns(scaled, *cols), tp)
        return w_gather(mine.reshape(-1, mine.shape[2]), *over).reshape(model, -1)

    def columns_out(grad, cols, tp, over):
        mine = w_scatter(grad.astype(BF16).reshape(2, 2, model // 4, -1), *over).astype(BF16)
        return from_columns(exchange(mine.reshape(8, -1, mine.shape[1]), tp), *cols).astype(F32)

    wx = jnp.pad(columns_in(w_x, gain1, REC_COLS, REC_TP, REC_W), ((0, 0), (0, extra)))
    xs_all = in_order(act_gather(xs, "x", "y"))
    wy = jnp.pad(columns_in(w_y, gain1, REC_COLS, REC_TP, REC_W), ((0, 0), (0, extra)))

    small = [conv_w, conv_b[:, None], b_rgate[:, None], b_igate[:, None], lam[:, None], w_rgate, w_igate]
    small_width = sum(v.shape[1] for v in small)
    packed = jnp.pad(jnp.concatenate([w_out] + small, axis=1), ((0, 0), (0, -small_width % 128)))
    halves = w_gather(packed, *REC_W)
    mine = lax.dynamic_slice(halves, (core, 0, 0, 0), (1,) + halves.shape[1:])[0]
    theirs = swap(lax.dynamic_slice(halves, (1 - core, 0, 0, 0), (1,) + halves.shape[1:])[0], "c")
    whole = jnp.zeros((2, 2) + packed.shape, BF16)
    whole = lax.dynamic_update_slice(whole, mine[:, None], (0, core, 0, 0))
    whole = lax.dynamic_update_slice(whole, theirs[:, None], (0, 1 - core, 0, 0))
    whole = jnp.pad(whole.reshape(channels, -1), ((0, extra), (0, 0)))
    wo = whole[:, :model]
    rest = whole[:, model : model + taps + 4].astype(F32).T
    lam_all = rest[taps + 3]
    vec = jnp.concatenate([rest[: taps + 1], jax.nn.softplus(-lam_all)[None], rest[taps + 1 : taps + 3]], axis=0)
    at = model + taps + 4
    gates = jnp.zeros((padded, 2 * padded), BF16)
    for g in range(2):
        for n in range(blocks):
            block = whole[n * width : (n + 1) * width, at + g * width : at + (g + 1) * width]
            gates = gates.at[n * width : (n + 1) * width, g * padded + n * width : g * padded + (n + 1) * width].set(block)
    mask = place_masks(lengths[0], total, taps)

    xb = dot32(xs_all, wx).astype(BF16)
    yb = dot32(xs_all, wy)
    xc, pa, px, before, mixed = rec_forward(xb, yb, mask, vec, gates)

    resid = xf + act_scatter(lambda k: dot32(rows_of(mixed, k), wo).astype(BF16), "x", "y")
    scale2 = lax.rsqrt(jnp.mean(resid * resid, axis=-1, keepdims=True) + NORM_EPS)
    xs2 = (resid * scale2).astype(BF16)

    wg = columns_in(w_gate, gain2, (FF_TP, FF_W), FF_TP, FF_W)
    wu = columns_in(w_up, gain2, (FF_TP, FF_W), FF_TP, FF_W)
    wd = w_gather(w_down, *FF_W).reshape(-1, model)
    cot_all = jnp.concatenate(act_gather(cot, FF_A, FF_B), axis=0)
    xs2_all = jnp.concatenate(act_gather(xs2, FF_A, FF_B), axis=0)
    gt = dot32(xs2_all, wg)
    up = dot32(xs2_all, wu)
    act, slope = gelu_both(gt)
    hidden = (act * up).astype(BF16)

    def tile_of(v, k):
        return v[k * rows : (k + 1) * rows]

    output = (resid + act_scatter(lambda k: dot32(tile_of(hidden, k), wd).astype(BF16), FF_A, FF_B)).astype(BF16)

    d_hidden = back_product(cot_all, wd)
    d_gt = (d_hidden * up * slope).astype(BF16)
    d_up = (d_hidden * act).astype(BF16)
    d_un2 = act_scatter(
        lambda k: (back_product(tile_of(d_gt, k), wg) + back_product(tile_of(d_up, k), wu)).astype(BF16), FF_A, FF_B
    )
    d_wd = w_scatter(row_contract(hidden, cot_all).astype(BF16).reshape(2, 2, -1, model), *FF_W)
    d_wg = columns_out(row_contract(xs2_all, d_gt), (FF_TP, FF_W), FF_TP, FF_W)
    d_wu = columns_out(row_contract(xs2_all, d_up), (FF_TP, FF_W), FF_TP, FF_W)
    d_gain2 = jnp.sum(w_gate.astype(F32) * d_wg + w_up.astype(F32) * d_wu, axis=1)

    d_resid = cot.astype(F32) + norm_back(d_un2, resid, scale2)
    d_mix = d_resid.astype(BF16)
    d_mix_all = in_order(act_gather(d_mix, "x", "y"))
    dm = back_product(d_mix_all, wo)
    dxb, dyb, d_gates, sums = rec_backward(dm, yb, before, pa, px, xc, xb, mask, vec, gates.T)
    d_un = act_scatter(
        lambda k: (back_product(rows_of(dxb, k), wx) + back_product(rows_of(dyb, k), wy)).astype(BF16), "x", "y"
    )
    d_input = (d_resid + norm_back(d_un, xf, scale1)).astype(BF16)

    d_wo = row_contract(mixed, d_mix_all)[:channels]
    d_wx = columns_out(row_contract(xs_all, dxb)[:, :channels], REC_COLS, REC_TP, REC_W)
    d_wy = columns_out(row_contract(xs_all, dyb)[:, :channels], REC_COLS, REC_TP, REC_W)
    d_gain1 = jnp.sum(w_x.astype(F32) * d_wx + w_y.astype(F32) * d_wy, axis=1)

    def channels_out(v, kind):
        v = v.astype(kind).reshape(2, 2, part, -1)
        size = (2, 1) + v.shape[2:]
        keep = lax.dynamic_slice(v, (0, core, 0, 0), size)[:, 0]
        send = lax.dynamic_slice(v, (0, 1 - core, 0, 0), size)[:, 0]
        out = jnp.zeros((2,) + keep.shape, kind)
        out = lax.dynamic_update_slice(out, keep[None], (core, 0, 0, 0))
        return lax.dynamic_update_slice(out, swap(send, "c")[None], (1 - core, 0, 0, 0))

    d_wo = w_scatter(channels_out(d_wo, BF16), *REC_W)
    sums = jnp.sum(sums.reshape(8, 8, padded), axis=1)
    d_lam_part = -jax.nn.sigmoid(-lam_all) * sums[5]
    d_cols = jnp.concatenate([sums[:5], sums[6:8], d_lam_part[None]], axis=0).T
    row_block = jnp.arange(channels)[:, None] // width
    d_blocks = []
    for g in range(2):
        block = d_gates[:channels, g * padded : g * padded + width]
        for n in range(1, blocks):
            at = g * padded + n * width
            block = jnp.where(row_block == n, d_gates[:channels, at : at + width], block)
        d_blocks.append(block)
    d_small = jnp.concatenate([d_cols[:channels]] + d_blocks, axis=1)
    d_small = lax.psum_scatter(channels_out(d_small, F32).reshape(4 * part, -1), REC_W, scatter_dimension=0, tiled=True)
    d_cw, d_cb, d_br, d_bi, d_lam = d_small[:, :4], d_small[:, 4], d_small[:, 5], d_small[:, 6], d_small[:, 7]
    d_wr, d_wi = d_small[:, 8 : 8 + width], d_small[:, 8 + width : 8 + 2 * width]
    return (
        output, d_input, d_gain1, gain1 * d_wx, gain1 * d_wy, d_cw, d_cb, d_wr, d_br, d_wi, d_bi, d_lam, d_wo,
        d_gain2, gain2 * d_wg, gain2 * d_wu, d_wd,
    )


def factored(mesh):
    if tuple(mesh.axis_names) != ("fsdp", "seq") or (mesh.shape["fsdp"], mesh.shape["seq"]) != (4, 8):
        return None
    return Mesh(np.asarray(mesh.devices).reshape((2,) * 5), NAMES)


def solution(mesh):
    small = factored(mesh)
    if small is not None:
        whole, groups = P(NAMES), P(("zh", "zl"))
        return jax.shard_map(
            tensor_parallel,
            mesh=small,
            in_specs=(whole, groups) + (whole,) * 16,
            out_specs=(whole,) * 17,
            check_vma=False,
        )
    in_specs = (
        P(("fsdp", "seq"), None),
        P("fsdp", None),
        P(("fsdp", "seq")),
        P(("fsdp", "seq"), None),
        P(("fsdp", "seq"), None),
        P(("fsdp", "seq"), None),
        P(("fsdp", "seq")),
        P(("fsdp", "seq"), None),
        P(("fsdp", "seq")),
        P(("fsdp", "seq"), None),
        P(("fsdp", "seq")),
        P(("fsdp", "seq")),
        P(("fsdp", "seq"), None),
        P(("fsdp", "seq")),
        P(("fsdp", "seq"), None),
        P(("fsdp", "seq"), None),
        P(("fsdp", "seq"), None),
        P(("fsdp", "seq"), None),
    )
    out_specs = (
        P(("fsdp", "seq"), None),
        P(("fsdp", "seq"), None),
        P(("fsdp", "seq")),
        P(("fsdp", "seq"), None),
        P(("fsdp", "seq"), None),
        P(("fsdp", "seq"), None),
        P(("fsdp", "seq")),
        P(("fsdp", "seq"), None),
        P(("fsdp", "seq")),
        P(("fsdp", "seq"), None),
        P(("fsdp", "seq")),
        P(("fsdp", "seq")),
        P(("fsdp", "seq"), None),
        P(("fsdp", "seq")),
        P(("fsdp", "seq"), None),
        P(("fsdp", "seq"), None),
        P(("fsdp", "seq"), None),
    )
    return jax.shard_map(
        on_device, mesh=mesh, in_specs=in_specs, out_specs=out_specs, check_vma=False
    )
```

```python
import functools

import jax
import jax.numpy as jnp
import numpy as np
from jax import lax
from jax.experimental import pallas as pl
from jax.experimental.pallas import tpu as pltpu
from jax.sharding import Mesh
from jax.sharding import PartitionSpec as P

DECAY_C = 8.0
NORM_EPS = 1e-06


def from_behind(x, axis, by):
    size = lax.axis_size(axis)
    pairs = [(i, i + by) for i in range(size) if 0 <= i + by < size]
    return lax.ppermute(x, axis, pairs)


def carried_in(value, axis, join, neutral, backward):
    count, mine = (lax.axis_size(axis), lax.axis_index(axis))
    pieces = jax.tree.map(lambda part: lax.all_gather(part, axis), value)
    if backward:
        pieces = jax.tree.map(lambda part: part[::-1], pieces)
        mine = count - 1 - mine
    subtotal = jax.tree.map(
        lambda part, zero: jnp.full_like(part, 0) + jnp.asarray(zero, part.dtype), value, neutral
    )

    def step(position, subtotal):
        longer = join(subtotal, jax.tree.map(lambda part: part[position], pieces))
        return jax.tree.map(lambda new, old: jnp.where(position < mine, new, old), longer, subtotal)

    return lax.fori_loop(0, count - 1, step, subtotal)


def rms_apply(value, gain):
    scale = lax.rsqrt(jnp.mean(value * value, axis=-1, keepdims=True) + NORM_EPS)
    return value * scale * gain


def combine(earlier, later):
    return (earlier[0] * later[0], later[0] * earlier[1] + later[1])


def lru_terms(pre_r, pre_i, lam_vec, conv_out, start):
    rate = jax.nn.softplus(-lam_vec)
    log_a = -DECAY_C * jax.nn.sigmoid(pre_r) * rate
    decay = jnp.where(start[:, None], 0.0, jnp.exp(log_a))
    scale = jnp.sqrt(jnp.maximum(-jnp.expm1(2.0 * log_a), 0.2 * DECAY_C * rate))
    scale = jnp.where(start[:, None], 1.0, scale)
    return (decay, scale * jax.nn.sigmoid(pre_i) * conv_out)


def row_contract(left, right):
    return lax.dot_general(
        left, right, (((0,), (0,)), ((), ())), preferred_element_type=jnp.float32
    )


def back_product(grad, weight):
    return lax.dot_general(
        grad, weight, (((1,), (1,)), ((), ())), preferred_element_type=jnp.float32
    )


def split_blocks(value, width):
    return value.reshape(value.shape[0], value.shape[1] // width, width)


def block_product(value, weight):
    width = weight.shape[1]
    mats = weight.reshape(weight.shape[0] // width, width, width)
    result = jnp.einsum(
        "nhi,hij->nhj", split_blocks(value, width), mats, preferred_element_type=jnp.float32
    )
    return result.reshape(value.shape[0], -1)


def block_back(grad, weight):
    width = weight.shape[1]
    mats = weight.reshape(weight.shape[0] // width, width, width)
    result = jnp.einsum(
        "nhj,hij->nhi", split_blocks(grad, width), mats, preferred_element_type=jnp.float32
    )
    return result.reshape(grad.shape[0], -1)


def gate_grad(value, grad, width):
    result = jnp.einsum(
        "nhi,nhj->hij",
        split_blocks(value, width),
        split_blocks(grad, width),
        preferred_element_type=jnp.float32,
    )
    return result.reshape(value.shape[1], width)


def seq_starts(lens_row):
    count = lens_row.shape[0]
    before = jnp.arange(count)[None, :] < jnp.arange(count)[:, None]
    return jnp.sum(jnp.where(before, lens_row[None, :], 0), axis=1)


def seq_masks(lens_row, first, rows, taps):
    starts = seq_starts(lens_row)
    place = first + jnp.arange(rows, dtype=jnp.int32)

    def segment(p):
        return jnp.sum((p[:, None] >= starts[None, :]).astype(jnp.int32), axis=1)

    seg_now = segment(place)
    start = jnp.any(place[:, None] == starts[None, :], axis=1)
    same = jnp.stack(
        [
            ((segment(place - k) == seg_now) & (place - k >= 0)).astype(jnp.float32)
            for k in range(taps)
        ],
        0,
    )
    return (start, same)


def on_device(
    layer_input,
    lengths,
    norm1_gain,
    w_x,
    w_y,
    conv_w,
    conv_b,
    w_rgate,
    b_rgate,
    w_igate,
    b_igate,
    lam,
    w_out,
    norm2_gain,
    w_gate,
    w_up,
    w_down,
    cot,
):
    rows = layer_input.shape[0]
    taps = conv_w.shape[1]
    width = w_rgate.shape[1]
    rim = taps - 1
    index = lax.axis_index("seq")
    start, same = seq_masks(lengths[0], index * rows, rows, taps)
    gain_one, wx, wy, cw, cb, wr, br, wi, bi, lam_all, wo = (
        lax.all_gather(norm1_gain, ("fsdp", "seq"), axis=0, tiled=True),
        lax.all_gather(w_x, ("fsdp", "seq"), axis=0, tiled=True),
        lax.all_gather(w_y, ("fsdp", "seq"), axis=0, tiled=True),
        lax.all_gather(conv_w, ("fsdp", "seq"), axis=0, tiled=True),
        lax.all_gather(conv_b, ("fsdp", "seq"), axis=0, tiled=True),
        lax.all_gather(w_rgate, ("fsdp", "seq"), axis=0, tiled=True),
        lax.all_gather(b_rgate, ("fsdp", "seq"), axis=0, tiled=True),
        lax.all_gather(w_igate, ("fsdp", "seq"), axis=0, tiled=True),
        lax.all_gather(b_igate, ("fsdp", "seq"), axis=0, tiled=True),
        lax.all_gather(lam, ("fsdp", "seq"), axis=0, tiled=True),
        lax.all_gather(w_out, ("fsdp", "seq"), axis=0, tiled=True),
    )
    xf = layer_input.astype(jnp.float32)
    gain1 = gain_one.astype(jnp.float32)
    un = rms_apply(xf, gain1).astype(jnp.bfloat16)
    xb = jnp.dot(un, wx, preferred_element_type=jnp.float32).astype(jnp.bfloat16)
    yb = jnp.dot(un, wy, preferred_element_type=jnp.float32)
    gy = jax.nn.gelu(yb)
    rim_in = from_behind(xb[rows - rim :], "seq", 1)
    extended = jnp.concatenate([rim_in, xb], axis=0).astype(jnp.float32)
    cwf = cw.astype(jnp.float32)
    conv = jnp.broadcast_to(cb.astype(jnp.float32)[None, :], (rows, cwf.shape[0]))
    for k in range(taps):
        conv = conv + cwf[:, k][None, :] * extended[rim - k : rim - k + rows] * same[k][:, None]
    xc = conv.astype(jnp.bfloat16)
    xcf = xc.astype(jnp.float32)
    pre_r = block_product(xc, wr) + br.astype(jnp.float32)[None, :]
    pre_i = block_product(xc, wi) + bi.astype(jnp.float32)[None, :]
    lamf = lam_all.astype(jnp.float32)
    decay, drive = lru_terms(pre_r, pre_i, lamf, xcf, start)
    decay_cum, state_loc = lax.associative_scan(combine, (decay, drive), axis=0)
    zero_vec = jnp.zeros((decay.shape[1],), jnp.float32)
    one_vec = jnp.ones((decay.shape[1],), jnp.float32)
    state_in = carried_in(
        (decay_cum[-1], state_loc[-1]), "seq", combine, (one_vec, zero_vec), False
    )[1]
    state = state_loc + decay_cum * state_in[None, :]
    state_prev = jnp.concatenate([state_in[None, :], state[:-1]], axis=0)
    mixed = (state * gy).astype(jnp.bfloat16)
    resid = xf + jnp.dot(mixed, wo, preferred_element_type=jnp.float32)
    gain_two, wg, wu, wd = (
        lax.all_gather(norm2_gain, ("fsdp", "seq"), axis=0, tiled=True),
        lax.all_gather(w_gate, ("fsdp", "seq"), axis=0, tiled=True),
        lax.all_gather(w_up, ("fsdp", "seq"), axis=0, tiled=True),
        lax.all_gather(w_down, ("fsdp", "seq"), axis=0, tiled=True),
    )
    gain2 = gain_two.astype(jnp.float32)
    un2 = rms_apply(resid, gain2).astype(jnp.bfloat16)
    gate_pre = jnp.dot(un2, wg, preferred_element_type=jnp.float32)
    up_pre = jnp.dot(un2, wu, preferred_element_type=jnp.float32)
    gate_act, gelu_back = jax.vjp(jax.nn.gelu, gate_pre)
    hidden = (gate_act * up_pre).astype(jnp.bfloat16)
    output = (resid + jnp.dot(hidden, wd, preferred_element_type=jnp.float32)).astype(jnp.bfloat16)
    grad = cot.astype(jnp.float32)
    gain_two, wg, wu, wd = (
        lax.all_gather(norm2_gain, ("fsdp", "seq"), axis=0, tiled=True),
        lax.all_gather(w_gate, ("fsdp", "seq"), axis=0, tiled=True),
        lax.all_gather(w_up, ("fsdp", "seq"), axis=0, tiled=True),
        lax.all_gather(w_down, ("fsdp", "seq"), axis=0, tiled=True),
    )
    gain2 = gain_two.astype(jnp.float32)
    d_wd = row_contract(hidden, cot)
    d_hidden = back_product(cot, wd)
    d_gate = gelu_back(d_hidden * up_pre)[0].astype(jnp.bfloat16)
    d_up = (d_hidden * gate_act).astype(jnp.bfloat16)
    d_wg = row_contract(un2, d_gate)
    d_wu = row_contract(un2, d_up)
    d_un2 = back_product(d_gate, wg) + back_product(d_up, wu)
    norm_two_back = jax.vjp(rms_apply, resid, gain2)[1]
    d_resid_norm, d_gain2 = norm_two_back(d_un2)
    mlp_grads = (
        lax.psum_scatter(d_gain2, ("fsdp", "seq"), scatter_dimension=0, tiled=True),
        lax.psum_scatter(d_wg, ("fsdp", "seq"), scatter_dimension=0, tiled=True),
        lax.psum_scatter(d_wu, ("fsdp", "seq"), scatter_dimension=0, tiled=True),
        lax.psum_scatter(d_wd, ("fsdp", "seq"), scatter_dimension=0, tiled=True),
    )
    d_resid = grad + d_resid_norm
    gain_one, wx, wy, cw, cb, wr, br, wi, bi, lam_all, wo = (
        lax.all_gather(norm1_gain, ("fsdp", "seq"), axis=0, tiled=True),
        lax.all_gather(w_x, ("fsdp", "seq"), axis=0, tiled=True),
        lax.all_gather(w_y, ("fsdp", "seq"), axis=0, tiled=True),
        lax.all_gather(conv_w, ("fsdp", "seq"), axis=0, tiled=True),
        lax.all_gather(conv_b, ("fsdp", "seq"), axis=0, tiled=True),
        lax.all_gather(w_rgate, ("fsdp", "seq"), axis=0, tiled=True),
        lax.all_gather(b_rgate, ("fsdp", "seq"), axis=0, tiled=True),
        lax.all_gather(w_igate, ("fsdp", "seq"), axis=0, tiled=True),
        lax.all_gather(b_igate, ("fsdp", "seq"), axis=0, tiled=True),
        lax.all_gather(lam, ("fsdp", "seq"), axis=0, tiled=True),
        lax.all_gather(w_out, ("fsdp", "seq"), axis=0, tiled=True),
    )
    gain1 = gain_one.astype(jnp.float32)
    cwf = cw.astype(jnp.float32)
    lamf = lam_all.astype(jnp.float32)
    d_mix = d_resid.astype(jnp.bfloat16)
    d_wo = row_contract(mixed, d_mix)
    d_mixed = back_product(d_mix, wo)
    d_state = d_mixed * gy
    gelu_y_back = jax.vjp(jax.nn.gelu, yb)[1]
    d_yb = gelu_y_back(d_mixed * state)[0].astype(jnp.bfloat16)
    next_decay = jnp.concatenate([decay[1:], one_vec[None, :]], axis=0)
    decay_after, adjoint_loc = lax.associative_scan(
        combine, (next_decay, d_state), reverse=True, axis=0
    )
    send_decay = decay[0] * decay_after[0]
    send_adjoint = decay[0] * adjoint_loc[0]
    adjoint_in = carried_in((send_decay, send_adjoint), "seq", combine, (one_vec, zero_vec), True)[
        1
    ]
    adjoint = adjoint_loc + decay_after * adjoint_in[None, :]

    def local_lru(pr, pi, lv, cv):
        return lru_terms(pr, pi, lv, cv, start)

    lru_back = jax.vjp(local_lru, pre_r, pre_i, lamf, xcf)[1]
    d_pre_r, d_pre_i, d_lam, d_xc_local = lru_back((adjoint * state_prev, adjoint))
    d_pr = d_pre_r.astype(jnp.bfloat16)
    d_pi = d_pre_i.astype(jnp.bfloat16)
    d_wr = gate_grad(xc, d_pr, width)
    d_wi = gate_grad(xc, d_pi, width)
    d_br = jnp.sum(d_pr.astype(jnp.float32), axis=0)
    d_bi = jnp.sum(d_pi.astype(jnp.float32), axis=0)
    d_xc = d_xc_local + block_back(d_pr, wr) + block_back(d_pi, wi)
    d_cb = jnp.sum(d_xc, axis=0)
    d_cw = jnp.stack(
        [
            jnp.sum(d_xc * extended[rim - k : rim - k + rows] * same[k][:, None], axis=0)
            for k in range(taps)
        ],
        axis=1,
    )
    d_extended = jnp.zeros((rows + rim, d_xc.shape[1]), jnp.float32)
    for k in range(taps):
        d_extended = d_extended + jnp.pad(
            d_xc * cwf[:, k][None, :] * same[k][:, None], ((rim - k, k), (0, 0))
        )
    rim_back = from_behind(d_extended[:rim], "seq", -1)
    d_xb = (d_extended[rim:] + jnp.pad(rim_back, ((rows - rim, 0), (0, 0)))).astype(jnp.bfloat16)
    d_wx = row_contract(un, d_xb)
    d_wy = row_contract(un, d_yb)
    d_un = back_product(d_xb, wx) + back_product(d_yb, wy)
    norm_one_back = jax.vjp(rms_apply, xf, gain1)[1]
    d_x_norm, d_gain1 = norm_one_back(d_un)
    d_input = (d_resid + d_x_norm).astype(jnp.bfloat16)
    block_grads = (
        lax.psum_scatter(d_gain1, ("fsdp", "seq"), scatter_dimension=0, tiled=True),
        lax.psum_scatter(d_wx, ("fsdp", "seq"), scatter_dimension=0, tiled=True),
        lax.psum_scatter(d_wy, ("fsdp", "seq"), scatter_dimension=0, tiled=True),
        lax.psum_scatter(d_cw, ("fsdp", "seq"), scatter_dimension=0, tiled=True),
        lax.psum_scatter(d_cb, ("fsdp", "seq"), scatter_dimension=0, tiled=True),
        lax.psum_scatter(d_wr, ("fsdp", "seq"), scatter_dimension=0, tiled=True),
        lax.psum_scatter(d_br, ("fsdp", "seq"), scatter_dimension=0, tiled=True),
        lax.psum_scatter(d_wi, ("fsdp", "seq"), scatter_dimension=0, tiled=True),
        lax.psum_scatter(d_bi, ("fsdp", "seq"), scatter_dimension=0, tiled=True),
        lax.psum_scatter(d_lam, ("fsdp", "seq"), scatter_dimension=0, tiled=True),
        lax.psum_scatter(d_wo, ("fsdp", "seq"), scatter_dimension=0, tiled=True),
    )
    return (
        output,
        d_input,
        block_grads[0],
        block_grads[1],
        block_grads[2],
        block_grads[3],
        block_grads[4],
        block_grads[5],
        block_grads[6],
        block_grads[7],
        block_grads[8],
        block_grads[9],
        block_grads[10],
        mlp_grads[0],
        mlp_grads[1],
        mlp_grads[2],
        mlp_grads[3],
    )


NAMES = ("zh", "zl", "y", "x", "c")
F32 = jnp.float32
BF16 = jnp.bfloat16
GELU_C = 0.7978845608
GELU_K = 0.044715


def swap(v, name):
    return lax.ppermute(v, name, [(0, 1), (1, 0)])


def add16(one, two):
    return (one.astype(F32) + two.astype(F32)).astype(BF16)


def act_gather(v, a, b):
    h = v.shape[0] // 2
    near, from_a, from_b = swap(v, "c"), swap(v, a), swap(v, b)
    far0, far1 = swap(from_a[:h], b), swap(from_b[h:], a)
    near_a, near_b = swap(from_a, "c"), swap(from_b, "c")
    far = jnp.concatenate([far0, far1], axis=0)
    return [v, near, from_a, near_a, from_b, near_b, far, swap(far, "c")]


def act_scatter(get, a, b):
    far, to_a, to_b = [add16(get(k), swap(get(k + 1), "c")) for k in (6, 2, 4)]
    own = get(0).astype(F32) + swap(get(1), "c").astype(F32)
    h = far.shape[0] // 2
    in_b, in_a = swap(far[:h], b), swap(far[h:], a)
    to_a = jnp.concatenate([add16(to_a[:h], in_b), to_a[h:]], axis=0)
    to_b = jnp.concatenate([to_b[:h], add16(to_b[h:], in_a)], axis=0)
    return own + swap(to_a, a).astype(F32) + swap(to_b, b).astype(F32)


def w_gather(v, w1, w2):
    i1, i2 = lax.axis_index(w1), lax.axis_index(w2)
    p1, p2 = swap(v, w1), swap(v, w2)
    p12 = swap(p1, w2)
    out = jnp.zeros((2, 2) + v.shape, v.dtype)
    tail = (0,) * v.ndim
    for part, j1, j2 in ((v, i1, i2), (p1, 1 - i1, i2), (p2, i1, 1 - i2), (p12, 1 - i1, 1 - i2)):
        out = lax.dynamic_update_slice(out, part[None, None], (j1, j2) + tail)
    return out


def w_scatter(v, w1, w2):
    i1, i2 = lax.axis_index(w1), lax.axis_index(w2)

    def get(j1, j2):
        return lax.dynamic_slice(v, (j1, j2) + (0,) * (v.ndim - 2), (1, 1) + v.shape[2:])[0, 0]

    other = add16(get(1 - i1, i2), swap(get(1 - i1, 1 - i2), w2))
    own = get(i1, i2).astype(F32) + swap(get(i1, 1 - i2), w2).astype(F32)
    return own + swap(other, w1).astype(F32)


def pack_kernel(plan, a_ref, b_ref, gain_ref, out_ref):
    half = out_ref.shape[2] // 2
    for first, ref in ((0, a_ref), (half, b_ref)):
        scaled = (ref[...].astype(F32) * gain_ref[...]).astype(BF16)
        for dest, pieces in enumerate(plan):
            at = first
            for source, size in pieces:
                out_ref[dest, :, at : at + size] = scaled[:, source : source + size]
                at += size
            if at < first + half:
                out_ref[dest, :, at : first + half] = jnp.zeros((scaled.shape[0], first + half - at), BF16)


def unpack_kernel(plan, grad_ref, a_ref, b_ref, gain_ref, da_ref, db_ref, dgain_ref):
    half = grad_ref.shape[2] // 2
    total = jnp.zeros(dgain_ref.shape, F32)
    for first, ref, out in ((0, a_ref, da_ref), (half, b_ref, db_ref)):
        for dest, pieces in enumerate(plan):
            at = first
            for source, size in pieces:
                piece = grad_ref[dest, :, at : at + size].astype(F32)
                out[:, source : source + size] = piece * gain_ref[...]
                weight = ref[:, source : source + size].astype(F32)
                total = total + jnp.sum(piece * weight, axis=1, keepdims=True)
                at += size
    dgain_ref[...] = total


def pack_columns(plan, half, one, two, gain):
    return pl.pallas_call(
        functools.partial(pack_kernel, plan),
        out_shape=jax.ShapeDtypeStruct((8, one.shape[0], 2 * half), BF16),
        compiler_params=pltpu.CompilerParams(vmem_limit_bytes=24 << 20),
        cost_estimate=pl.CostEstimate(flops=4 * one.size, transcendentals=0, bytes_accessed=8 * one.size),
        name="pack_columns",
    )(one, two, gain)


def unpack_columns(plan, grad, one, two, gain):
    shape = jax.ShapeDtypeStruct(one.shape, F32)
    return pl.pallas_call(
        functools.partial(unpack_kernel, plan),
        out_shape=[shape, shape, jax.ShapeDtypeStruct((one.shape[0], 1), F32)],
        compiler_params=pltpu.CompilerParams(vmem_limit_bytes=24 << 20),
        cost_estimate=pl.CostEstimate(flops=8 * one.size, transcendentals=0, bytes_accessed=16 * one.size),
        name="unpack_columns",
    )(grad, one, two, gain)


def exchange(v, tp):
    return lax.all_to_all(v, tp, split_axis=0, concat_axis=0, tiled=True)


def neg_expm1(v):
    series = 1.0 + v * (1.0 / 10.0)
    for n in range(9, 1, -1):
        series = 1.0 + v * (1.0 / n) * series
    return jnp.where(v > -0.5, -v * series, 1.0 - jnp.exp(v))


def gate_terms(pa, px, rate, start):
    sr = jax.nn.sigmoid(pa)
    si = jax.nn.sigmoid(px)
    la = -DECAY_C * sr * rate
    decay = jnp.where(start, 0.0, jnp.exp(la))
    e2 = neg_expm1(2.0 * la)
    floor = 0.2 * DECAY_C * rate
    scale = jnp.where(start, 1.0, jnp.sqrt(jnp.maximum(e2, floor)))
    return sr, si, decay, e2, floor, scale


def gelu(v):
    return 0.5 * v * (1.0 + jnp.tanh(GELU_C * (v + GELU_K * v * v * v)))


def gelu_both(v):
    t = jnp.tanh(GELU_C * (v + GELU_K * v * v * v))
    half = 0.5 * (1.0 + t)
    return v * half, half + 0.5 * v * (1.0 - t * t) * GELU_C * (1.0 + 3.0 * GELU_K * v * v)


def scan_tile(decay, drive, into):
    row = lax.broadcasted_iota(jnp.int32, decay.shape, 0)
    for by in (1, 2, 4):
        keep = row >= by
        drive = jnp.where(keep, decay * pltpu.roll(drive, by, 0) + drive, drive)
        decay = jnp.where(keep, decay * pltpu.roll(decay, by, 0), decay)
    return decay * into + drive


def scan_tile_back(decay, drive, into):
    row = lax.broadcasted_iota(jnp.int32, decay.shape, 0)
    for by in (1, 2, 4):
        keep = row < 8 - by
        drive = jnp.where(keep, decay * pltpu.roll(drive, 8 - by, 0) + drive, drive)
        decay = jnp.where(keep, decay * pltpu.roll(decay, 8 - by, 0), decay)
    return decay * into + drive


STEP = 16


def since_start(meta_ref, place, width):
    at = place + lax.broadcasted_iota(jnp.int32, (STEP, 128), 0)
    since, start = at, 0
    for n in range(1, meta_ref.shape[0] - 1):
        start = start + meta_ref[n]
        since = jnp.where(at >= start, at - start, since)
    return jnp.concatenate([since] * (width // 128), axis=1)


def rec_fwd_kernel(meta_ref, xb_ref, yb_ref, vec_ref, w_ref, xc_ref, pa_ref, px_ref, sp_ref, mixed_ref, ext, carry):
    rows, width = xb_ref.shape
    base = pl.program_id(0) * rows

    @pl.when(pl.program_id(0) == 0)
    def _():
        ext[0:8, :] = jnp.zeros((8, width), F32)
        carry[...] = jnp.zeros_like(carry)

    ext[8 : 8 + rows, :] = xb_ref[...].astype(BF16).astype(F32)

    def conv_step(r, _):
        at = pl.multiple_of(r * STEP, STEP)
        window = ext[pl.ds(at, STEP + 8), :]
        since = since_start(meta_ref, base + at, width)
        total = vec_ref[4:5, :] + vec_ref[0:1, :] * window[8:, :]
        for k in range(1, 4):
            moved = jnp.where(since >= k, window[8 - k : 8 - k + STEP, :], 0.0)
            total = total + vec_ref[k : k + 1, :] * moved
        xc_ref[pl.ds(at, STEP), :] = total.astype(BF16)
        return 0

    lax.fori_loop(0, rows // STEP, conv_step, 0, unroll=2)
    ext[0:8, :] = ext[rows : rows + 8, :]
    xc = xc_ref[...]
    pa_ref[...] = jnp.dot(xc, w_ref[:, :width], preferred_element_type=F32) + vec_ref[6:7, :]
    px_ref[...] = jnp.dot(xc, w_ref[:, width:], preferred_element_type=F32) + vec_ref[7:8, :]
    top = lax.broadcasted_iota(jnp.int32, (8, width), 0) == 0

    def scan_step(r, held):
        here = pl.ds(pl.multiple_of(r * STEP, STEP), STEP)
        start = since_start(meta_ref, base + r * STEP, width) == 0
        _, si, decay, _, _, scale = gate_terms(pa_ref[here, :], px_ref[here, :], vec_ref[5:6, :], start)
        drive = scale * si * xc_ref[here, :].astype(F32)
        states, before = [], []
        for part in range(0, STEP, 8):
            now = scan_tile(decay[part : part + 8], drive[part : part + 8], held)
            states.append(now)
            before.append(jnp.where(top, held, pltpu.roll(now, 1, 0)))
            held = jnp.broadcast_to(now[7:8, :], (8, width))
        sp_ref[here, :] = jnp.concatenate(before, axis=0)
        mixed_ref[here, :] = (jnp.concatenate(states, axis=0) * gelu(yb_ref[here, :])).astype(BF16)
        return held

    carry[...] = lax.fori_loop(0, rows // STEP, scan_step, carry[...], unroll=2)


def rec_bwd_kernel(
    meta_ref, dm_ref, yb_ref, sp_ref, pa_ref, px_ref, xc_ref, xb_ref, vec_ref, wt_ref,
    dxy_ref, dw_ref, sum_ref, ext, dp, carry,
):
    rows, width = xb_ref.shape
    base = (pl.num_programs(0) - 1 - pl.program_id(0)) * rows

    @pl.when(pl.program_id(0) == 0)
    def _():
        ext[rows : rows + 8, :] = jnp.zeros((8, width), F32)
        carry[...] = jnp.zeros_like(carry)
        dw_ref[...] = jnp.zeros_like(dw_ref)
        sum_ref[...] = jnp.zeros_like(sum_ref)

    row = lax.broadcasted_iota(jnp.int32, (8, width), 0)
    steps = rows // STEP

    def fold(v):
        return v[0:8, :] + v[8:16, :]

    def scan_step(i, state):
        held, s_rate, s_r, s_i = state
        at = pl.multiple_of((steps - 1 - i) * STEP, STEP)
        here = pl.ds(at, STEP)
        start = since_start(meta_ref, base + at, width) == 0
        rate = vec_ref[5:6, :]
        sr, si, decay, e2, floor, scale = gate_terms(pa_ref[here, :], px_ref[here, :], rate, start)
        xc = xc_ref[here, :].astype(F32)
        before = sp_ref[here, :]
        gate = si * xc
        now = decay * before + scale * gate
        dm = dm_ref[here, :]
        act, slope = gelu_both(yb_ref[here, :])
        dxy_ref[here, width:] = (dm * now * slope).astype(BF16)
        dstate = dm * act
        parts = []
        for part in range(STEP - 8, -1, -8):
            here_decay = decay[part : part + 8]
            coef = jnp.where(row == 7, 1.0, pltpu.roll(here_decay, 7, 0))
            adj = scan_tile_back(coef, dstate[part : part + 8], held)
            held = jnp.broadcast_to((here_decay * adj)[0:1, :], (8, width))
            parts.append(adj)
        adj = jnp.concatenate(parts[::-1], axis=0)
        d_scale = adj * gate
        d_half = jnp.where(start, 0.0, d_scale * 0.5 / scale)
        share = jnp.where(e2 > floor, 1.0, jnp.where(e2 == floor, 0.5, 0.0))
        kept = adj * scale
        d_la = decay * (adj * before - 2.0 * decay * d_half * share)
        d_rate = -DECAY_C * sr * d_la + (0.2 * DECAY_C) * d_half * (1.0 - share)
        d_pa = (-DECAY_C * rate * d_la * sr * (1.0 - sr)).astype(BF16)
        d_px = (kept * xc * si * (1.0 - si)).astype(BF16)
        dp[here, :width] = d_pa
        dp[here, width:] = d_px
        ext[here, :] = kept * si
        return held, s_rate + fold(d_rate), s_r + fold(d_pa.astype(F32)), s_i + fold(d_px.astype(F32))

    held, s_rate, s_r, s_i = lax.fori_loop(
        0, steps, scan_step, (carry[...], sum_ref[40:48, :], sum_ref[48:56, :], sum_ref[56:64, :]), unroll=2
    )
    carry[...] = held
    sum_ref[40:48, :] = s_rate
    sum_ref[48:56, :] = s_r
    sum_ref[56:64, :] = s_i
    ext[0:rows, :] += jnp.dot(dp[...], wt_ref[...], preferred_element_type=F32)
    dw_ref[...] += row_contract(xc_ref[...], dp[...])

    def conv_step(r, sums):
        at = pl.multiple_of(r * STEP, STEP)
        window = ext[pl.ds(at, STEP + 8), :]
        xb = xb_ref[pl.ds(at, STEP), :].astype(BF16).astype(F32)
        total = jnp.zeros((STEP, width), F32)
        new = []
        for k in range(4):
            moved = window[k : k + STEP, :]
            if k:
                moved = jnp.where(since_start(meta_ref, base + at + k, width) >= k, moved, 0.0)
            total = total + vec_ref[k : k + 1, :] * moved
            new.append(sums[k] + fold(moved * xb))
        new.append(sums[4] + fold(window[:STEP, :]))
        dxy_ref[pl.ds(at, STEP), :width] = total.astype(BF16)
        return tuple(new)

    sums = lax.fori_loop(0, steps, conv_step, tuple(sum_ref[8 * q : 8 * q + 8, :] for q in range(5)), unroll=2)
    for q in range(5):
        sum_ref[8 * q : 8 * q + 8, :] = sums[q]
    ext[rows : rows + 8, :] = ext[0:8, :]


def rec_forward(meta, xy, vec, w, tile):
    total, width = xy.shape[0], xy.shape[1] // 2
    block = pl.BlockSpec((tile, width), lambda i, m: (i ^ m[0], 0))
    right = pl.BlockSpec((tile, width), lambda i, m: (i ^ m[0], 1))
    whole = lambda v: pl.BlockSpec(v.shape, lambda i, m: (0, 0))
    return pl.pallas_call(
        rec_fwd_kernel,
        grid_spec=pltpu.PrefetchScalarGridSpec(
            num_scalar_prefetch=1,
            grid=(total // tile,),
            in_specs=[block, right, whole(vec), whole(w)],
            out_specs=[block] * 5,
            scratch_shapes=[pltpu.VMEM((tile + 8, width), F32), pltpu.VMEM((8, width), F32)],
        ),
        out_shape=[jax.ShapeDtypeStruct((total, width), t) for t in (BF16, F32, F32, F32, BF16)],
        compiler_params=pltpu.CompilerParams(vmem_limit_bytes=32 << 20),
        cost_estimate=pl.CostEstimate(
            flops=100 * total * width + 4 * total * width * width,
            transcendentals=6 * total * width,
            bytes_accessed=24 * total * width,
        ),
        name="recurrence_forward",
    )(meta, xy, xy, vec, w)


def rec_backward(meta, dm, xy, sp, pa, px, xc, vec, wt, tile):
    total, width = dm.shape
    steps = total // tile
    block = pl.BlockSpec((tile, width), lambda i, m: ((steps - 1 - i) ^ m[0], 0))
    right = pl.BlockSpec((tile, width), lambda i, m: ((steps - 1 - i) ^ m[0], 1))
    whole = lambda v: pl.BlockSpec(v.shape, lambda i, m: (0, 0))
    return pl.pallas_call(
        rec_bwd_kernel,
        grid_spec=pltpu.PrefetchScalarGridSpec(
            num_scalar_prefetch=1,
            grid=(steps,),
            in_specs=[block, right, block, block, block, block, block, whole(vec), whole(wt)],
            out_specs=[
                pl.BlockSpec((tile, 2 * width), lambda i, m: ((steps - 1 - i) ^ m[0], 0)),
                pl.BlockSpec((width, 2 * width), lambda i, m: (0, 0)),
                pl.BlockSpec((64, width), lambda i, m: (0, 0)),
            ],
            scratch_shapes=[
                pltpu.VMEM((tile + 8, width), F32),
                pltpu.VMEM((tile, 2 * width), BF16),
                pltpu.VMEM((8, width), F32),
            ],
        ),
        out_shape=[
            jax.ShapeDtypeStruct((total, 2 * width), BF16),
            jax.ShapeDtypeStruct((width, 2 * width), F32),
            jax.ShapeDtypeStruct((64, width), F32),
        ],
        compiler_params=pltpu.CompilerParams(vmem_limit_bytes=32 << 20),
        cost_estimate=pl.CostEstimate(
            flops=180 * total * width + 8 * total * width * width,
            transcendentals=6 * total * width,
            bytes_accessed=30 * total * width,
        ),
        name="recurrence_backward",
    )(meta, dm, xy, sp, pa, px, xc, xy, vec, wt)


def dot32(one, two):
    return jnp.dot(one, two, preferred_element_type=F32)


def norm_back(dv, v, scale):
    return scale * dv - scale * scale * scale * v * jnp.mean(dv * v, axis=-1, keepdims=True)


PLANE = ("y", "x", "c")
STACK = ("zh", "zl")


def tensor_parallel(
    layer_input, lengths, norm1_gain, w_x, w_y, conv_w, conv_b, w_rgate, b_rgate, w_igate, b_igate, lam,
    w_out, norm2_gain, w_gate, w_up, w_down, cot,
):
    rows, model = layer_input.shape
    taps = conv_w.shape[1]
    width = w_rgate.shape[1]
    part = w_out.shape[0]
    channels = 4 * part
    padded = -(-channels // 128) * 128
    extra = padded - channels
    blocks = channels // width
    units = w_down.shape[0]
    core = lax.axis_index("c")
    me = (lax.axis_index("y") * 2 + lax.axis_index("x")) * 2 + core
    meta = jnp.concatenate([me.astype(jnp.int32)[None], lengths[0].astype(jnp.int32)])

    def tile_of(v, k):
        return v[k * rows : (k + 1) * rows]

    gain1 = norm1_gain.astype(F32)[:, None]
    gain2 = norm2_gain.astype(F32)[:, None]
    rec_plan = tuple(
        tuple((((2 * (t % 2) + z) * 4 + t // 2) * width, width) for z in range(2)) for t in range(8)
    )
    ff_plan = tuple(tuple(((f * 8 + t) * units, units) for f in range(4)) for t in range(8))

    wxy = exchange(pack_columns(rec_plan, padded, w_x, w_y, gain1), PLANE)
    xf = layer_input.astype(F32)
    scale1 = lax.rsqrt(jnp.mean(xf * xf, axis=-1, keepdims=True) + NORM_EPS)
    xs = (xf * scale1).astype(BF16)
    wd = lax.all_gather(w_down, STACK, axis=0, tiled=True)
    xs_all = jnp.concatenate(act_gather(xs, "x", "y"), axis=0)
    wxy, packed_gu = lax.optimization_barrier((wxy, pack_columns(ff_plan, 4 * units, w_gate, w_up, gain2)))
    wxy = w_gather(wxy.reshape(-1, 2 * padded), *STACK).reshape(model, -1)
    wgu = lax.all_gather(exchange(packed_gu, PLANE).reshape(-1, 8 * units), STACK, axis=0, tiled=True)

    small = [conv_w, conv_b[:, None], b_rgate[:, None], b_igate[:, None], lam[:, None], w_rgate, w_igate]
    small_width = sum(v.shape[1] for v in small)
    packed = jnp.pad(jnp.concatenate([w_out] + small, axis=1), ((0, 0), (0, -small_width % 128)))
    halves = w_gather(packed, *STACK)
    mine = lax.dynamic_slice(halves, (core, 0, 0, 0), (1,) + halves.shape[1:])[0]
    theirs = swap(lax.dynamic_slice(halves, (1 - core, 0, 0, 0), (1,) + halves.shape[1:])[0], "c")
    whole = jnp.zeros((2, 2) + packed.shape, BF16)
    whole = lax.dynamic_update_slice(whole, mine[:, None], (0, core, 0, 0))
    whole = lax.dynamic_update_slice(whole, theirs[:, None], (0, 1 - core, 0, 0))
    whole = jnp.pad(whole.reshape(channels, -1), ((0, extra), (0, 0)))
    wo = whole[:, :model]
    rest = whole[:, model : model + taps + 4].astype(F32).T
    lam_all = rest[taps + 3]
    vec = jnp.concatenate([rest[: taps + 1], jax.nn.softplus(-lam_all)[None], rest[taps + 1 : taps + 3]], axis=0)
    at = model + taps + 4
    gates = jnp.zeros((padded, 2 * padded), BF16)
    for g in range(2):
        for n in range(blocks):
            block = whole[n * width : (n + 1) * width, at + g * width : at + (g + 1) * width]
            gates = gates.at[n * width : (n + 1) * width, g * padded + n * width : g * padded + (n + 1) * width].set(block)

    xy = dot32(xs_all, wxy)
    xc, pa, px, before, mixed = rec_forward(meta, xy, vec, gates, rows)

    resid = xf + act_scatter(lambda k: dot32(tile_of(mixed, k), wo).astype(BF16), "x", "y")
    scale2 = lax.rsqrt(jnp.mean(resid * resid, axis=-1, keepdims=True) + NORM_EPS)
    xs2 = (resid * scale2).astype(BF16)
    xs2_all = jnp.concatenate(act_gather(xs2, "x", "y"), axis=0)
    late_cot = lax.optimization_barrier((cot, mixed))[0]
    cot_all = jnp.concatenate(act_gather(late_cot, "x", "y"), axis=0)
    half = 4 * units
    gu = dot32(xs2_all, wgu)
    gt, up = gu[:, :half], gu[:, half:]
    act, slope = gelu_both(gt)
    hidden = (act * up).astype(BF16)
    d_hidden = back_product(cot_all, wd)
    d_gu = jnp.concatenate([(d_hidden * up * slope).astype(BF16), (d_hidden * act).astype(BF16)], axis=1)
    d_un2 = act_scatter(lambda k: back_product(tile_of(d_gu, k), wgu).astype(BF16), "x", "y")
    d_resid = cot.astype(F32) + norm_back(d_un2, resid, scale2)
    d_mix = d_resid.astype(BF16)
    d_mix_all = jnp.concatenate(act_gather(d_mix, "x", "y"), axis=0)

    d_wd = lax.psum_scatter(row_contract(hidden, cot_all).astype(BF16), STACK, scatter_dimension=0, tiled=True)
    d_wgu = lax.psum_scatter(row_contract(xs2_all, d_gu).astype(BF16), STACK, scatter_dimension=0, tiled=True)
    d_wg, d_wu, d_gain2 = unpack_columns(ff_plan, exchange(d_wgu.reshape(8, -1, 2 * half), PLANE), w_gate, w_up, gain2)

    late_hidden = lax.optimization_barrier((hidden, d_mix_all))[0]
    output = (resid + act_scatter(lambda k: dot32(tile_of(late_hidden, k), wd).astype(BF16), "x", "y")).astype(BF16)

    dm = back_product(d_mix_all, wo)
    dxy, d_gates, sums = rec_backward(meta, dm, xy, before, pa, px, xc, vec, gates.T, rows)
    d_un = act_scatter(lambda k: back_product(tile_of(dxy, k), wxy).astype(BF16), "x", "y")
    d_input = (d_resid + norm_back(d_un, xf, scale1)).astype(BF16)
    d_wxy = w_scatter(row_contract(xs_all, dxy).astype(BF16).reshape(2, 2, model // 4, -1), *STACK).astype(BF16)
    d_wx, d_wy, d_gain1 = unpack_columns(rec_plan, exchange(d_wxy.reshape(8, -1, 2 * padded), PLANE), w_x, w_y, gain1)

    def channels_out(v, kind):
        v = v.astype(kind).reshape(2, 2, part, -1)
        size = (2, 1) + v.shape[2:]
        keep = lax.dynamic_slice(v, (0, core, 0, 0), size)[:, 0]
        send = lax.dynamic_slice(v, (0, 1 - core, 0, 0), size)[:, 0]
        out = jnp.zeros((2,) + keep.shape, kind)
        out = lax.dynamic_update_slice(out, keep[None], (core, 0, 0, 0))
        return lax.dynamic_update_slice(out, swap(send, "c")[None], (1 - core, 0, 0, 0))

    d_wo = w_scatter(channels_out(row_contract(mixed, d_mix_all)[:channels], BF16), *STACK)
    sums = jnp.sum(sums.reshape(8, 8, padded), axis=1)
    d_lam_part = -jax.nn.sigmoid(-lam_all) * sums[5]
    d_cols = jnp.concatenate([sums[:5], sums[6:8], d_lam_part[None]], axis=0).T
    row_block = jnp.arange(channels)[:, None] // width
    d_blocks = []
    for g in range(2):
        block = d_gates[:channels, g * padded : g * padded + width]
        for n in range(1, blocks):
            at = g * padded + n * width
            block = jnp.where(row_block == n, d_gates[:channels, at : at + width], block)
        d_blocks.append(block)
    d_small = jnp.concatenate([d_cols[:channels]] + d_blocks, axis=1)
    d_small = lax.psum_scatter(channels_out(d_small, F32).reshape(4 * part, -1), STACK, scatter_dimension=0, tiled=True)
    d_cw, d_cb, d_br, d_bi, d_lam = d_small[:, :4], d_small[:, 4], d_small[:, 5], d_small[:, 6], d_small[:, 7]
    d_wr, d_wi = d_small[:, 8 : 8 + width], d_small[:, 8 + width : 8 + 2 * width]
    return (
        output, d_input, d_gain1[:, 0], d_wx, d_wy, d_cw, d_cb, d_wr, d_br, d_wi, d_bi, d_lam, d_wo,
        d_gain2[:, 0], d_wg, d_wu, d_wd.astype(F32),
    )


def factored(mesh):
    if tuple(mesh.axis_names) != ("fsdp", "seq") or (mesh.shape["fsdp"], mesh.shape["seq"]) != (4, 8):
        return None
    return Mesh(np.asarray(mesh.devices).reshape((2,) * 5), NAMES)


def solution(mesh):
    small = factored(mesh)
    if small is not None:
        whole, groups = P(NAMES), P(("zh", "zl"))
        return jax.shard_map(
            tensor_parallel,
            mesh=small,
            in_specs=(whole, groups) + (whole,) * 16,
            out_specs=(whole,) * 17,
            check_vma=False,
        )
    in_specs = (
        P(("fsdp", "seq"), None),
        P("fsdp", None),
        P(("fsdp", "seq")),
        P(("fsdp", "seq"), None),
        P(("fsdp", "seq"), None),
        P(("fsdp", "seq"), None),
        P(("fsdp", "seq")),
        P(("fsdp", "seq"), None),
        P(("fsdp", "seq")),
        P(("fsdp", "seq"), None),
        P(("fsdp", "seq")),
        P(("fsdp", "seq")),
        P(("fsdp", "seq"), None),
        P(("fsdp", "seq")),
        P(("fsdp", "seq"), None),
        P(("fsdp", "seq"), None),
        P(("fsdp", "seq"), None),
        P(("fsdp", "seq"), None),
    )
    out_specs = (
        P(("fsdp", "seq"), None),
        P(("fsdp", "seq"), None),
        P(("fsdp", "seq")),
        P(("fsdp", "seq"), None),
        P(("fsdp", "seq"), None),
        P(("fsdp", "seq"), None),
        P(("fsdp", "seq")),
        P(("fsdp", "seq"), None),
        P(("fsdp", "seq")),
        P(("fsdp", "seq"), None),
        P(("fsdp", "seq")),
        P(("fsdp", "seq")),
        P(("fsdp", "seq"), None),
        P(("fsdp", "seq")),
        P(("fsdp", "seq"), None),
        P(("fsdp", "seq"), None),
        P(("fsdp", "seq"), None),
    )
    return jax.shard_map(
        on_device, mesh=mesh, in_specs=in_specs, out_specs=out_specs, check_vma=False
    )
```

```python
import functools

import jax
import jax.numpy as jnp
import numpy as np
from jax import lax
from jax.experimental import pallas as pl
from jax.experimental.pallas import tpu as pltpu
from jax.sharding import Mesh
from jax.sharding import PartitionSpec as P

DECAY_C = 8.0
NORM_EPS = 1e-06


def from_behind(x, axis, by):
    size = lax.axis_size(axis)
    pairs = [(i, i + by) for i in range(size) if 0 <= i + by < size]
    return lax.ppermute(x, axis, pairs)


def carried_in(value, axis, join, neutral, backward):
    count, mine = (lax.axis_size(axis), lax.axis_index(axis))
    pieces = jax.tree.map(lambda part: lax.all_gather(part, axis), value)
    if backward:
        pieces = jax.tree.map(lambda part: part[::-1], pieces)
        mine = count - 1 - mine
    subtotal = jax.tree.map(
        lambda part, zero: jnp.full_like(part, 0) + jnp.asarray(zero, part.dtype), value, neutral
    )

    def step(position, subtotal):
        longer = join(subtotal, jax.tree.map(lambda part: part[position], pieces))
        return jax.tree.map(lambda new, old: jnp.where(position < mine, new, old), longer, subtotal)

    return lax.fori_loop(0, count - 1, step, subtotal)


def rms_apply(value, gain):
    scale = lax.rsqrt(jnp.mean(value * value, axis=-1, keepdims=True) + NORM_EPS)
    return value * scale * gain


def combine(earlier, later):
    return (earlier[0] * later[0], later[0] * earlier[1] + later[1])


def lru_terms(pre_r, pre_i, lam_vec, conv_out, start):
    rate = jax.nn.softplus(-lam_vec)
    log_a = -DECAY_C * jax.nn.sigmoid(pre_r) * rate
    decay = jnp.where(start[:, None], 0.0, jnp.exp(log_a))
    scale = jnp.sqrt(jnp.maximum(-jnp.expm1(2.0 * log_a), 0.2 * DECAY_C * rate))
    scale = jnp.where(start[:, None], 1.0, scale)
    return (decay, scale * jax.nn.sigmoid(pre_i) * conv_out)


def row_contract(left, right):
    return lax.dot_general(
        left, right, (((0,), (0,)), ((), ())), preferred_element_type=jnp.float32
    )


def back_product(grad, weight):
    return lax.dot_general(
        grad, weight, (((1,), (1,)), ((), ())), preferred_element_type=jnp.float32
    )


def split_blocks(value, width):
    return value.reshape(value.shape[0], value.shape[1] // width, width)


def block_product(value, weight):
    width = weight.shape[1]
    mats = weight.reshape(weight.shape[0] // width, width, width)
    result = jnp.einsum(
        "nhi,hij->nhj", split_blocks(value, width), mats, preferred_element_type=jnp.float32
    )
    return result.reshape(value.shape[0], -1)


def block_back(grad, weight):
    width = weight.shape[1]
    mats = weight.reshape(weight.shape[0] // width, width, width)
    result = jnp.einsum(
        "nhj,hij->nhi", split_blocks(grad, width), mats, preferred_element_type=jnp.float32
    )
    return result.reshape(grad.shape[0], -1)


def gate_grad(value, grad, width):
    result = jnp.einsum(
        "nhi,nhj->hij",
        split_blocks(value, width),
        split_blocks(grad, width),
        preferred_element_type=jnp.float32,
    )
    return result.reshape(value.shape[1], width)


def seq_starts(lens_row):
    count = lens_row.shape[0]
    before = jnp.arange(count)[None, :] < jnp.arange(count)[:, None]
    return jnp.sum(jnp.where(before, lens_row[None, :], 0), axis=1)


def seq_masks(lens_row, first, rows, taps):
    starts = seq_starts(lens_row)
    place = first + jnp.arange(rows, dtype=jnp.int32)

    def segment(p):
        return jnp.sum((p[:, None] >= starts[None, :]).astype(jnp.int32), axis=1)

    seg_now = segment(place)
    start = jnp.any(place[:, None] == starts[None, :], axis=1)
    same = jnp.stack(
        [
            ((segment(place - k) == seg_now) & (place - k >= 0)).astype(jnp.float32)
            for k in range(taps)
        ],
        0,
    )
    return (start, same)


def on_device(
    layer_input,
    lengths,
    norm1_gain,
    w_x,
    w_y,
    conv_w,
    conv_b,
    w_rgate,
    b_rgate,
    w_igate,
    b_igate,
    lam,
    w_out,
    norm2_gain,
    w_gate,
    w_up,
    w_down,
    cot,
):
    rows = layer_input.shape[0]
    taps = conv_w.shape[1]
    width = w_rgate.shape[1]
    rim = taps - 1
    index = lax.axis_index("seq")
    start, same = seq_masks(lengths[0], index * rows, rows, taps)
    gain_one, wx, wy, cw, cb, wr, br, wi, bi, lam_all, wo = (
        lax.all_gather(norm1_gain, ("fsdp", "seq"), axis=0, tiled=True),
        lax.all_gather(w_x, ("fsdp", "seq"), axis=0, tiled=True),
        lax.all_gather(w_y, ("fsdp", "seq"), axis=0, tiled=True),
        lax.all_gather(conv_w, ("fsdp", "seq"), axis=0, tiled=True),
        lax.all_gather(conv_b, ("fsdp", "seq"), axis=0, tiled=True),
        lax.all_gather(w_rgate, ("fsdp", "seq"), axis=0, tiled=True),
        lax.all_gather(b_rgate, ("fsdp", "seq"), axis=0, tiled=True),
        lax.all_gather(w_igate, ("fsdp", "seq"), axis=0, tiled=True),
        lax.all_gather(b_igate, ("fsdp", "seq"), axis=0, tiled=True),
        lax.all_gather(lam, ("fsdp", "seq"), axis=0, tiled=True),
        lax.all_gather(w_out, ("fsdp", "seq"), axis=0, tiled=True),
    )
    xf = layer_input.astype(jnp.float32)
    gain1 = gain_one.astype(jnp.float32)
    un = rms_apply(xf, gain1).astype(jnp.bfloat16)
    xb = jnp.dot(un, wx, preferred_element_type=jnp.float32).astype(jnp.bfloat16)
    yb = jnp.dot(un, wy, preferred_element_type=jnp.float32)
    gy = jax.nn.gelu(yb)
    rim_in = from_behind(xb[rows - rim :], "seq", 1)
    extended = jnp.concatenate([rim_in, xb], axis=0).astype(jnp.float32)
    cwf = cw.astype(jnp.float32)
    conv = jnp.broadcast_to(cb.astype(jnp.float32)[None, :], (rows, cwf.shape[0]))
    for k in range(taps):
        conv = conv + cwf[:, k][None, :] * extended[rim - k : rim - k + rows] * same[k][:, None]
    xc = conv.astype(jnp.bfloat16)
    xcf = xc.astype(jnp.float32)
    pre_r = block_product(xc, wr) + br.astype(jnp.float32)[None, :]
    pre_i = block_product(xc, wi) + bi.astype(jnp.float32)[None, :]
    lamf = lam_all.astype(jnp.float32)
    decay, drive = lru_terms(pre_r, pre_i, lamf, xcf, start)
    decay_cum, state_loc = lax.associative_scan(combine, (decay, drive), axis=0)
    zero_vec = jnp.zeros((decay.shape[1],), jnp.float32)
    one_vec = jnp.ones((decay.shape[1],), jnp.float32)
    state_in = carried_in(
        (decay_cum[-1], state_loc[-1]), "seq", combine, (one_vec, zero_vec), False
    )[1]
    state = state_loc + decay_cum * state_in[None, :]
    state_prev = jnp.concatenate([state_in[None, :], state[:-1]], axis=0)
    mixed = (state * gy).astype(jnp.bfloat16)
    resid = xf + jnp.dot(mixed, wo, preferred_element_type=jnp.float32)
    gain_two, wg, wu, wd = (
        lax.all_gather(norm2_gain, ("fsdp", "seq"), axis=0, tiled=True),
        lax.all_gather(w_gate, ("fsdp", "seq"), axis=0, tiled=True),
        lax.all_gather(w_up, ("fsdp", "seq"), axis=0, tiled=True),
        lax.all_gather(w_down, ("fsdp", "seq"), axis=0, tiled=True),
    )
    gain2 = gain_two.astype(jnp.float32)
    un2 = rms_apply(resid, gain2).astype(jnp.bfloat16)
    gate_pre = jnp.dot(un2, wg, preferred_element_type=jnp.float32)
    up_pre = jnp.dot(un2, wu, preferred_element_type=jnp.float32)
    gate_act, gelu_back = jax.vjp(jax.nn.gelu, gate_pre)
    hidden = (gate_act * up_pre).astype(jnp.bfloat16)
    output = (resid + jnp.dot(hidden, wd, preferred_element_type=jnp.float32)).astype(jnp.bfloat16)
    grad = cot.astype(jnp.float32)
    gain_two, wg, wu, wd = (
        lax.all_gather(norm2_gain, ("fsdp", "seq"), axis=0, tiled=True),
        lax.all_gather(w_gate, ("fsdp", "seq"), axis=0, tiled=True),
        lax.all_gather(w_up, ("fsdp", "seq"), axis=0, tiled=True),
        lax.all_gather(w_down, ("fsdp", "seq"), axis=0, tiled=True),
    )
    gain2 = gain_two.astype(jnp.float32)
    d_wd = row_contract(hidden, cot)
    d_hidden = back_product(cot, wd)
    d_gate = gelu_back(d_hidden * up_pre)[0].astype(jnp.bfloat16)
    d_up = (d_hidden * gate_act).astype(jnp.bfloat16)
    d_wg = row_contract(un2, d_gate)
    d_wu = row_contract(un2, d_up)
    d_un2 = back_product(d_gate, wg) + back_product(d_up, wu)
    norm_two_back = jax.vjp(rms_apply, resid, gain2)[1]
    d_resid_norm, d_gain2 = norm_two_back(d_un2)
    mlp_grads = (
        lax.psum_scatter(d_gain2, ("fsdp", "seq"), scatter_dimension=0, tiled=True),
        lax.psum_scatter(d_wg, ("fsdp", "seq"), scatter_dimension=0, tiled=True),
        lax.psum_scatter(d_wu, ("fsdp", "seq"), scatter_dimension=0, tiled=True),
        lax.psum_scatter(d_wd, ("fsdp", "seq"), scatter_dimension=0, tiled=True),
    )
    d_resid = grad + d_resid_norm
    gain_one, wx, wy, cw, cb, wr, br, wi, bi, lam_all, wo = (
        lax.all_gather(norm1_gain, ("fsdp", "seq"), axis=0, tiled=True),
        lax.all_gather(w_x, ("fsdp", "seq"), axis=0, tiled=True),
        lax.all_gather(w_y, ("fsdp", "seq"), axis=0, tiled=True),
        lax.all_gather(conv_w, ("fsdp", "seq"), axis=0, tiled=True),
        lax.all_gather(conv_b, ("fsdp", "seq"), axis=0, tiled=True),
        lax.all_gather(w_rgate, ("fsdp", "seq"), axis=0, tiled=True),
        lax.all_gather(b_rgate, ("fsdp", "seq"), axis=0, tiled=True),
        lax.all_gather(w_igate, ("fsdp", "seq"), axis=0, tiled=True),
        lax.all_gather(b_igate, ("fsdp", "seq"), axis=0, tiled=True),
        lax.all_gather(lam, ("fsdp", "seq"), axis=0, tiled=True),
        lax.all_gather(w_out, ("fsdp", "seq"), axis=0, tiled=True),
    )
    gain1 = gain_one.astype(jnp.float32)
    cwf = cw.astype(jnp.float32)
    lamf = lam_all.astype(jnp.float32)
    d_mix = d_resid.astype(jnp.bfloat16)
    d_wo = row_contract(mixed, d_mix)
    d_mixed = back_product(d_mix, wo)
    d_state = d_mixed * gy
    gelu_y_back = jax.vjp(jax.nn.gelu, yb)[1]
    d_yb = gelu_y_back(d_mixed * state)[0].astype(jnp.bfloat16)
    next_decay = jnp.concatenate([decay[1:], one_vec[None, :]], axis=0)
    decay_after, adjoint_loc = lax.associative_scan(
        combine, (next_decay, d_state), reverse=True, axis=0
    )
    send_decay = decay[0] * decay_after[0]
    send_adjoint = decay[0] * adjoint_loc[0]
    adjoint_in = carried_in((send_decay, send_adjoint), "seq", combine, (one_vec, zero_vec), True)[
        1
    ]
    adjoint = adjoint_loc + decay_after * adjoint_in[None, :]

    def local_lru(pr, pi, lv, cv):
        return lru_terms(pr, pi, lv, cv, start)

    lru_back = jax.vjp(local_lru, pre_r, pre_i, lamf, xcf)[1]
    d_pre_r, d_pre_i, d_lam, d_xc_local = lru_back((adjoint * state_prev, adjoint))
    d_pr = d_pre_r.astype(jnp.bfloat16)
    d_pi = d_pre_i.astype(jnp.bfloat16)
    d_wr = gate_grad(xc, d_pr, width)
    d_wi = gate_grad(xc, d_pi, width)
    d_br = jnp.sum(d_pr.astype(jnp.float32), axis=0)
    d_bi = jnp.sum(d_pi.astype(jnp.float32), axis=0)
    d_xc = d_xc_local + block_back(d_pr, wr) + block_back(d_pi, wi)
    d_cb = jnp.sum(d_xc, axis=0)
    d_cw = jnp.stack(
        [
            jnp.sum(d_xc * extended[rim - k : rim - k + rows] * same[k][:, None], axis=0)
            for k in range(taps)
        ],
        axis=1,
    )
    d_extended = jnp.zeros((rows + rim, d_xc.shape[1]), jnp.float32)
    for k in range(taps):
        d_extended = d_extended + jnp.pad(
            d_xc * cwf[:, k][None, :] * same[k][:, None], ((rim - k, k), (0, 0))
        )
    rim_back = from_behind(d_extended[:rim], "seq", -1)
    d_xb = (d_extended[rim:] + jnp.pad(rim_back, ((rows - rim, 0), (0, 0)))).astype(jnp.bfloat16)
    d_wx = row_contract(un, d_xb)
    d_wy = row_contract(un, d_yb)
    d_un = back_product(d_xb, wx) + back_product(d_yb, wy)
    norm_one_back = jax.vjp(rms_apply, xf, gain1)[1]
    d_x_norm, d_gain1 = norm_one_back(d_un)
    d_input = (d_resid + d_x_norm).astype(jnp.bfloat16)
    block_grads = (
        lax.psum_scatter(d_gain1, ("fsdp", "seq"), scatter_dimension=0, tiled=True),
        lax.psum_scatter(d_wx, ("fsdp", "seq"), scatter_dimension=0, tiled=True),
        lax.psum_scatter(d_wy, ("fsdp", "seq"), scatter_dimension=0, tiled=True),
        lax.psum_scatter(d_cw, ("fsdp", "seq"), scatter_dimension=0, tiled=True),
        lax.psum_scatter(d_cb, ("fsdp", "seq"), scatter_dimension=0, tiled=True),
        lax.psum_scatter(d_wr, ("fsdp", "seq"), scatter_dimension=0, tiled=True),
        lax.psum_scatter(d_br, ("fsdp", "seq"), scatter_dimension=0, tiled=True),
        lax.psum_scatter(d_wi, ("fsdp", "seq"), scatter_dimension=0, tiled=True),
        lax.psum_scatter(d_bi, ("fsdp", "seq"), scatter_dimension=0, tiled=True),
        lax.psum_scatter(d_lam, ("fsdp", "seq"), scatter_dimension=0, tiled=True),
        lax.psum_scatter(d_wo, ("fsdp", "seq"), scatter_dimension=0, tiled=True),
    )
    return (
        output,
        d_input,
        block_grads[0],
        block_grads[1],
        block_grads[2],
        block_grads[3],
        block_grads[4],
        block_grads[5],
        block_grads[6],
        block_grads[7],
        block_grads[8],
        block_grads[9],
        block_grads[10],
        mlp_grads[0],
        mlp_grads[1],
        mlp_grads[2],
        mlp_grads[3],
    )


NAMES = ("zh", "zl", "y", "x", "c")
F32 = jnp.float32
BF16 = jnp.bfloat16
GELU_C = 0.7978845608
GELU_K = 0.044715


def swap(v, name):
    return lax.ppermute(v, name, [(0, 1), (1, 0)])


def add16(one, two):
    return (one.astype(F32) + two.astype(F32)).astype(BF16)


def act_gather(v, a, b):
    h = v.shape[0] // 2
    near, from_a, from_b = swap(v, "c"), swap(v, a), swap(v, b)
    far0, far1 = swap(from_a[:h], b), swap(from_b[h:], a)
    near_a, near_b = swap(from_a, "c"), swap(from_b, "c")
    far = jnp.concatenate([far0, far1], axis=0)
    return [v, near, from_a, near_a, from_b, near_b, far, swap(far, "c")]


def act_scatter(get, a, b):
    far, to_a, to_b = [add16(get(k), swap(get(k + 1), "c")) for k in (6, 2, 4)]
    own = get(0).astype(F32) + swap(get(1), "c").astype(F32)
    h = far.shape[0] // 2
    in_b, in_a = swap(far[:h], b), swap(far[h:], a)
    to_a = jnp.concatenate([add16(to_a[:h], in_b), to_a[h:]], axis=0)
    to_b = jnp.concatenate([to_b[:h], add16(to_b[h:], in_a)], axis=0)
    return own + swap(to_a, a).astype(F32) + swap(to_b, b).astype(F32)


def w_gather(v, w1, w2):
    i1, i2 = lax.axis_index(w1), lax.axis_index(w2)
    p1, p2 = swap(v, w1), swap(v, w2)
    p12 = swap(p1, w2)
    out = jnp.zeros((2, 2) + v.shape, v.dtype)
    tail = (0,) * v.ndim
    for part, j1, j2 in ((v, i1, i2), (p1, 1 - i1, i2), (p2, i1, 1 - i2), (p12, 1 - i1, 1 - i2)):
        out = lax.dynamic_update_slice(out, part[None, None], (j1, j2) + tail)
    return out


def w_scatter(v, w1, w2):
    i1, i2 = lax.axis_index(w1), lax.axis_index(w2)

    def get(j1, j2):
        return lax.dynamic_slice(v, (j1, j2) + (0,) * (v.ndim - 2), (1, 1) + v.shape[2:])[0, 0]

    other = add16(get(1 - i1, i2), swap(get(1 - i1, 1 - i2), w2))
    own = get(i1, i2).astype(F32) + swap(get(i1, 1 - i2), w2).astype(F32)
    return own + swap(other, w1).astype(F32)


def pack_kernel(plan, a_ref, b_ref, gain_ref, out_ref):
    half = out_ref.shape[2] // 2
    for first, ref in ((0, a_ref), (half, b_ref)):
        scaled = (ref[...].astype(F32) * gain_ref[...]).astype(BF16)
        for dest, pieces in enumerate(plan):
            at = first
            for source, size in pieces:
                out_ref[dest, :, at : at + size] = scaled[:, source : source + size]
                at += size
            if at < first + half:
                out_ref[dest, :, at : first + half] = jnp.zeros((scaled.shape[0], first + half - at), BF16)


def unpack_kernel(plan, grad_ref, a_ref, b_ref, gain_ref, da_ref, db_ref, dgain_ref):
    half = grad_ref.shape[2] // 2
    total = jnp.zeros(dgain_ref.shape, F32)
    for first, ref, out in ((0, a_ref, da_ref), (half, b_ref, db_ref)):
        for dest, pieces in enumerate(plan):
            at = first
            for source, size in pieces:
                piece = grad_ref[dest, :, at : at + size].astype(F32)
                out[:, source : source + size] = piece * gain_ref[...]
                weight = ref[:, source : source + size].astype(F32)
                total = total + jnp.sum(piece * weight, axis=1, keepdims=True)
                at += size
    dgain_ref[...] = total


def pack_columns(plan, half, one, two, gain):
    return pl.pallas_call(
        functools.partial(pack_kernel, plan),
        out_shape=jax.ShapeDtypeStruct((8, one.shape[0], 2 * half), BF16),
        compiler_params=pltpu.CompilerParams(vmem_limit_bytes=24 << 20),
        cost_estimate=pl.CostEstimate(flops=4 * one.size, transcendentals=0, bytes_accessed=8 * one.size),
        name="pack_columns",
    )(one, two, gain)


def unpack_columns(plan, grad, one, two, gain):
    shape = jax.ShapeDtypeStruct(one.shape, F32)
    return pl.pallas_call(
        functools.partial(unpack_kernel, plan),
        out_shape=[shape, shape, jax.ShapeDtypeStruct((one.shape[0], 1), F32)],
        compiler_params=pltpu.CompilerParams(vmem_limit_bytes=24 << 20),
        cost_estimate=pl.CostEstimate(flops=8 * one.size, transcendentals=0, bytes_accessed=16 * one.size),
        name="unpack_columns",
    )(grad, one, two, gain)


def exchange(v, tp):
    return lax.all_to_all(v, tp, split_axis=0, concat_axis=0, tiled=True)


def neg_expm1(v):
    series = 1.0 + v * (1.0 / 10.0)
    for n in range(9, 1, -1):
        series = 1.0 + v * (1.0 / n) * series
    return jnp.where(v > -0.5, -v * series, 1.0 - jnp.exp(v))


def gate_terms(pa, px, rate, start):
    sr = jax.nn.sigmoid(pa)
    si = jax.nn.sigmoid(px)
    la = -DECAY_C * sr * rate
    decay = jnp.where(start, 0.0, jnp.exp(la))
    e2 = neg_expm1(2.0 * la)
    floor = 0.2 * DECAY_C * rate
    scale = jnp.where(start, 1.0, jnp.sqrt(jnp.maximum(e2, floor)))
    return sr, si, decay, e2, floor, scale


def gelu(v):
    return 0.5 * v * (1.0 + jnp.tanh(GELU_C * (v + GELU_K * v * v * v)))


def gelu_both(v):
    t = jnp.tanh(GELU_C * (v + GELU_K * v * v * v))
    half = 0.5 * (1.0 + t)
    return v * half, half + 0.5 * v * (1.0 - t * t) * GELU_C * (1.0 + 3.0 * GELU_K * v * v)


def scan_tile(decay, drive, into):
    row = lax.broadcasted_iota(jnp.int32, decay.shape, 0)
    for by in (1, 2, 4):
        keep = row >= by
        drive = jnp.where(keep, decay * pltpu.roll(drive, by, 0) + drive, drive)
        decay = jnp.where(keep, decay * pltpu.roll(decay, by, 0), decay)
    return decay * into + drive


def scan_tile_back(decay, drive, into):
    row = lax.broadcasted_iota(jnp.int32, decay.shape, 0)
    for by in (1, 2, 4):
        keep = row < 8 - by
        drive = jnp.where(keep, decay * pltpu.roll(drive, 8 - by, 0) + drive, drive)
        decay = jnp.where(keep, decay * pltpu.roll(decay, 8 - by, 0), decay)
    return decay * into + drive


STEP = 16


def since_start(meta_ref, place, width):
    at = place + lax.broadcasted_iota(jnp.int32, (STEP, 128), 0)
    since, start = at, 0
    for n in range(1, meta_ref.shape[0] - 1):
        start = start + meta_ref[n]
        since = jnp.where(at >= start, at - start, since)
    return jnp.concatenate([since] * (width // 128), axis=1)


def rec_fwd_kernel(meta_ref, xb_ref, yb_ref, vec_ref, w_ref, xc_ref, pa_ref, px_ref, sp_ref, mixed_ref, ext, carry):
    rows, width = xb_ref.shape
    base = pl.program_id(0) * rows

    @pl.when(pl.program_id(0) == 0)
    def _():
        ext[0:8, :] = jnp.zeros((8, width), F32)
        carry[...] = jnp.zeros_like(carry)

    ext[8 : 8 + rows, :] = xb_ref[...].astype(BF16).astype(F32)

    def conv_step(r, _):
        at = pl.multiple_of(r * STEP, STEP)
        window = ext[pl.ds(at, STEP + 8), :]
        since = since_start(meta_ref, base + at, width)
        total = vec_ref[4:5, :] + vec_ref[0:1, :] * window[8:, :]
        for k in range(1, 4):
            moved = jnp.where(since >= k, window[8 - k : 8 - k + STEP, :], 0.0)
            total = total + vec_ref[k : k + 1, :] * moved
        xc_ref[pl.ds(at, STEP), :] = total.astype(BF16)
        return 0

    lax.fori_loop(0, rows // STEP, conv_step, 0, unroll=2)
    ext[0:8, :] = ext[rows : rows + 8, :]
    xc = xc_ref[...]
    pa_ref[...] = jnp.dot(xc, w_ref[:, :width], preferred_element_type=F32) + vec_ref[6:7, :]
    px_ref[...] = jnp.dot(xc, w_ref[:, width:], preferred_element_type=F32) + vec_ref[7:8, :]
    top = lax.broadcasted_iota(jnp.int32, (8, width), 0) == 0

    def scan_step(r, held):
        here = pl.ds(pl.multiple_of(r * STEP, STEP), STEP)
        start = since_start(meta_ref, base + r * STEP, width) == 0
        _, si, decay, _, _, scale = gate_terms(pa_ref[here, :], px_ref[here, :], vec_ref[5:6, :], start)
        drive = scale * si * xc_ref[here, :].astype(F32)
        states, before = [], []
        for part in range(0, STEP, 8):
            now = scan_tile(decay[part : part + 8], drive[part : part + 8], held)
            states.append(now)
            before.append(jnp.where(top, held, pltpu.roll(now, 1, 0)))
            held = jnp.broadcast_to(now[7:8, :], (8, width))
        sp_ref[here, :] = jnp.concatenate(before, axis=0)
        mixed_ref[here, :] = (jnp.concatenate(states, axis=0) * gelu(yb_ref[here, :])).astype(BF16)
        return held

    carry[...] = lax.fori_loop(0, rows // STEP, scan_step, carry[...], unroll=2)


def rec_bwd_kernel(
    meta_ref, dm_ref, yb_ref, sp_ref, pa_ref, px_ref, xc_ref, xb_ref, vec_ref, wt_ref,
    dxy_ref, dw_ref, sum_ref, ext, dp, carry,
):
    rows, width = xb_ref.shape
    base = (pl.num_programs(0) - 1 - pl.program_id(0)) * rows

    @pl.when(pl.program_id(0) == 0)
    def _():
        ext[rows : rows + 8, :] = jnp.zeros((8, width), F32)
        carry[...] = jnp.zeros_like(carry)
        dw_ref[...] = jnp.zeros_like(dw_ref)
        sum_ref[...] = jnp.zeros_like(sum_ref)

    row = lax.broadcasted_iota(jnp.int32, (8, width), 0)
    steps = rows // STEP

    def fold(v):
        return v[0:8, :] + v[8:16, :]

    def scan_step(i, state):
        held, s_rate, s_r, s_i = state
        at = pl.multiple_of((steps - 1 - i) * STEP, STEP)
        here = pl.ds(at, STEP)
        start = since_start(meta_ref, base + at, width) == 0
        rate = vec_ref[5:6, :]
        sr, si, decay, e2, floor, scale = gate_terms(pa_ref[here, :], px_ref[here, :], rate, start)
        xc = xc_ref[here, :].astype(F32)
        before = sp_ref[here, :]
        gate = si * xc
        now = decay * before + scale * gate
        dm = dm_ref[here, :]
        act, slope = gelu_both(yb_ref[here, :])
        dxy_ref[here, width:] = (dm * now * slope).astype(BF16)
        dstate = dm * act
        parts = []
        for part in range(STEP - 8, -1, -8):
            here_decay = decay[part : part + 8]
            coef = jnp.where(row == 7, 1.0, pltpu.roll(here_decay, 7, 0))
            adj = scan_tile_back(coef, dstate[part : part + 8], held)
            held = jnp.broadcast_to((here_decay * adj)[0:1, :], (8, width))
            parts.append(adj)
        adj = jnp.concatenate(parts[::-1], axis=0)
        d_scale = adj * gate
        d_half = jnp.where(start, 0.0, d_scale * 0.5 / scale)
        share = jnp.where(e2 > floor, 1.0, jnp.where(e2 == floor, 0.5, 0.0))
        kept = adj * scale
        d_la = decay * (adj * before - 2.0 * decay * d_half * share)
        d_rate = -DECAY_C * sr * d_la + (0.2 * DECAY_C) * d_half * (1.0 - share)
        d_pa = (-DECAY_C * rate * d_la * sr * (1.0 - sr)).astype(BF16)
        d_px = (kept * xc * si * (1.0 - si)).astype(BF16)
        dp[here, :width] = d_pa
        dp[here, width:] = d_px
        ext[here, :] = kept * si
        return held, s_rate + fold(d_rate), s_r + fold(d_pa.astype(F32)), s_i + fold(d_px.astype(F32))

    held, s_rate, s_r, s_i = lax.fori_loop(
        0, steps, scan_step, (carry[...], sum_ref[40:48, :], sum_ref[48:56, :], sum_ref[56:64, :]), unroll=2
    )
    carry[...] = held
    sum_ref[40:48, :] = s_rate
    sum_ref[48:56, :] = s_r
    sum_ref[56:64, :] = s_i
    ext[0:rows, :] += jnp.dot(dp[...], wt_ref[...], preferred_element_type=F32)
    dw_ref[...] += row_contract(xc_ref[...], dp[...])

    def conv_step(r, sums):
        at = pl.multiple_of(r * STEP, STEP)
        window = ext[pl.ds(at, STEP + 8), :]
        xb = xb_ref[pl.ds(at, STEP), :].astype(BF16).astype(F32)
        total = jnp.zeros((STEP, width), F32)
        new = []
        for k in range(4):
            moved = window[k : k + STEP, :]
            if k:
                moved = jnp.where(since_start(meta_ref, base + at + k, width) >= k, moved, 0.0)
            total = total + vec_ref[k : k + 1, :] * moved
            new.append(sums[k] + fold(moved * xb))
        new.append(sums[4] + fold(window[:STEP, :]))
        dxy_ref[pl.ds(at, STEP), :width] = total.astype(BF16)
        return tuple(new)

    sums = lax.fori_loop(0, steps, conv_step, tuple(sum_ref[8 * q : 8 * q + 8, :] for q in range(5)), unroll=2)
    for q in range(5):
        sum_ref[8 * q : 8 * q + 8, :] = sums[q]
    ext[rows : rows + 8, :] = ext[0:8, :]


def rec_forward(meta, xy, vec, w, tile):
    total, width = xy.shape[0], xy.shape[1] // 2
    block = pl.BlockSpec((tile, width), lambda i, m: (i ^ m[0], 0))
    right = pl.BlockSpec((tile, width), lambda i, m: (i ^ m[0], 1))
    whole = lambda v: pl.BlockSpec(v.shape, lambda i, m: (0, 0))
    return pl.pallas_call(
        rec_fwd_kernel,
        grid_spec=pltpu.PrefetchScalarGridSpec(
            num_scalar_prefetch=1,
            grid=(total // tile,),
            in_specs=[block, right, whole(vec), whole(w)],
            out_specs=[block] * 5,
            scratch_shapes=[pltpu.VMEM((tile + 8, width), F32), pltpu.VMEM((8, width), F32)],
        ),
        out_shape=[jax.ShapeDtypeStruct((total, width), t) for t in (BF16, F32, F32, F32, BF16)],
        compiler_params=pltpu.CompilerParams(vmem_limit_bytes=32 << 20),
        cost_estimate=pl.CostEstimate(
            flops=100 * total * width + 4 * total * width * width,
            transcendentals=6 * total * width,
            bytes_accessed=24 * total * width,
        ),
        name="recurrence_forward",
    )(meta, xy, xy, vec, w)


def rec_backward(meta, dm, xy, sp, pa, px, xc, vec, wt, tile):
    total, width = dm.shape
    steps = total // tile
    block = pl.BlockSpec((tile, width), lambda i, m: ((steps - 1 - i) ^ m[0], 0))
    right = pl.BlockSpec((tile, width), lambda i, m: ((steps - 1 - i) ^ m[0], 1))
    whole = lambda v: pl.BlockSpec(v.shape, lambda i, m: (0, 0))
    return pl.pallas_call(
        rec_bwd_kernel,
        grid_spec=pltpu.PrefetchScalarGridSpec(
            num_scalar_prefetch=1,
            grid=(steps,),
            in_specs=[block, right, block, block, block, block, block, whole(vec), whole(wt)],
            out_specs=[
                pl.BlockSpec((tile, 2 * width), lambda i, m: ((steps - 1 - i) ^ m[0], 0)),
                pl.BlockSpec((width, 2 * width), lambda i, m: (0, 0)),
                pl.BlockSpec((64, width), lambda i, m: (0, 0)),
            ],
            scratch_shapes=[
                pltpu.VMEM((tile + 8, width), F32),
                pltpu.VMEM((tile, 2 * width), BF16),
                pltpu.VMEM((8, width), F32),
            ],
        ),
        out_shape=[
            jax.ShapeDtypeStruct((total, 2 * width), BF16),
            jax.ShapeDtypeStruct((width, 2 * width), F32),
            jax.ShapeDtypeStruct((64, width), F32),
        ],
        compiler_params=pltpu.CompilerParams(vmem_limit_bytes=32 << 20),
        cost_estimate=pl.CostEstimate(
            flops=180 * total * width + 8 * total * width * width,
            transcendentals=6 * total * width,
            bytes_accessed=30 * total * width,
        ),
        name="recurrence_backward",
    )(meta, dm, xy, sp, pa, px, xc, xy, vec, wt)


def dot32(one, two):
    return jnp.dot(one, two, preferred_element_type=F32)


def columns_of(width, most):
    return next(n for n in range(min(width, most), 0, -128) if width % n == 0)


def store_blocks(step, value_ref, outs, rows):
    per = value_ref.shape[0] // rows
    for n, out in enumerate(outs):

        @pl.when(step == n // per)
        def _(n=n, out=out):
            out[...] = value_ref[(n % per) * rows : (n % per + 1) * rows, :]


def blocks_kernel(flip, a_ref, w_ref, *rest):
    outs, value = rest[:-1], rest[-1]
    model = outs[0].shape[1]
    wide = columns_of(model, 512)
    a = a_ref[...]
    for at in range(0, model, wide):
        if flip:
            part = back_product(a, w_ref[at : at + wide, :])
        else:
            part = dot32(a, w_ref[:, at : at + wide])
        value[:, at : at + wide] = part.astype(BF16)
    store_blocks(pl.program_id(0), value, outs, outs[0].shape[0])


def product_blocks(a, w, flip):
    total, deep = a.shape
    model = w.shape[0] if flip else w.shape[1]
    tile, rows = total // 4, total // 8
    return pl.pallas_call(
        functools.partial(blocks_kernel, flip),
        grid=(4,),
        in_specs=[pl.BlockSpec((tile, deep), lambda i: (i, 0)), pl.BlockSpec(w.shape, lambda i: (0, 0))],
        out_specs=[pl.BlockSpec((rows, model), lambda i: (0, 0))] * 8,
        out_shape=[jax.ShapeDtypeStruct((rows, model), BF16)] * 8,
        scratch_shapes=[pltpu.VMEM((tile, model), BF16)],
        compiler_params=pltpu.CompilerParams(vmem_limit_bytes=44 << 20),
        cost_estimate=pl.CostEstimate(
            flops=2 * total * deep * model,
            transcendentals=0,
            bytes_accessed=2 * (total * deep + w.size + total * model),
        ),
        name="product_blocks",
    )(a, w)


def ff_kernel(x_ref, cot_ref, wgu_ref, wd_ref, hidden_ref, dgu_ref, *rest):
    outs, value = rest[:-1], rest[-1]
    half, model = wd_ref.shape
    narrow, wide = columns_of(half, 256), columns_of(model, 512)
    x, cot = x_ref[...], cot_ref[...]
    for at in range(0, half, narrow):
        gt = dot32(x, wgu_ref[:, at : at + narrow])
        up = dot32(x, wgu_ref[:, half + at : half + at + narrow])
        dh = back_product(cot, wd_ref[at : at + narrow, :])
        act, slope = gelu_both(gt)
        hidden_ref[:, at : at + narrow] = (act * up).astype(BF16)
        dgu_ref[:, at : at + narrow] = (dh * up * slope).astype(BF16)
        dgu_ref[:, half + at : half + at + narrow] = (dh * act).astype(BF16)
    grad = dgu_ref[...]
    for at in range(0, model, wide):
        value[:, at : at + wide] = back_product(grad, wgu_ref[at : at + wide, :]).astype(BF16)
    store_blocks(pl.program_id(0), value, outs, outs[0].shape[0])


def feed_forward(x, cot, wgu, wd):
    total, model = x.shape
    half = wd.shape[0]
    tile, rows = total // 4, total // 8
    at = lambda cols: pl.BlockSpec((tile, cols), lambda i: (i, 0))
    whole = lambda v: pl.BlockSpec(v.shape, lambda i: (0, 0), pipeline_mode=pl.Buffered(1))
    return pl.pallas_call(
        ff_kernel,
        grid=(4,),
        in_specs=[at(model), at(model), whole(wgu), whole(wd)],
        out_specs=[at(half), at(2 * half)] + [pl.BlockSpec((rows, model), lambda i: (0, 0))] * 8,
        out_shape=[jax.ShapeDtypeStruct((total, half), BF16), jax.ShapeDtypeStruct((total, 2 * half), BF16)]
        + [jax.ShapeDtypeStruct((rows, model), BF16)] * 8,
        scratch_shapes=[pltpu.VMEM((tile, model), BF16)],
        compiler_params=pltpu.CompilerParams(vmem_limit_bytes=52 << 20),
        cost_estimate=pl.CostEstimate(
            flops=10 * total * model * half,
            transcendentals=total * half,
            bytes_accessed=2 * (3 * total * model + 3 * half * model + 3 * total * half),
        ),
        name="feed_forward",
    )(x, cot, wgu, wd)


def norm_back(dv, v, scale):
    return scale * dv - scale * scale * scale * v * jnp.mean(dv * v, axis=-1, keepdims=True)


PLANE = ("y", "x", "c")
STACK = ("zh", "zl")
UNITS = ("zl", "x", "c")
SHARDS = ("zh", "y")


def tensor_parallel(
    layer_input, lengths, norm1_gain, w_x, w_y, conv_w, conv_b, w_rgate, b_rgate, w_igate, b_igate, lam,
    w_out, norm2_gain, w_gate, w_up, w_down, cot,
):
    rows, model = layer_input.shape
    taps = conv_w.shape[1]
    width = w_rgate.shape[1]
    part = w_out.shape[0]
    channels = 4 * part
    padded = -(-channels // 128) * 128
    extra = padded - channels
    blocks = channels // width
    units = w_down.shape[0]
    core = lax.axis_index("c")
    me = (lax.axis_index("y") * 2 + lax.axis_index("x")) * 2 + core
    meta = jnp.concatenate([me.astype(jnp.int32)[None], lengths[0].astype(jnp.int32)])

    gain1 = norm1_gain.astype(F32)[:, None]
    gain2 = norm2_gain.astype(F32)[:, None]
    rec_plan = tuple(
        tuple((((2 * (t % 2) + z) * 4 + t // 2) * width, width) for z in range(2)) for t in range(8)
    )
    ff_plan = tuple(
        tuple((((f // 2) * 16 + (t // 4) * 8 + (f % 2) * 4 + t % 4) * units, units) for f in range(4)) for t in range(8)
    )

    def shard_order(v):
        return v.reshape(v.shape[0], 2, 2, 2, -1).swapaxes(2, 3).reshape(v.shape)

    packed_xy = pack_columns(rec_plan, padded, w_x, w_y, gain1)
    wd = lax.all_gather(w_down, SHARDS, axis=0, tiled=True)
    late_input = lax.optimization_barrier((layer_input, packed_xy))[0]
    wxy = exchange(packed_xy, PLANE)
    xf = late_input.astype(F32)
    scale1 = lax.rsqrt(jnp.mean(xf * xf, axis=-1, keepdims=True) + NORM_EPS)
    xs = (xf * scale1).astype(BF16)
    xs_all = jnp.concatenate(act_gather(xs, "x", "y"), axis=0)
    wxy, packed_gu = lax.optimization_barrier((wxy, pack_columns(ff_plan, 4 * units, w_gate, w_up, gain2)))
    wxy = w_gather(wxy.reshape(-1, 2 * padded), *STACK).reshape(model, -1)
    packed_gu, wd = lax.optimization_barrier((exchange(packed_gu, UNITS), wd))
    wgu = lax.all_gather(packed_gu.reshape(-1, 8 * units), SHARDS, axis=0, tiled=True)

    small = [conv_w, conv_b[:, None], b_rgate[:, None], b_igate[:, None], lam[:, None], w_rgate, w_igate]
    small_width = sum(v.shape[1] for v in small)
    packed = jnp.pad(jnp.concatenate([w_out] + small, axis=1), ((0, 0), (0, -small_width % 128)))
    halves = w_gather(packed, *STACK)
    mine = lax.dynamic_slice(halves, (core, 0, 0, 0), (1,) + halves.shape[1:])[0]
    theirs = swap(lax.dynamic_slice(halves, (1 - core, 0, 0, 0), (1,) + halves.shape[1:])[0], "c")
    whole = jnp.zeros((2, 2) + packed.shape, BF16)
    whole = lax.dynamic_update_slice(whole, mine[:, None], (0, core, 0, 0))
    whole = lax.dynamic_update_slice(whole, theirs[:, None], (0, 1 - core, 0, 0))
    whole = jnp.pad(whole.reshape(channels, -1), ((0, extra), (0, 0)))
    wo = whole[:, :model]
    rest = whole[:, model : model + taps + 4].astype(F32).T
    lam_all = rest[taps + 3]
    vec = jnp.concatenate([rest[: taps + 1], jax.nn.softplus(-lam_all)[None], rest[taps + 1 : taps + 3]], axis=0)
    at = model + taps + 4
    gates = jnp.zeros((padded, 2 * padded), BF16)
    for g in range(2):
        for n in range(blocks):
            block = whole[n * width : (n + 1) * width, at + g * width : at + (g + 1) * width]
            gates = gates.at[n * width : (n + 1) * width, g * padded + n * width : g * padded + (n + 1) * width].set(block)

    xy = dot32(xs_all, wxy)
    xc, pa, px, before, mixed = rec_forward(meta, xy, vec, gates, rows)

    blocks_r = product_blocks(mixed, wo, False)
    resid = xf + act_scatter(lambda k: blocks_r[k], "x", "y")
    scale2 = lax.rsqrt(jnp.mean(resid * resid, axis=-1, keepdims=True) + NORM_EPS)
    xs2 = shard_order((resid * scale2).astype(BF16))
    early_cot = lax.optimization_barrier((cot, xs_all))[0]
    cot_all = jnp.concatenate(act_gather(early_cot, "x", "zl"), axis=0)
    xs2_all = jnp.concatenate(act_gather(xs2, "x", "zl"), axis=0)
    hidden, d_gu, *blocks_2 = feed_forward(xs2_all, cot_all, wgu, wd)
    d_un2 = shard_order(act_scatter(lambda k: blocks_2[k], "x", "zl"))
    d_resid = cot.astype(F32) + norm_back(d_un2, resid, scale2)
    d_wd = row_contract(hidden, cot_all).astype(BF16)
    d_wgu = row_contract(xs2_all, d_gu).astype(BF16)
    d_mix, d_wd, d_wgu = lax.optimization_barrier((d_resid.astype(BF16), d_wd, d_wgu))
    d_wd = lax.psum_scatter(d_wd, SHARDS, scatter_dimension=0, tiled=True)
    d_wgu = lax.psum_scatter(d_wgu, SHARDS, scatter_dimension=0, tiled=True)
    d_wg, d_wu, d_gain2 = unpack_columns(ff_plan, exchange(d_wgu.reshape(8, -1, 8 * units), UNITS), w_gate, w_up, gain2)

    d_mix_all = jnp.concatenate(act_gather(d_mix, "x", "y"), axis=0)
    dm = back_product(d_mix_all, wo)
    dxy, d_gates, sums = rec_backward(meta, dm, xy, before, pa, px, xc, vec, gates.T, rows)
    blocks_1 = product_blocks(dxy, wxy, True)
    d_un = act_scatter(lambda k: blocks_1[k], "x", "y")
    d_input = (d_resid + norm_back(d_un, xf, scale1)).astype(BF16)
    late_hidden = lax.optimization_barrier((hidden, blocks_1[0]))[0]
    blocks_o = product_blocks(late_hidden, wd, False)
    output = (resid + act_scatter(lambda k: blocks_o[k], "x", "zl")).astype(BF16)
    d_wxy = w_scatter(row_contract(xs_all, dxy).astype(BF16).reshape(2, 2, model // 4, -1), *STACK).astype(BF16)
    d_wx, d_wy, d_gain1 = unpack_columns(rec_plan, exchange(d_wxy.reshape(8, -1, 2 * padded), PLANE), w_x, w_y, gain1)

    def channels_out(v, kind):
        v = v.astype(kind).reshape(2, 2, part, -1)
        size = (2, 1) + v.shape[2:]
        keep = lax.dynamic_slice(v, (0, core, 0, 0), size)[:, 0]
        send = lax.dynamic_slice(v, (0, 1 - core, 0, 0), size)[:, 0]
        out = jnp.zeros((2,) + keep.shape, kind)
        out = lax.dynamic_update_slice(out, keep[None], (core, 0, 0, 0))
        return lax.dynamic_update_slice(out, swap(send, "c")[None], (1 - core, 0, 0, 0))

    d_wo = w_scatter(channels_out(row_contract(mixed, d_mix_all)[:channels], BF16), *STACK)
    sums = jnp.sum(sums.reshape(8, 8, padded), axis=1)
    d_lam_part = -jax.nn.sigmoid(-lam_all) * sums[5]
    d_cols = jnp.concatenate([sums[:5], sums[6:8], d_lam_part[None]], axis=0).T
    row_block = jnp.arange(channels)[:, None] // width
    d_blocks = []
    for g in range(2):
        block = d_gates[:channels, g * padded : g * padded + width]
        for n in range(1, blocks):
            at = g * padded + n * width
            block = jnp.where(row_block == n, d_gates[:channels, at : at + width], block)
        d_blocks.append(block)
    d_small = jnp.concatenate([d_cols[:channels]] + d_blocks, axis=1)
    d_small = lax.psum_scatter(channels_out(d_small, F32).reshape(4 * part, -1), STACK, scatter_dimension=0, tiled=True)
    d_cw, d_cb, d_br, d_bi, d_lam = d_small[:, :4], d_small[:, 4], d_small[:, 5], d_small[:, 6], d_small[:, 7]
    d_wr, d_wi = d_small[:, 8 : 8 + width], d_small[:, 8 + width : 8 + 2 * width]
    return (
        output, d_input, d_gain1[:, 0], d_wx, d_wy, d_cw, d_cb, d_wr, d_br, d_wi, d_bi, d_lam, d_wo,
        d_gain2[:, 0], d_wg, d_wu, d_wd.astype(F32),
    )


def factored(mesh):
    if tuple(mesh.axis_names) != ("fsdp", "seq") or (mesh.shape["fsdp"], mesh.shape["seq"]) != (4, 8):
        return None
    return Mesh(np.asarray(mesh.devices).reshape((2,) * 5), NAMES)


def solution(mesh):
    small = factored(mesh)
    if small is not None:
        whole, groups = P(NAMES), P(("zh", "zl"))
        return jax.shard_map(
            tensor_parallel,
            mesh=small,
            in_specs=(whole, groups) + (whole,) * 16,
            out_specs=(whole,) * 17,
            check_vma=False,
        )
    in_specs = (
        P(("fsdp", "seq"), None),
        P("fsdp", None),
        P(("fsdp", "seq")),
        P(("fsdp", "seq"), None),
        P(("fsdp", "seq"), None),
        P(("fsdp", "seq"), None),
        P(("fsdp", "seq")),
        P(("fsdp", "seq"), None),
        P(("fsdp", "seq")),
        P(("fsdp", "seq"), None),
        P(("fsdp", "seq")),
        P(("fsdp", "seq")),
        P(("fsdp", "seq"), None),
        P(("fsdp", "seq")),
        P(("fsdp", "seq"), None),
        P(("fsdp", "seq"), None),
        P(("fsdp", "seq"), None),
        P(("fsdp", "seq"), None),
    )
    out_specs = (
        P(("fsdp", "seq"), None),
        P(("fsdp", "seq"), None),
        P(("fsdp", "seq")),
        P(("fsdp", "seq"), None),
        P(("fsdp", "seq"), None),
        P(("fsdp", "seq"), None),
        P(("fsdp", "seq")),
        P(("fsdp", "seq"), None),
        P(("fsdp", "seq")),
        P(("fsdp", "seq"), None),
        P(("fsdp", "seq")),
        P(("fsdp", "seq")),
        P(("fsdp", "seq"), None),
        P(("fsdp", "seq")),
        P(("fsdp", "seq"), None),
        P(("fsdp", "seq"), None),
        P(("fsdp", "seq"), None),
    )
    return jax.shard_map(
        on_device, mesh=mesh, in_specs=in_specs, out_specs=out_specs, check_vma=False
    )
```

```python
import functools

import jax
import jax.numpy as jnp
import numpy as np
from jax import lax
from jax.experimental import pallas as pl
from jax.experimental.pallas import tpu as pltpu
from jax.sharding import Mesh
from jax.sharding import PartitionSpec as P

DECAY_C = 8.0
NORM_EPS = 1e-06


def from_behind(x, axis, by):
    size = lax.axis_size(axis)
    pairs = [(i, i + by) for i in range(size) if 0 <= i + by < size]
    return lax.ppermute(x, axis, pairs)


def carried_in(value, axis, join, neutral, backward):
    count, mine = (lax.axis_size(axis), lax.axis_index(axis))
    pieces = jax.tree.map(lambda part: lax.all_gather(part, axis), value)
    if backward:
        pieces = jax.tree.map(lambda part: part[::-1], pieces)
        mine = count - 1 - mine
    subtotal = jax.tree.map(
        lambda part, zero: jnp.full_like(part, 0) + jnp.asarray(zero, part.dtype), value, neutral
    )

    def step(position, subtotal):
        longer = join(subtotal, jax.tree.map(lambda part: part[position], pieces))
        return jax.tree.map(lambda new, old: jnp.where(position < mine, new, old), longer, subtotal)

    return lax.fori_loop(0, count - 1, step, subtotal)


def rms_apply(value, gain):
    scale = lax.rsqrt(jnp.mean(value * value, axis=-1, keepdims=True) + NORM_EPS)
    return value * scale * gain


def combine(earlier, later):
    return (earlier[0] * later[0], later[0] * earlier[1] + later[1])


def lru_terms(pre_r, pre_i, lam_vec, conv_out, start):
    rate = jax.nn.softplus(-lam_vec)
    log_a = -DECAY_C * jax.nn.sigmoid(pre_r) * rate
    decay = jnp.where(start[:, None], 0.0, jnp.exp(log_a))
    scale = jnp.sqrt(jnp.maximum(-jnp.expm1(2.0 * log_a), 0.2 * DECAY_C * rate))
    scale = jnp.where(start[:, None], 1.0, scale)
    return (decay, scale * jax.nn.sigmoid(pre_i) * conv_out)


def row_contract(left, right):
    return lax.dot_general(
        left, right, (((0,), (0,)), ((), ())), preferred_element_type=jnp.float32
    )


def back_product(grad, weight):
    return lax.dot_general(
        grad, weight, (((1,), (1,)), ((), ())), preferred_element_type=jnp.float32
    )


def split_blocks(value, width):
    return value.reshape(value.shape[0], value.shape[1] // width, width)


def block_product(value, weight):
    width = weight.shape[1]
    mats = weight.reshape(weight.shape[0] // width, width, width)
    result = jnp.einsum(
        "nhi,hij->nhj", split_blocks(value, width), mats, preferred_element_type=jnp.float32
    )
    return result.reshape(value.shape[0], -1)


def block_back(grad, weight):
    width = weight.shape[1]
    mats = weight.reshape(weight.shape[0] // width, width, width)
    result = jnp.einsum(
        "nhj,hij->nhi", split_blocks(grad, width), mats, preferred_element_type=jnp.float32
    )
    return result.reshape(grad.shape[0], -1)


def gate_grad(value, grad, width):
    result = jnp.einsum(
        "nhi,nhj->hij",
        split_blocks(value, width),
        split_blocks(grad, width),
        preferred_element_type=jnp.float32,
    )
    return result.reshape(value.shape[1], width)


def seq_starts(lens_row):
    count = lens_row.shape[0]
    before = jnp.arange(count)[None, :] < jnp.arange(count)[:, None]
    return jnp.sum(jnp.where(before, lens_row[None, :], 0), axis=1)


def seq_masks(lens_row, first, rows, taps):
    starts = seq_starts(lens_row)
    place = first + jnp.arange(rows, dtype=jnp.int32)

    def segment(p):
        return jnp.sum((p[:, None] >= starts[None, :]).astype(jnp.int32), axis=1)

    seg_now = segment(place)
    start = jnp.any(place[:, None] == starts[None, :], axis=1)
    same = jnp.stack(
        [
            ((segment(place - k) == seg_now) & (place - k >= 0)).astype(jnp.float32)
            for k in range(taps)
        ],
        0,
    )
    return (start, same)


def on_device(
    layer_input,
    lengths,
    norm1_gain,
    w_x,
    w_y,
    conv_w,
    conv_b,
    w_rgate,
    b_rgate,
    w_igate,
    b_igate,
    lam,
    w_out,
    norm2_gain,
    w_gate,
    w_up,
    w_down,
    cot,
):
    rows = layer_input.shape[0]
    taps = conv_w.shape[1]
    width = w_rgate.shape[1]
    rim = taps - 1
    index = lax.axis_index("seq")
    start, same = seq_masks(lengths[0], index * rows, rows, taps)
    gain_one, wx, wy, cw, cb, wr, br, wi, bi, lam_all, wo = (
        lax.all_gather(norm1_gain, ("fsdp", "seq"), axis=0, tiled=True),
        lax.all_gather(w_x, ("fsdp", "seq"), axis=0, tiled=True),
        lax.all_gather(w_y, ("fsdp", "seq"), axis=0, tiled=True),
        lax.all_gather(conv_w, ("fsdp", "seq"), axis=0, tiled=True),
        lax.all_gather(conv_b, ("fsdp", "seq"), axis=0, tiled=True),
        lax.all_gather(w_rgate, ("fsdp", "seq"), axis=0, tiled=True),
        lax.all_gather(b_rgate, ("fsdp", "seq"), axis=0, tiled=True),
        lax.all_gather(w_igate, ("fsdp", "seq"), axis=0, tiled=True),
        lax.all_gather(b_igate, ("fsdp", "seq"), axis=0, tiled=True),
        lax.all_gather(lam, ("fsdp", "seq"), axis=0, tiled=True),
        lax.all_gather(w_out, ("fsdp", "seq"), axis=0, tiled=True),
    )
    xf = layer_input.astype(jnp.float32)
    gain1 = gain_one.astype(jnp.float32)
    un = rms_apply(xf, gain1).astype(jnp.bfloat16)
    xb = jnp.dot(un, wx, preferred_element_type=jnp.float32).astype(jnp.bfloat16)
    yb = jnp.dot(un, wy, preferred_element_type=jnp.float32)
    gy = jax.nn.gelu(yb)
    rim_in = from_behind(xb[rows - rim :], "seq", 1)
    extended = jnp.concatenate([rim_in, xb], axis=0).astype(jnp.float32)
    cwf = cw.astype(jnp.float32)
    conv = jnp.broadcast_to(cb.astype(jnp.float32)[None, :], (rows, cwf.shape[0]))
    for k in range(taps):
        conv = conv + cwf[:, k][None, :] * extended[rim - k : rim - k + rows] * same[k][:, None]
    xc = conv.astype(jnp.bfloat16)
    xcf = xc.astype(jnp.float32)
    pre_r = block_product(xc, wr) + br.astype(jnp.float32)[None, :]
    pre_i = block_product(xc, wi) + bi.astype(jnp.float32)[None, :]
    lamf = lam_all.astype(jnp.float32)
    decay, drive = lru_terms(pre_r, pre_i, lamf, xcf, start)
    decay_cum, state_loc = lax.associative_scan(combine, (decay, drive), axis=0)
    zero_vec = jnp.zeros((decay.shape[1],), jnp.float32)
    one_vec = jnp.ones((decay.shape[1],), jnp.float32)
    state_in = carried_in(
        (decay_cum[-1], state_loc[-1]), "seq", combine, (one_vec, zero_vec), False
    )[1]
    state = state_loc + decay_cum * state_in[None, :]
    state_prev = jnp.concatenate([state_in[None, :], state[:-1]], axis=0)
    mixed = (state * gy).astype(jnp.bfloat16)
    resid = xf + jnp.dot(mixed, wo, preferred_element_type=jnp.float32)
    gain_two, wg, wu, wd = (
        lax.all_gather(norm2_gain, ("fsdp", "seq"), axis=0, tiled=True),
        lax.all_gather(w_gate, ("fsdp", "seq"), axis=0, tiled=True),
        lax.all_gather(w_up, ("fsdp", "seq"), axis=0, tiled=True),
        lax.all_gather(w_down, ("fsdp", "seq"), axis=0, tiled=True),
    )
    gain2 = gain_two.astype(jnp.float32)
    un2 = rms_apply(resid, gain2).astype(jnp.bfloat16)
    gate_pre = jnp.dot(un2, wg, preferred_element_type=jnp.float32)
    up_pre = jnp.dot(un2, wu, preferred_element_type=jnp.float32)
    gate_act, gelu_back = jax.vjp(jax.nn.gelu, gate_pre)
    hidden = (gate_act * up_pre).astype(jnp.bfloat16)
    output = (resid + jnp.dot(hidden, wd, preferred_element_type=jnp.float32)).astype(jnp.bfloat16)
    grad = cot.astype(jnp.float32)
    gain_two, wg, wu, wd = (
        lax.all_gather(norm2_gain, ("fsdp", "seq"), axis=0, tiled=True),
        lax.all_gather(w_gate, ("fsdp", "seq"), axis=0, tiled=True),
        lax.all_gather(w_up, ("fsdp", "seq"), axis=0, tiled=True),
        lax.all_gather(w_down, ("fsdp", "seq"), axis=0, tiled=True),
    )
    gain2 = gain_two.astype(jnp.float32)
    d_wd = row_contract(hidden, cot)
    d_hidden = back_product(cot, wd)
    d_gate = gelu_back(d_hidden * up_pre)[0].astype(jnp.bfloat16)
    d_up = (d_hidden * gate_act).astype(jnp.bfloat16)
    d_wg = row_contract(un2, d_gate)
    d_wu = row_contract(un2, d_up)
    d_un2 = back_product(d_gate, wg) + back_product(d_up, wu)
    norm_two_back = jax.vjp(rms_apply, resid, gain2)[1]
    d_resid_norm, d_gain2 = norm_two_back(d_un2)
    mlp_grads = (
        lax.psum_scatter(d_gain2, ("fsdp", "seq"), scatter_dimension=0, tiled=True),
        lax.psum_scatter(d_wg, ("fsdp", "seq"), scatter_dimension=0, tiled=True),
        lax.psum_scatter(d_wu, ("fsdp", "seq"), scatter_dimension=0, tiled=True),
        lax.psum_scatter(d_wd, ("fsdp", "seq"), scatter_dimension=0, tiled=True),
    )
    d_resid = grad + d_resid_norm
    gain_one, wx, wy, cw, cb, wr, br, wi, bi, lam_all, wo = (
        lax.all_gather(norm1_gain, ("fsdp", "seq"), axis=0, tiled=True),
        lax.all_gather(w_x, ("fsdp", "seq"), axis=0, tiled=True),
        lax.all_gather(w_y, ("fsdp", "seq"), axis=0, tiled=True),
        lax.all_gather(conv_w, ("fsdp", "seq"), axis=0, tiled=True),
        lax.all_gather(conv_b, ("fsdp", "seq"), axis=0, tiled=True),
        lax.all_gather(w_rgate, ("fsdp", "seq"), axis=0, tiled=True),
        lax.all_gather(b_rgate, ("fsdp", "seq"), axis=0, tiled=True),
        lax.all_gather(w_igate, ("fsdp", "seq"), axis=0, tiled=True),
        lax.all_gather(b_igate, ("fsdp", "seq"), axis=0, tiled=True),
        lax.all_gather(lam, ("fsdp", "seq"), axis=0, tiled=True),
        lax.all_gather(w_out, ("fsdp", "seq"), axis=0, tiled=True),
    )
    gain1 = gain_one.astype(jnp.float32)
    cwf = cw.astype(jnp.float32)
    lamf = lam_all.astype(jnp.float32)
    d_mix = d_resid.astype(jnp.bfloat16)
    d_wo = row_contract(mixed, d_mix)
    d_mixed = back_product(d_mix, wo)
    d_state = d_mixed * gy
    gelu_y_back = jax.vjp(jax.nn.gelu, yb)[1]
    d_yb = gelu_y_back(d_mixed * state)[0].astype(jnp.bfloat16)
    next_decay = jnp.concatenate([decay[1:], one_vec[None, :]], axis=0)
    decay_after, adjoint_loc = lax.associative_scan(
        combine, (next_decay, d_state), reverse=True, axis=0
    )
    send_decay = decay[0] * decay_after[0]
    send_adjoint = decay[0] * adjoint_loc[0]
    adjoint_in = carried_in((send_decay, send_adjoint), "seq", combine, (one_vec, zero_vec), True)[
        1
    ]
    adjoint = adjoint_loc + decay_after * adjoint_in[None, :]

    def local_lru(pr, pi, lv, cv):
        return lru_terms(pr, pi, lv, cv, start)

    lru_back = jax.vjp(local_lru, pre_r, pre_i, lamf, xcf)[1]
    d_pre_r, d_pre_i, d_lam, d_xc_local = lru_back((adjoint * state_prev, adjoint))
    d_pr = d_pre_r.astype(jnp.bfloat16)
    d_pi = d_pre_i.astype(jnp.bfloat16)
    d_wr = gate_grad(xc, d_pr, width)
    d_wi = gate_grad(xc, d_pi, width)
    d_br = jnp.sum(d_pr.astype(jnp.float32), axis=0)
    d_bi = jnp.sum(d_pi.astype(jnp.float32), axis=0)
    d_xc = d_xc_local + block_back(d_pr, wr) + block_back(d_pi, wi)
    d_cb = jnp.sum(d_xc, axis=0)
    d_cw = jnp.stack(
        [
            jnp.sum(d_xc * extended[rim - k : rim - k + rows] * same[k][:, None], axis=0)
            for k in range(taps)
        ],
        axis=1,
    )
    d_extended = jnp.zeros((rows + rim, d_xc.shape[1]), jnp.float32)
    for k in range(taps):
        d_extended = d_extended + jnp.pad(
            d_xc * cwf[:, k][None, :] * same[k][:, None], ((rim - k, k), (0, 0))
        )
    rim_back = from_behind(d_extended[:rim], "seq", -1)
    d_xb = (d_extended[rim:] + jnp.pad(rim_back, ((rows - rim, 0), (0, 0)))).astype(jnp.bfloat16)
    d_wx = row_contract(un, d_xb)
    d_wy = row_contract(un, d_yb)
    d_un = back_product(d_xb, wx) + back_product(d_yb, wy)
    norm_one_back = jax.vjp(rms_apply, xf, gain1)[1]
    d_x_norm, d_gain1 = norm_one_back(d_un)
    d_input = (d_resid + d_x_norm).astype(jnp.bfloat16)
    block_grads = (
        lax.psum_scatter(d_gain1, ("fsdp", "seq"), scatter_dimension=0, tiled=True),
        lax.psum_scatter(d_wx, ("fsdp", "seq"), scatter_dimension=0, tiled=True),
        lax.psum_scatter(d_wy, ("fsdp", "seq"), scatter_dimension=0, tiled=True),
        lax.psum_scatter(d_cw, ("fsdp", "seq"), scatter_dimension=0, tiled=True),
        lax.psum_scatter(d_cb, ("fsdp", "seq"), scatter_dimension=0, tiled=True),
        lax.psum_scatter(d_wr, ("fsdp", "seq"), scatter_dimension=0, tiled=True),
        lax.psum_scatter(d_br, ("fsdp", "seq"), scatter_dimension=0, tiled=True),
        lax.psum_scatter(d_wi, ("fsdp", "seq"), scatter_dimension=0, tiled=True),
        lax.psum_scatter(d_bi, ("fsdp", "seq"), scatter_dimension=0, tiled=True),
        lax.psum_scatter(d_lam, ("fsdp", "seq"), scatter_dimension=0, tiled=True),
        lax.psum_scatter(d_wo, ("fsdp", "seq"), scatter_dimension=0, tiled=True),
    )
    return (
        output,
        d_input,
        block_grads[0],
        block_grads[1],
        block_grads[2],
        block_grads[3],
        block_grads[4],
        block_grads[5],
        block_grads[6],
        block_grads[7],
        block_grads[8],
        block_grads[9],
        block_grads[10],
        mlp_grads[0],
        mlp_grads[1],
        mlp_grads[2],
        mlp_grads[3],
    )


NAMES = ("zh", "zl", "y", "x", "c")
F32 = jnp.float32
BF16 = jnp.bfloat16
GELU_C = 0.7978845608
GELU_K = 0.044715


def after(v, *first):
    return lax.optimization_barrier((v,) + first)[0]


def swap(v, name):
    return lax.ppermute(v, name, [(0, 1), (1, 0)])


def add16(one, two):
    return (one.astype(F32) + two.astype(F32)).astype(BF16)


def act_gather(v, a, b, second=(), third=()):
    h = v.shape[0] // 2
    near, from_a, from_b = swap(v, "c"), swap(v, a), swap(v, b)
    from_a, from_b, near = lax.optimization_barrier((from_a, from_b, near) + tuple(second))[:3]
    far0, far1 = swap(from_a[:h], b), swap(from_b[h:], a)
    near_a, near_b = swap(from_a, "c"), swap(from_b, "c")
    far0, far1, near_a, near_b = lax.optimization_barrier((far0, far1, near_a, near_b) + tuple(third))[:4]
    far = jnp.concatenate([far0, far1], axis=0)
    return [v, near, from_a, near_a, from_b, near_b, far, swap(far, "c")]


def act_scatter(blocks, a, b, second=(), third=(), last=None):
    far, to_a, to_b = [add16(blocks[k], swap(blocks[k + 1], "c")) for k in (6, 2, 4)]
    far = after(far, *second)
    own = blocks[0].astype(F32) + swap(blocks[1], "c").astype(F32)
    h = far.shape[0] // 2
    in_b, in_a = swap(far[:h], b), swap(far[h:], a)
    to_a = jnp.concatenate([add16(to_a[:h], in_b), to_a[h:]], axis=0)
    to_b = jnp.concatenate([to_b[:h], add16(to_b[h:], in_a)], axis=0)
    to_a, to_b = lax.optimization_barrier((to_a, to_b) + tuple(third))[:2]
    from_a, from_b = swap(to_a, a), swap(to_b, b)
    if last is not None:
        from_a, from_b = lax.optimization_barrier((from_a, from_b) + tuple(last(to_a)))[:2]
    return own + from_a.astype(F32) + from_b.astype(F32)


def w_parts(v, w1, w2, second=()):
    from_1, from_2 = lax.optimization_barrier((swap(v, w1), swap(v, w2)) + tuple(second))[:2]
    return [v, from_1, from_2, swap(from_1, w2)]


def w_place(parts, w1, w2):
    i1, i2 = lax.axis_index(w1), lax.axis_index(w2)
    out = jnp.zeros((2, 2) + parts[0].shape, parts[0].dtype)
    tail = (0,) * parts[0].ndim
    for part, j1, j2 in zip(parts, (i1, 1 - i1, i1, 1 - i1), (i2, i2, 1 - i2, 1 - i2)):
        out = lax.dynamic_update_slice(out, part[None, None], (j1, j2) + tail)
    return out


def w_scatter(v, w1, w2):
    i1, i2 = lax.axis_index(w1), lax.axis_index(w2)

    def get(j1, j2):
        return lax.dynamic_slice(v, (j1, j2) + (0,) * (v.ndim - 2), (1, 1) + v.shape[2:])[0, 0]

    other = get(1 - i1, i2).astype(F32) + swap(get(1 - i1, 1 - i2), w2).astype(F32)
    other = other.astype(v.dtype)
    own = get(i1, i2).astype(F32) + swap(get(i1, 1 - i2), w2).astype(F32)
    return own + swap(other, w1).astype(F32), other


def pack_kernel(plan, a_ref, b_ref, gain_ref, out_ref):
    half = out_ref.shape[2] // 2
    for first, ref in ((0, a_ref), (half, b_ref)):
        scaled = (ref[...].astype(F32) * gain_ref[...]).astype(BF16)
        for dest, pieces in enumerate(plan):
            at = first
            for source, size in pieces:
                out_ref[dest, :, at : at + size] = scaled[:, source : source + size]
                at += size
            if at < first + half:
                out_ref[dest, :, at : first + half] = jnp.zeros((scaled.shape[0], first + half - at), BF16)


def unpack_kernel(plan, ga_ref, gb_ref, a_ref, b_ref, gain_ref, da_ref, db_ref, dgain_ref):
    total = jnp.zeros(dgain_ref.shape, F32)
    for grad_ref, ref, out in ((ga_ref, a_ref, da_ref), (gb_ref, b_ref, db_ref)):
        for dest, pieces in enumerate(plan):
            at = 0
            for source, size in pieces:
                piece = grad_ref[dest, :, at : at + size].astype(F32)
                out[:, source : source + size] = piece * gain_ref[...]
                weight = ref[:, source : source + size].astype(F32)
                total = total + jnp.sum(piece * weight, axis=1, keepdims=True)
                at += size
    dgain_ref[...] = total


def pack_columns(plan, half, one, two, gain):
    return pl.pallas_call(
        functools.partial(pack_kernel, plan),
        out_shape=jax.ShapeDtypeStruct((8, one.shape[0], 2 * half), BF16),
        compiler_params=pltpu.CompilerParams(vmem_limit_bytes=24 << 20),
        cost_estimate=pl.CostEstimate(flops=4 * one.size, transcendentals=0, bytes_accessed=8 * one.size),
        name="pack_columns",
    )(one, two, gain)


def unpack_columns(plan, grad_one, grad_two, one, two, gain):
    half = grad_one.shape[2] if grad_two is not None else grad_one.shape[2] // 2
    rows, cols = one.shape
    whole = lambda *shape: pl.BlockSpec(shape, lambda i: (0,) * len(shape))
    grads = [
        pl.BlockSpec((8, rows, half), lambda i: (0, 0, 0)),
        pl.BlockSpec((8, rows, half), lambda i: (0, 0, 0 if grad_two is not None else 1)),
    ]
    shape = jax.ShapeDtypeStruct(one.shape, F32)
    return pl.pallas_call(
        functools.partial(unpack_kernel, plan),
        grid=(1,),
        in_specs=grads + [whole(rows, cols), whole(rows, cols), whole(rows, 1)],
        out_specs=[whole(rows, cols), whole(rows, cols), whole(rows, 1)],
        out_shape=[shape, shape, jax.ShapeDtypeStruct((rows, 1), F32)],
        compiler_params=pltpu.CompilerParams(vmem_limit_bytes=32 << 20),
        cost_estimate=pl.CostEstimate(flops=8 * one.size, transcendentals=0, bytes_accessed=16 * one.size),
        name="unpack_columns",
    )(grad_one, grad_one if grad_two is None else grad_two, one, two, gain)


def exchange(v, tp):
    return lax.all_to_all(v, tp, split_axis=0, concat_axis=0, tiled=True)


def neg_expm1(v):
    series = 1.0 + v * (1.0 / 10.0)
    for n in range(9, 1, -1):
        series = 1.0 + v * (1.0 / n) * series
    return jnp.where(v > -0.5, -v * series, 1.0 - jnp.exp(v))


def gate_terms(pa, px, rate, start):
    sr = jax.nn.sigmoid(pa)
    si = jax.nn.sigmoid(px)
    la = -DECAY_C * sr * rate
    decay = jnp.where(start, 0.0, jnp.exp(la))
    e2 = neg_expm1(2.0 * la)
    floor = 0.2 * DECAY_C * rate
    scale = jnp.where(start, 1.0, jnp.sqrt(jnp.maximum(e2, floor)))
    return sr, si, decay, e2, floor, scale


def gelu(v):
    return 0.5 * v * (1.0 + jnp.tanh(GELU_C * (v + GELU_K * v * v * v)))


def gelu_both(v):
    t = jnp.tanh(GELU_C * (v + GELU_K * v * v * v))
    half = 0.5 * (1.0 + t)
    return v * half, half + 0.5 * v * (1.0 - t * t) * GELU_C * (1.0 + 3.0 * GELU_K * v * v)


def scan_tile(decay, drive, into):
    row = lax.broadcasted_iota(jnp.int32, decay.shape, 0)
    for by in (1, 2, 4):
        keep = row >= by
        drive = jnp.where(keep, decay * pltpu.roll(drive, by, 0) + drive, drive)
        decay = jnp.where(keep, decay * pltpu.roll(decay, by, 0), decay)
    return decay * into + drive


def scan_tile_back(decay, drive, into):
    row = lax.broadcasted_iota(jnp.int32, decay.shape, 0)
    for by in (1, 2, 4):
        keep = row < 8 - by
        drive = jnp.where(keep, decay * pltpu.roll(drive, 8 - by, 0) + drive, drive)
        decay = jnp.where(keep, decay * pltpu.roll(decay, 8 - by, 0), decay)
    return decay * into + drive


STEP = 16


def since_start(meta_ref, place, width):
    at = place + lax.broadcasted_iota(jnp.int32, (STEP, 128), 0)
    since, start = at, 0
    for n in range(1, meta_ref.shape[0] - 1):
        start = start + meta_ref[n]
        since = jnp.where(at >= start, at - start, since)
    return jnp.concatenate([since] * (width // 128), axis=1)


def rec_fwd_kernel(meta_ref, xb_ref, yb_ref, vec_ref, w_ref, xc_ref, pa_ref, px_ref, sp_ref, mixed_ref, ext, carry):
    rows, width = xb_ref.shape
    base = pl.program_id(0) * rows

    @pl.when(pl.program_id(0) == 0)
    def _():
        ext[0:8, :] = jnp.zeros((8, width), F32)
        carry[...] = jnp.zeros_like(carry)

    ext[8 : 8 + rows, :] = xb_ref[...].astype(BF16).astype(F32)

    def conv_step(r, _):
        at = pl.multiple_of(r * STEP, STEP)
        window = ext[pl.ds(at, STEP + 8), :]
        since = since_start(meta_ref, base + at, width)
        total = vec_ref[4:5, :] + vec_ref[0:1, :] * window[8:, :]
        for k in range(1, 4):
            moved = jnp.where(since >= k, window[8 - k : 8 - k + STEP, :], 0.0)
            total = total + vec_ref[k : k + 1, :] * moved
        xc_ref[pl.ds(at, STEP), :] = total.astype(BF16)
        return 0

    lax.fori_loop(0, rows // STEP, conv_step, 0, unroll=2)
    ext[0:8, :] = ext[rows : rows + 8, :]
    xc = xc_ref[...]
    pa_ref[...] = jnp.dot(xc, w_ref[:, :width], preferred_element_type=F32) + vec_ref[6:7, :]
    px_ref[...] = jnp.dot(xc, w_ref[:, width:], preferred_element_type=F32) + vec_ref[7:8, :]
    top = lax.broadcasted_iota(jnp.int32, (8, width), 0) == 0

    def scan_step(r, held):
        here = pl.ds(pl.multiple_of(r * STEP, STEP), STEP)
        start = since_start(meta_ref, base + r * STEP, width) == 0
        _, si, decay, _, _, scale = gate_terms(pa_ref[here, :], px_ref[here, :], vec_ref[5:6, :], start)
        drive = scale * si * xc_ref[here, :].astype(F32)
        states, before = [], []
        for part in range(0, STEP, 8):
            now = scan_tile(decay[part : part + 8], drive[part : part + 8], held)
            states.append(now)
            before.append(jnp.where(top, held, pltpu.roll(now, 1, 0)))
            held = jnp.broadcast_to(now[7:8, :], (8, width))
        sp_ref[here, :] = jnp.concatenate(before, axis=0)
        mixed_ref[here, :] = (jnp.concatenate(states, axis=0) * gelu(yb_ref[here, :])).astype(BF16)
        return held

    carry[...] = lax.fori_loop(0, rows // STEP, scan_step, carry[...], unroll=2)


def rec_bwd_kernel(
    meta_ref, dm_ref, yb_ref, sp_ref, pa_ref, px_ref, xc_ref, xb_ref, vec_ref, wt_ref,
    dxy_ref, dw_ref, sum_ref, ext, dp, carry,
):
    rows, width = xb_ref.shape
    base = (pl.num_programs(0) - 1 - pl.program_id(0)) * rows

    @pl.when(pl.program_id(0) == 0)
    def _():
        ext[rows : rows + 8, :] = jnp.zeros((8, width), F32)
        carry[...] = jnp.zeros_like(carry)
        dw_ref[...] = jnp.zeros_like(dw_ref)
        sum_ref[...] = jnp.zeros_like(sum_ref)

    row = lax.broadcasted_iota(jnp.int32, (8, width), 0)
    steps = rows // STEP

    def fold(v):
        return v[0:8, :] + v[8:16, :]

    def scan_step(i, state):
        held, s_rate, s_r, s_i = state
        at = pl.multiple_of((steps - 1 - i) * STEP, STEP)
        here = pl.ds(at, STEP)
        start = since_start(meta_ref, base + at, width) == 0
        rate = vec_ref[5:6, :]
        sr, si, decay, e2, floor, scale = gate_terms(pa_ref[here, :], px_ref[here, :], rate, start)
        xc = xc_ref[here, :].astype(F32)
        before = sp_ref[here, :]
        gate = si * xc
        now = decay * before + scale * gate
        dm = dm_ref[here, :]
        act, slope = gelu_both(yb_ref[here, :])
        dxy_ref[here, width:] = (dm * now * slope).astype(BF16)
        dstate = dm * act
        parts = []
        for part in range(STEP - 8, -1, -8):
            here_decay = decay[part : part + 8]
            coef = jnp.where(row == 7, 1.0, pltpu.roll(here_decay, 7, 0))
            adj = scan_tile_back(coef, dstate[part : part + 8], held)
            held = jnp.broadcast_to((here_decay * adj)[0:1, :], (8, width))
            parts.append(adj)
        adj = jnp.concatenate(parts[::-1], axis=0)
        d_scale = adj * gate
        d_half = jnp.where(start, 0.0, d_scale * 0.5 / scale)
        share = jnp.where(e2 > floor, 1.0, jnp.where(e2 == floor, 0.5, 0.0))
        kept = adj * scale
        d_la = decay * (adj * before - 2.0 * decay * d_half * share)
        d_rate = -DECAY_C * sr * d_la + (0.2 * DECAY_C) * d_half * (1.0 - share)
        d_pa = (-DECAY_C * rate * d_la * sr * (1.0 - sr)).astype(BF16)
        d_px = (kept * xc * si * (1.0 - si)).astype(BF16)
        dp[here, :width] = d_pa
        dp[here, width:] = d_px
        ext[here, :] = kept * si
        return held, s_rate + fold(d_rate), s_r + fold(d_pa.astype(F32)), s_i + fold(d_px.astype(F32))

    held, s_rate, s_r, s_i = lax.fori_loop(
        0, steps, scan_step, (carry[...], sum_ref[40:48, :], sum_ref[48:56, :], sum_ref[56:64, :]), unroll=2
    )
    carry[...] = held
    sum_ref[40:48, :] = s_rate
    sum_ref[48:56, :] = s_r
    sum_ref[56:64, :] = s_i
    ext[0:rows, :] += jnp.dot(dp[...], wt_ref[...], preferred_element_type=F32)
    dw_ref[...] += row_contract(xc_ref[...], dp[...])

    def conv_step(r, sums):
        at = pl.multiple_of(r * STEP, STEP)
        window = ext[pl.ds(at, STEP + 8), :]
        xb = xb_ref[pl.ds(at, STEP), :].astype(BF16).astype(F32)
        total = jnp.zeros((STEP, width), F32)
        new = []
        for k in range(4):
            moved = window[k : k + STEP, :]
            if k:
                moved = jnp.where(since_start(meta_ref, base + at + k, width) >= k, moved, 0.0)
            total = total + vec_ref[k : k + 1, :] * moved
            new.append(sums[k] + fold(moved * xb))
        new.append(sums[4] + fold(window[:STEP, :]))
        dxy_ref[pl.ds(at, STEP), :width] = total.astype(BF16)
        return tuple(new)

    sums = lax.fori_loop(0, steps, conv_step, tuple(sum_ref[8 * q : 8 * q + 8, :] for q in range(5)), unroll=2)
    for q in range(5):
        sum_ref[8 * q : 8 * q + 8, :] = sums[q]
    ext[rows : rows + 8, :] = ext[0:8, :]


def place_kernel(width, taps, meta_ref, *refs):
    parts, (wo_ref, gates_ref, vec_ref, cols) = refs[:4], refs[4:]
    part, model = parts[0].shape[0], wo_ref.shape[1]
    padded = wo_ref.shape[0]
    zl, core = meta_ref[0], meta_ref[1]
    lanes = cols.shape[1]
    wo_ref[4 * part :, :] = jnp.zeros((padded - 4 * part, model), BF16)
    gates_ref[...] = jnp.zeros_like(gates_ref)
    cols[4 * part :, :] = jnp.zeros((padded - 4 * part, lanes), F32)
    for n in range(4):
        here_zl = zl if n % 2 == 0 else 1 - zl
        half = core if n < 2 else 1 - core
        at = pl.multiple_of((here_zl * 2 + half) * part, STEP)
        wo_ref[pl.ds(at, part), :] = parts[n][:, :model]
        rest = parts[n][:, model:]
        cols[pl.ds(at, part), :] = rest[:, :lanes].astype(F32)
        for block in range(2):

            @pl.when(here_zl == block)
            def _(rest=rest, at=at, block=block):
                for g in range(2):
                    source = taps + 4 + g * width
                    target = g * padded + block * width
                    gates_ref[pl.ds(at, part), target : target + width] = rest[:, source : source + width]

    vec_ref[...] = cols[...].T[:8, :]


def place_channels(meta, parts, model, width, taps):
    part = parts[0].shape[0]
    padded = -(-4 * part // 128) * 128
    shape = jax.ShapeDtypeStruct
    return pl.pallas_call(
        functools.partial(place_kernel, width, taps),
        grid_spec=pltpu.PrefetchScalarGridSpec(
            num_scalar_prefetch=1,
            grid=(1,),
            in_specs=[pl.BlockSpec(v.shape, lambda i, m: (0, 0)) for v in parts],
            out_specs=[
                pl.BlockSpec((padded, model), lambda i, m: (0, 0)),
                pl.BlockSpec((padded, 2 * padded), lambda i, m: (0, 0)),
                pl.BlockSpec((8, padded), lambda i, m: (0, 0)),
            ],
            scratch_shapes=[pltpu.VMEM((padded, 128), F32)],
        ),
        out_shape=[shape((padded, model), BF16), shape((padded, 2 * padded), BF16), shape((8, padded), F32)],
        compiler_params=pltpu.CompilerParams(vmem_limit_bytes=24 << 20),
        cost_estimate=pl.CostEstimate(flops=padded * model, transcendentals=0, bytes_accessed=8 * padded * model),
        name="place_channels",
    )(meta, *parts)


def rec_forward(meta, xy, vec, w, tile):
    total, width = xy.shape[0], xy.shape[1] // 2
    block = pl.BlockSpec((tile, width), lambda i, m: (i ^ m[0], 0))
    right = pl.BlockSpec((tile, width), lambda i, m: (i ^ m[0], 1))
    whole = lambda v: pl.BlockSpec(v.shape, lambda i, m: (0, 0))
    return pl.pallas_call(
        rec_fwd_kernel,
        grid_spec=pltpu.PrefetchScalarGridSpec(
            num_scalar_prefetch=1,
            grid=(total // tile,),
            in_specs=[block, right, whole(vec), whole(w)],
            out_specs=[block] * 5,
            scratch_shapes=[pltpu.VMEM((tile + 8, width), F32), pltpu.VMEM((8, width), F32)],
        ),
        out_shape=[jax.ShapeDtypeStruct((total, width), t) for t in (BF16, F32, F32, F32, BF16)],
        compiler_params=pltpu.CompilerParams(vmem_limit_bytes=32 << 20),
        cost_estimate=pl.CostEstimate(
            flops=100 * total * width + 4 * total * width * width,
            transcendentals=6 * total * width,
            bytes_accessed=24 * total * width,
        ),
        name="recurrence_forward",
    )(meta, xy, xy, vec, w)


def rec_backward(meta, dm, xy, sp, pa, px, xc, vec, wt, tile):
    total, width = dm.shape
    steps = total // tile
    block = pl.BlockSpec((tile, width), lambda i, m: ((steps - 1 - i) ^ m[0], 0))
    right = pl.BlockSpec((tile, width), lambda i, m: ((steps - 1 - i) ^ m[0], 1))
    whole = lambda v: pl.BlockSpec(v.shape, lambda i, m: (0, 0))
    return pl.pallas_call(
        rec_bwd_kernel,
        grid_spec=pltpu.PrefetchScalarGridSpec(
            num_scalar_prefetch=1,
            grid=(steps,),
            in_specs=[block, right, block, block, block, block, block, whole(vec), whole(wt)],
            out_specs=[
                pl.BlockSpec((tile, 2 * width), lambda i, m: ((steps - 1 - i) ^ m[0], 0)),
                pl.BlockSpec((width, 2 * width), lambda i, m: (0, 0)),
                pl.BlockSpec((64, width), lambda i, m: (0, 0)),
            ],
            scratch_shapes=[
                pltpu.VMEM((tile + 8, width), F32),
                pltpu.VMEM((tile, 2 * width), BF16),
                pltpu.VMEM((8, width), F32),
            ],
        ),
        out_shape=[
            jax.ShapeDtypeStruct((total, 2 * width), BF16),
            jax.ShapeDtypeStruct((width, 2 * width), F32),
            jax.ShapeDtypeStruct((64, width), F32),
        ],
        compiler_params=pltpu.CompilerParams(vmem_limit_bytes=32 << 20),
        cost_estimate=pl.CostEstimate(
            flops=180 * total * width + 8 * total * width * width,
            transcendentals=6 * total * width,
            bytes_accessed=30 * total * width,
        ),
        name="recurrence_backward",
    )(meta, dm, xy, sp, pa, px, xc, xy, vec, wt)


def dot32(one, two):
    return jnp.dot(one, two, preferred_element_type=F32)


def columns_of(width, most):
    return next(n for n in range(min(width, most), 0, -128) if width % n == 0)


def store_blocks(step, value_ref, outs, rows):
    per = value_ref.shape[0] // rows
    for n, out in enumerate(outs):

        @pl.when(step == n // per)
        def _(n=n, out=out):
            out[...] = value_ref[(n % per) * rows : (n % per + 1) * rows, :]


def blocks_kernel(flip, a_ref, w_ref, *rest):
    outs, value = rest[:-1], rest[-1]
    model = outs[0].shape[1]
    wide = columns_of(model, 512)
    a = a_ref[...]
    for at in range(0, model, wide):
        if flip:
            part = back_product(a, w_ref[at : at + wide, :])
        else:
            part = dot32(a, w_ref[:, at : at + wide])
        value[:, at : at + wide] = part.astype(BF16)
    store_blocks(pl.program_id(0), value, outs, outs[0].shape[0])


def product_blocks(a, w, flip):
    total, deep = a.shape
    model = w.shape[0] if flip else w.shape[1]
    tile, rows = total // 4, total // 8
    return pl.pallas_call(
        functools.partial(blocks_kernel, flip),
        grid=(4,),
        in_specs=[pl.BlockSpec((tile, deep), lambda i: (i, 0)), pl.BlockSpec(w.shape, lambda i: (0, 0))],
        out_specs=[pl.BlockSpec((rows, model), lambda i: (0, 0))] * 8,
        out_shape=[jax.ShapeDtypeStruct((rows, model), BF16)] * 8,
        scratch_shapes=[pltpu.VMEM((tile, model), BF16)],
        compiler_params=pltpu.CompilerParams(vmem_limit_bytes=44 << 20),
        cost_estimate=pl.CostEstimate(
            flops=2 * total * deep * model,
            transcendentals=0,
            bytes_accessed=2 * (total * deep + w.size + total * model),
        ),
        name="product_blocks",
    )(a, w)


def join_pieces(step, pieces, all_ref):
    rows = pieces[0].shape[0]
    per = all_ref.shape[0] // rows
    for n, piece in enumerate(pieces):

        @pl.when(step == n // per)
        def _(n=n, piece=piece):
            all_ref[(n % per) * rows : (n % per + 1) * rows, :] = piece[...]


def pieces_kernel(flip, *refs):
    pieces, (w_ref, all_ref, out_ref) = refs[:8], refs[8:]
    join_pieces(pl.program_id(0), pieces, all_ref)
    a = all_ref[...]
    wide = columns_of(out_ref.shape[1], 384)
    for at in range(0, out_ref.shape[1], wide):
        if flip:
            out_ref[:, at : at + wide] = back_product(a, w_ref[at : at + wide, :])
        else:
            out_ref[:, at : at + wide] = dot32(a, w_ref[:, at : at + wide])


def pieces_product(pieces, w, flip):
    rows, deep = pieces[0].shape
    total, tile = 8 * rows, 2 * rows
    cols = w.shape[0] if flip else w.shape[1]
    once = lambda v: pl.BlockSpec(v.shape, lambda i: (0, 0), pipeline_mode=pl.Buffered(1))
    return pl.pallas_call(
        functools.partial(pieces_kernel, flip),
        grid=(4,),
        in_specs=[once(v) for v in pieces] + [once(w)],
        out_specs=[pl.BlockSpec((tile, deep), lambda i: (i, 0)), pl.BlockSpec((tile, cols), lambda i: (i, 0))],
        out_shape=[jax.ShapeDtypeStruct((total, deep), BF16), jax.ShapeDtypeStruct((total, cols), F32)],
        compiler_params=pltpu.CompilerParams(vmem_limit_bytes=44 << 20),
        cost_estimate=pl.CostEstimate(
            flops=2 * total * deep * cols, transcendentals=0, bytes_accessed=4 * total * (deep + cols) + 2 * w.size
        ),
        name="pieces_product",
    )(*pieces, w)


def ff_kernel(*refs):
    pieces, (cot_ref, wg_ref, wu_ref, wd_ref, x_ref, hidden_ref, dgt_ref, dup_ref), rest = refs[:8], refs[8:16], refs[16:]
    outs, value = rest[:-1], rest[-1]
    half, model = wd_ref.shape
    narrow, wide = columns_of(half, 256), columns_of(model, 512)
    join_pieces(pl.program_id(0), pieces, x_ref)
    x, cot = x_ref[...], cot_ref[...]
    for at in range(0, half, narrow):
        gt = dot32(x, wg_ref[:, at : at + narrow])
        up = dot32(x, wu_ref[:, at : at + narrow])
        dh = back_product(cot, wd_ref[at : at + narrow, :])
        act, slope = gelu_both(gt)
        hidden_ref[:, at : at + narrow] = (act * up).astype(BF16)
        dgt_ref[:, at : at + narrow] = (dh * up * slope).astype(BF16)
        dup_ref[:, at : at + narrow] = (dh * act).astype(BF16)
    d_gt, d_up = dgt_ref[...], dup_ref[...]
    for at in range(0, model, wide):
        part = back_product(d_gt, wg_ref[at : at + wide, :]) + back_product(d_up, wu_ref[at : at + wide, :])
        value[:, at : at + wide] = part.astype(BF16)
    store_blocks(pl.program_id(0), value, outs, outs[0].shape[0])


def feed_forward(pieces, cot, wgu, wd):
    rows, model = pieces[0].shape
    half = wd.shape[0]
    total, tile = 8 * rows, 2 * rows
    at = lambda cols: pl.BlockSpec((tile, cols), lambda i: (i, 0))
    once = lambda v: pl.BlockSpec(v.shape, lambda i: (0, 0), pipeline_mode=pl.Buffered(1))
    side = lambda n: pl.BlockSpec((model, half), lambda i: (0, n), pipeline_mode=pl.Buffered(1))
    widths = (model, half, half, half)
    return pl.pallas_call(
        ff_kernel,
        grid=(4,),
        in_specs=[once(v) for v in pieces] + [at(model), side(0), side(1), once(wd)],
        out_specs=[at(n) for n in widths] + [pl.BlockSpec((rows, model), lambda i: (0, 0))] * 8,
        out_shape=[jax.ShapeDtypeStruct((total, n), BF16) for n in widths] + [jax.ShapeDtypeStruct((rows, model), BF16)] * 8,
        scratch_shapes=[pltpu.VMEM((tile, model), BF16)],
        compiler_params=pltpu.CompilerParams(vmem_limit_bytes=56 << 20),
        cost_estimate=pl.CostEstimate(
            flops=10 * total * model * half,
            transcendentals=total * half,
            bytes_accessed=2 * (4 * total * model + 3 * half * model + 3 * total * half),
        ),
        name="feed_forward",
    )(*pieces, cot, wgu, wgu, wd)


def norm_back(dv, v, scale):
    return scale * dv - scale * scale * scale * v * jnp.mean(dv * v, axis=-1, keepdims=True)


PLANE = ("y", "x", "c")
STACK = ("zh", "zl")


def tensor_parallel(
    layer_input, lengths, norm1_gain, w_x, w_y, conv_w, conv_b, w_rgate, b_rgate, w_igate, b_igate, lam,
    w_out, norm2_gain, w_gate, w_up, w_down, cot,
):
    rows, model = layer_input.shape
    taps = conv_w.shape[1]
    width = w_rgate.shape[1]
    part = w_out.shape[0]
    channels = 4 * part
    padded = -(-channels // 128) * 128
    extra = padded - channels
    blocks = channels // width
    units = w_down.shape[0]
    core = lax.axis_index("c")
    me = (lax.axis_index("y") * 2 + lax.axis_index("x")) * 2 + core
    meta = jnp.concatenate([me.astype(jnp.int32)[None], lengths[0].astype(jnp.int32)])

    gain1 = norm1_gain.astype(F32)[:, None]
    gain2 = norm2_gain.astype(F32)[:, None]
    rec_plan = tuple(
        tuple((((2 * (t % 2) + z) * 4 + t // 2) * width, width) for z in range(2)) for t in range(8)
    )
    ff_plan = tuple(tuple(((f * 8 + t) * units, units) for f in range(4)) for t in range(8))

    packed_xy = pack_columns(rec_plan, padded, w_x, w_y, gain1)
    wxy = exchange(packed_xy, PLANE)
    conv_w, conv_b, b_rgate, b_igate, lam, w_rgate, w_igate, w_out = lax.optimization_barrier(
        (conv_w, conv_b, b_rgate, b_igate, lam, w_rgate, w_igate, w_out, packed_xy)
    )[:8]
    small = [w_out, conv_w, conv_b[:, None], b_rgate[:, None], b_igate[:, None], lam[:, None], w_rgate, w_igate]
    small_width = sum(v.shape[1] for v in small)
    small = jnp.pad(jnp.concatenate(small, axis=1), ((0, 0), (0, -small_width % 128)))

    stacked = w_parts(small, *STACK)
    wxy_parts = w_parts(after(wxy.reshape(-1, 2 * padded), stacked[1], stacked[2]), *STACK, (stacked[3],))
    upper = lax.axis_index("zh") == core
    keep = [jnp.where(upper, stacked[n], stacked[n + 1]) for n in (0, 2)]
    give = [swap(jnp.where(upper, stacked[n + 1], stacked[n]), "c") for n in (0, 2)]
    place = jnp.stack([lax.axis_index("zl"), core]).astype(jnp.int32)
    wo, gates, vec = place_channels(place, keep + give, model, width, taps)
    lam_all = vec[taps + 3]
    vec = jnp.concatenate([vec[: taps + 1], jax.nn.softplus(-lam_all)[None], vec[taps + 1 : taps + 3]], axis=0)

    xf = layer_input.astype(F32)
    scale1 = lax.rsqrt(jnp.mean(xf * xf, axis=-1, keepdims=True) + NORM_EPS)
    xs_pieces = act_gather(after((xf * scale1).astype(BF16), wxy), "x", "y", (), (wxy_parts[3],))
    packed_gu = after(pack_columns(ff_plan, 4 * units, w_gate, w_up, gain2), xs_pieces[2], wxy_parts[1])
    packed_gu = exchange(packed_gu, PLANE).reshape(-1, 8 * units)
    wd = lax.all_gather(after(w_down, wxy_parts[3]), STACK, axis=0, tiled=True)
    wxy_parts = wxy_parts[:3] + [after(wxy_parts[3], packed_gu, wo, gates)]
    wxy = w_place(wxy_parts, *STACK).reshape(model, -1)
    wgu = lax.all_gather(packed_gu, STACK, axis=0, tiled=True)
    xs_all, xy = pieces_product(xs_pieces, wxy, False)
    xc, pa, px, before, mixed = rec_forward(meta, xy, vec, gates, rows)
    cot_pieces = act_gather(after(cot, mixed), "x", "y")
    blocks_r = product_blocks(mixed, wo, False)
    cot_all = jnp.concatenate(cot_pieces, axis=0)
    resid = xf + act_scatter(blocks_r, "x", "y", (wd,))
    scale2 = lax.rsqrt(jnp.mean(resid * resid, axis=-1, keepdims=True) + NORM_EPS)
    xs2_pieces = act_gather((resid * scale2).astype(BF16), "x", "y", (cot_all,))
    xs2_all, hidden, d_gt, d_up, *blocks_2 = feed_forward(xs2_pieces, cot_all, wgu, wd)
    d_wd = row_contract(hidden, cot_all).astype(BF16)
    d_un2 = act_scatter(blocks_2, "x", "y", (), (d_wd,))
    d_resid = cot.astype(F32) + norm_back(d_un2, resid, scale2)
    d_mix = d_resid.astype(BF16)
    d_wd = lax.psum_scatter(d_wd, STACK, scatter_dimension=0, tiled=True)
    d_wg = row_contract(xs2_all, after(d_gt, d_mix)).astype(BF16)
    d_wu = row_contract(xs2_all, after(d_up, d_mix)).astype(BF16)
    d_mix_pieces = act_gather(d_mix, "x", "y", (d_wg,), (d_wu, d_wd))
    d_wg = lax.psum_scatter(d_wg, STACK, scatter_dimension=0, tiled=True)
    d_wu = lax.psum_scatter(d_wu, STACK, scatter_dimension=0, tiled=True)

    d_mix_all, dm = pieces_product(d_mix_pieces, wo, True)
    dxy, d_gates, sums = rec_backward(meta, dm, xy, before, pa, px, xc, vec, gates.T, rows)
    d_wg = exchange(d_wg.reshape(8, -1, 4 * units), PLANE)
    blocks_1 = product_blocks(after(dxy, d_wg), wxy, True)
    d_wxy = row_contract(xs_all, after(dxy, blocks_1[0])).astype(BF16)
    d_wxy_sum, sent = w_scatter(d_wxy.reshape(2, 2, model // 4, -1), *STACK)
    blocks_o = []

    def output_blocks(marker):
        blocks_o.extend(product_blocks(after(hidden, marker), wd, False))
        return sent, blocks_o[0]

    d_un = act_scatter(blocks_1, "x", "y", (d_wxy,), (), output_blocks)
    d_input = (d_resid + norm_back(after(d_un, d_wu), xf, scale1)).astype(BF16)
    d_wxy = d_wxy_sum.astype(BF16)
    output = (resid + act_scatter(blocks_o, "x", "y", (d_input,), (d_wxy,))).astype(BF16)
    d_wxy = exchange(d_wxy.reshape(8, -1, 2 * padded), PLANE)
    d_wx, d_wy, d_gain1 = unpack_columns(rec_plan, d_wxy, None, w_x, w_y, gain1)
    d_wu = exchange(d_wu.reshape(8, -1, 4 * units), PLANE)
    d_wg, d_wu, d_gain2 = unpack_columns(ff_plan, d_wg, d_wu, w_gate, w_up, gain2)

    def channels_out(v, kind):
        v = v.astype(kind).reshape(2, 2, part, -1)
        size = (2, 1) + v.shape[2:]
        keep = lax.dynamic_slice(v, (0, core, 0, 0), size)[:, 0]
        send = lax.dynamic_slice(v, (0, 1 - core, 0, 0), size)[:, 0]
        out = jnp.zeros((2,) + keep.shape, kind)
        out = lax.dynamic_update_slice(out, keep[None], (core, 0, 0, 0))
        return lax.dynamic_update_slice(out, swap(send, "c")[None], (1 - core, 0, 0, 0))

    d_wo = w_scatter(channels_out(row_contract(after(mixed, sent), d_mix_all)[:channels], BF16), *STACK)[0]
    sums = jnp.sum(sums.reshape(8, 8, padded), axis=1)
    d_lam_part = -jax.nn.sigmoid(-lam_all) * sums[5]
    d_cols = jnp.concatenate([sums[:5], sums[6:8], d_lam_part[None]], axis=0).T
    row_block = jnp.arange(channels)[:, None] // width
    d_blocks = []
    for g in range(2):
        block = d_gates[:channels, g * padded : g * padded + width]
        for n in range(1, blocks):
            at = g * padded + n * width
            block = jnp.where(row_block == n, d_gates[:channels, at : at + width], block)
        d_blocks.append(block)
    d_small = jnp.concatenate([d_cols[:channels]] + d_blocks, axis=1)
    d_small = w_scatter(channels_out(d_small, F32), *STACK)[0]
    d_cw, d_cb, d_br, d_bi, d_lam = d_small[:, :4], d_small[:, 4], d_small[:, 5], d_small[:, 6], d_small[:, 7]
    d_wr, d_wi = d_small[:, 8 : 8 + width], d_small[:, 8 + width : 8 + 2 * width]
    return (
        output, d_input, d_gain1[:, 0], d_wx, d_wy, d_cw, d_cb, d_wr, d_br, d_wi, d_bi, d_lam, d_wo,
        d_gain2[:, 0], d_wg, d_wu, d_wd.astype(F32),
    )


def factored(mesh):
    if tuple(mesh.axis_names) != ("fsdp", "seq") or (mesh.shape["fsdp"], mesh.shape["seq"]) != (4, 8):
        return None
    return Mesh(np.asarray(mesh.devices).reshape((2,) * 5), NAMES)


def solution(mesh):
    small = factored(mesh)
    if small is not None:
        whole, groups = P(NAMES), P(("zh", "zl"))
        return jax.shard_map(
            tensor_parallel,
            mesh=small,
            in_specs=(whole, groups) + (whole,) * 16,
            out_specs=(whole,) * 17,
            check_vma=False,
        )
    in_specs = (
        P(("fsdp", "seq"), None),
        P("fsdp", None),
        P(("fsdp", "seq")),
        P(("fsdp", "seq"), None),
        P(("fsdp", "seq"), None),
        P(("fsdp", "seq"), None),
        P(("fsdp", "seq")),
        P(("fsdp", "seq"), None),
        P(("fsdp", "seq")),
        P(("fsdp", "seq"), None),
        P(("fsdp", "seq")),
        P(("fsdp", "seq")),
        P(("fsdp", "seq"), None),
        P(("fsdp", "seq")),
        P(("fsdp", "seq"), None),
        P(("fsdp", "seq"), None),
        P(("fsdp", "seq"), None),
        P(("fsdp", "seq"), None),
    )
    out_specs = (
        P(("fsdp", "seq"), None),
        P(("fsdp", "seq"), None),
        P(("fsdp", "seq")),
        P(("fsdp", "seq"), None),
        P(("fsdp", "seq"), None),
        P(("fsdp", "seq"), None),
        P(("fsdp", "seq")),
        P(("fsdp", "seq"), None),
        P(("fsdp", "seq")),
        P(("fsdp", "seq"), None),
        P(("fsdp", "seq")),
        P(("fsdp", "seq")),
        P(("fsdp", "seq"), None),
        P(("fsdp", "seq")),
        P(("fsdp", "seq"), None),
        P(("fsdp", "seq"), None),
        P(("fsdp", "seq"), None),
    )
    return jax.shard_map(
        on_device, mesh=mesh, in_specs=in_specs, out_specs=out_specs, check_vma=False
    )
```

```python
import functools

import jax
import jax.numpy as jnp
import numpy as np
from jax import lax
from jax.experimental import pallas as pl
from jax.experimental.pallas import tpu as pltpu
from jax.sharding import Mesh
from jax.sharding import PartitionSpec as P

DECAY_C = 8.0
NORM_EPS = 1e-06


def from_behind(x, axis, by):
    size = lax.axis_size(axis)
    pairs = [(i, i + by) for i in range(size) if 0 <= i + by < size]
    return lax.ppermute(x, axis, pairs)


def carried_in(value, axis, join, neutral, backward):
    count, mine = (lax.axis_size(axis), lax.axis_index(axis))
    pieces = jax.tree.map(lambda part: lax.all_gather(part, axis), value)
    if backward:
        pieces = jax.tree.map(lambda part: part[::-1], pieces)
        mine = count - 1 - mine
    subtotal = jax.tree.map(
        lambda part, zero: jnp.full_like(part, 0) + jnp.asarray(zero, part.dtype), value, neutral
    )

    def step(position, subtotal):
        longer = join(subtotal, jax.tree.map(lambda part: part[position], pieces))
        return jax.tree.map(lambda new, old: jnp.where(position < mine, new, old), longer, subtotal)

    return lax.fori_loop(0, count - 1, step, subtotal)


def rms_apply(value, gain):
    scale = lax.rsqrt(jnp.mean(value * value, axis=-1, keepdims=True) + NORM_EPS)
    return value * scale * gain


def combine(earlier, later):
    return (earlier[0] * later[0], later[0] * earlier[1] + later[1])


def lru_terms(pre_r, pre_i, lam_vec, conv_out, start):
    rate = jax.nn.softplus(-lam_vec)
    log_a = -DECAY_C * jax.nn.sigmoid(pre_r) * rate
    decay = jnp.where(start[:, None], 0.0, jnp.exp(log_a))
    scale = jnp.sqrt(jnp.maximum(-jnp.expm1(2.0 * log_a), 0.2 * DECAY_C * rate))
    scale = jnp.where(start[:, None], 1.0, scale)
    return (decay, scale * jax.nn.sigmoid(pre_i) * conv_out)


def row_contract(left, right):
    return lax.dot_general(
        left, right, (((0,), (0,)), ((), ())), preferred_element_type=jnp.float32
    )


def back_product(grad, weight):
    return lax.dot_general(
        grad, weight, (((1,), (1,)), ((), ())), preferred_element_type=jnp.float32
    )


def split_blocks(value, width):
    return value.reshape(value.shape[0], value.shape[1] // width, width)


def block_product(value, weight):
    width = weight.shape[1]
    mats = weight.reshape(weight.shape[0] // width, width, width)
    result = jnp.einsum(
        "nhi,hij->nhj", split_blocks(value, width), mats, preferred_element_type=jnp.float32
    )
    return result.reshape(value.shape[0], -1)


def block_back(grad, weight):
    width = weight.shape[1]
    mats = weight.reshape(weight.shape[0] // width, width, width)
    result = jnp.einsum(
        "nhj,hij->nhi", split_blocks(grad, width), mats, preferred_element_type=jnp.float32
    )
    return result.reshape(grad.shape[0], -1)


def gate_grad(value, grad, width):
    result = jnp.einsum(
        "nhi,nhj->hij",
        split_blocks(value, width),
        split_blocks(grad, width),
        preferred_element_type=jnp.float32,
    )
    return result.reshape(value.shape[1], width)


def seq_starts(lens_row):
    count = lens_row.shape[0]
    before = jnp.arange(count)[None, :] < jnp.arange(count)[:, None]
    return jnp.sum(jnp.where(before, lens_row[None, :], 0), axis=1)


def seq_masks(lens_row, first, rows, taps):
    starts = seq_starts(lens_row)
    place = first + jnp.arange(rows, dtype=jnp.int32)

    def segment(p):
        return jnp.sum((p[:, None] >= starts[None, :]).astype(jnp.int32), axis=1)

    seg_now = segment(place)
    start = jnp.any(place[:, None] == starts[None, :], axis=1)
    same = jnp.stack(
        [
            ((segment(place - k) == seg_now) & (place - k >= 0)).astype(jnp.float32)
            for k in range(taps)
        ],
        0,
    )
    return (start, same)


def on_device(
    layer_input,
    lengths,
    norm1_gain,
    w_x,
    w_y,
    conv_w,
    conv_b,
    w_rgate,
    b_rgate,
    w_igate,
    b_igate,
    lam,
    w_out,
    norm2_gain,
    w_gate,
    w_up,
    w_down,
    cot,
):
    rows = layer_input.shape[0]
    taps = conv_w.shape[1]
    width = w_rgate.shape[1]
    rim = taps - 1
    index = lax.axis_index("seq")
    start, same = seq_masks(lengths[0], index * rows, rows, taps)
    gain_one, wx, wy, cw, cb, wr, br, wi, bi, lam_all, wo = (
        lax.all_gather(norm1_gain, ("fsdp", "seq"), axis=0, tiled=True),
        lax.all_gather(w_x, ("fsdp", "seq"), axis=0, tiled=True),
        lax.all_gather(w_y, ("fsdp", "seq"), axis=0, tiled=True),
        lax.all_gather(conv_w, ("fsdp", "seq"), axis=0, tiled=True),
        lax.all_gather(conv_b, ("fsdp", "seq"), axis=0, tiled=True),
        lax.all_gather(w_rgate, ("fsdp", "seq"), axis=0, tiled=True),
        lax.all_gather(b_rgate, ("fsdp", "seq"), axis=0, tiled=True),
        lax.all_gather(w_igate, ("fsdp", "seq"), axis=0, tiled=True),
        lax.all_gather(b_igate, ("fsdp", "seq"), axis=0, tiled=True),
        lax.all_gather(lam, ("fsdp", "seq"), axis=0, tiled=True),
        lax.all_gather(w_out, ("fsdp", "seq"), axis=0, tiled=True),
    )
    xf = layer_input.astype(jnp.float32)
    gain1 = gain_one.astype(jnp.float32)
    un = rms_apply(xf, gain1).astype(jnp.bfloat16)
    xb = jnp.dot(un, wx, preferred_element_type=jnp.float32).astype(jnp.bfloat16)
    yb = jnp.dot(un, wy, preferred_element_type=jnp.float32)
    gy = jax.nn.gelu(yb)
    rim_in = from_behind(xb[rows - rim :], "seq", 1)
    extended = jnp.concatenate([rim_in, xb], axis=0).astype(jnp.float32)
    cwf = cw.astype(jnp.float32)
    conv = jnp.broadcast_to(cb.astype(jnp.float32)[None, :], (rows, cwf.shape[0]))
    for k in range(taps):
        conv = conv + cwf[:, k][None, :] * extended[rim - k : rim - k + rows] * same[k][:, None]
    xc = conv.astype(jnp.bfloat16)
    xcf = xc.astype(jnp.float32)
    pre_r = block_product(xc, wr) + br.astype(jnp.float32)[None, :]
    pre_i = block_product(xc, wi) + bi.astype(jnp.float32)[None, :]
    lamf = lam_all.astype(jnp.float32)
    decay, drive = lru_terms(pre_r, pre_i, lamf, xcf, start)
    decay_cum, state_loc = lax.associative_scan(combine, (decay, drive), axis=0)
    zero_vec = jnp.zeros((decay.shape[1],), jnp.float32)
    one_vec = jnp.ones((decay.shape[1],), jnp.float32)
    state_in = carried_in(
        (decay_cum[-1], state_loc[-1]), "seq", combine, (one_vec, zero_vec), False
    )[1]
    state = state_loc + decay_cum * state_in[None, :]
    state_prev = jnp.concatenate([state_in[None, :], state[:-1]], axis=0)
    mixed = (state * gy).astype(jnp.bfloat16)
    resid = xf + jnp.dot(mixed, wo, preferred_element_type=jnp.float32)
    gain_two, wg, wu, wd = (
        lax.all_gather(norm2_gain, ("fsdp", "seq"), axis=0, tiled=True),
        lax.all_gather(w_gate, ("fsdp", "seq"), axis=0, tiled=True),
        lax.all_gather(w_up, ("fsdp", "seq"), axis=0, tiled=True),
        lax.all_gather(w_down, ("fsdp", "seq"), axis=0, tiled=True),
    )
    gain2 = gain_two.astype(jnp.float32)
    un2 = rms_apply(resid, gain2).astype(jnp.bfloat16)
    gate_pre = jnp.dot(un2, wg, preferred_element_type=jnp.float32)
    up_pre = jnp.dot(un2, wu, preferred_element_type=jnp.float32)
    gate_act, gelu_back = jax.vjp(jax.nn.gelu, gate_pre)
    hidden = (gate_act * up_pre).astype(jnp.bfloat16)
    output = (resid + jnp.dot(hidden, wd, preferred_element_type=jnp.float32)).astype(jnp.bfloat16)
    grad = cot.astype(jnp.float32)
    gain_two, wg, wu, wd = (
        lax.all_gather(norm2_gain, ("fsdp", "seq"), axis=0, tiled=True),
        lax.all_gather(w_gate, ("fsdp", "seq"), axis=0, tiled=True),
        lax.all_gather(w_up, ("fsdp", "seq"), axis=0, tiled=True),
        lax.all_gather(w_down, ("fsdp", "seq"), axis=0, tiled=True),
    )
    gain2 = gain_two.astype(jnp.float32)
    d_wd = row_contract(hidden, cot)
    d_hidden = back_product(cot, wd)
    d_gate = gelu_back(d_hidden * up_pre)[0].astype(jnp.bfloat16)
    d_up = (d_hidden * gate_act).astype(jnp.bfloat16)
    d_wg = row_contract(un2, d_gate)
    d_wu = row_contract(un2, d_up)
    d_un2 = back_product(d_gate, wg) + back_product(d_up, wu)
    norm_two_back = jax.vjp(rms_apply, resid, gain2)[1]
    d_resid_norm, d_gain2 = norm_two_back(d_un2)
    mlp_grads = (
        lax.psum_scatter(d_gain2, ("fsdp", "seq"), scatter_dimension=0, tiled=True),
        lax.psum_scatter(d_wg, ("fsdp", "seq"), scatter_dimension=0, tiled=True),
        lax.psum_scatter(d_wu, ("fsdp", "seq"), scatter_dimension=0, tiled=True),
        lax.psum_scatter(d_wd, ("fsdp", "seq"), scatter_dimension=0, tiled=True),
    )
    d_resid = grad + d_resid_norm
    gain_one, wx, wy, cw, cb, wr, br, wi, bi, lam_all, wo = (
        lax.all_gather(norm1_gain, ("fsdp", "seq"), axis=0, tiled=True),
        lax.all_gather(w_x, ("fsdp", "seq"), axis=0, tiled=True),
        lax.all_gather(w_y, ("fsdp", "seq"), axis=0, tiled=True),
        lax.all_gather(conv_w, ("fsdp", "seq"), axis=0, tiled=True),
        lax.all_gather(conv_b, ("fsdp", "seq"), axis=0, tiled=True),
        lax.all_gather(w_rgate, ("fsdp", "seq"), axis=0, tiled=True),
        lax.all_gather(b_rgate, ("fsdp", "seq"), axis=0, tiled=True),
        lax.all_gather(w_igate, ("fsdp", "seq"), axis=0, tiled=True),
        lax.all_gather(b_igate, ("fsdp", "seq"), axis=0, tiled=True),
        lax.all_gather(lam, ("fsdp", "seq"), axis=0, tiled=True),
        lax.all_gather(w_out, ("fsdp", "seq"), axis=0, tiled=True),
    )
    gain1 = gain_one.astype(jnp.float32)
    cwf = cw.astype(jnp.float32)
    lamf = lam_all.astype(jnp.float32)
    d_mix = d_resid.astype(jnp.bfloat16)
    d_wo = row_contract(mixed, d_mix)
    d_mixed = back_product(d_mix, wo)
    d_state = d_mixed * gy
    gelu_y_back = jax.vjp(jax.nn.gelu, yb)[1]
    d_yb = gelu_y_back(d_mixed * state)[0].astype(jnp.bfloat16)
    next_decay = jnp.concatenate([decay[1:], one_vec[None, :]], axis=0)
    decay_after, adjoint_loc = lax.associative_scan(
        combine, (next_decay, d_state), reverse=True, axis=0
    )
    send_decay = decay[0] * decay_after[0]
    send_adjoint = decay[0] * adjoint_loc[0]
    adjoint_in = carried_in((send_decay, send_adjoint), "seq", combine, (one_vec, zero_vec), True)[
        1
    ]
    adjoint = adjoint_loc + decay_after * adjoint_in[None, :]

    def local_lru(pr, pi, lv, cv):
        return lru_terms(pr, pi, lv, cv, start)

    lru_back = jax.vjp(local_lru, pre_r, pre_i, lamf, xcf)[1]
    d_pre_r, d_pre_i, d_lam, d_xc_local = lru_back((adjoint * state_prev, adjoint))
    d_pr = d_pre_r.astype(jnp.bfloat16)
    d_pi = d_pre_i.astype(jnp.bfloat16)
    d_wr = gate_grad(xc, d_pr, width)
    d_wi = gate_grad(xc, d_pi, width)
    d_br = jnp.sum(d_pr.astype(jnp.float32), axis=0)
    d_bi = jnp.sum(d_pi.astype(jnp.float32), axis=0)
    d_xc = d_xc_local + block_back(d_pr, wr) + block_back(d_pi, wi)
    d_cb = jnp.sum(d_xc, axis=0)
    d_cw = jnp.stack(
        [
            jnp.sum(d_xc * extended[rim - k : rim - k + rows] * same[k][:, None], axis=0)
            for k in range(taps)
        ],
        axis=1,
    )
    d_extended = jnp.zeros((rows + rim, d_xc.shape[1]), jnp.float32)
    for k in range(taps):
        d_extended = d_extended + jnp.pad(
            d_xc * cwf[:, k][None, :] * same[k][:, None], ((rim - k, k), (0, 0))
        )
    rim_back = from_behind(d_extended[:rim], "seq", -1)
    d_xb = (d_extended[rim:] + jnp.pad(rim_back, ((rows - rim, 0), (0, 0)))).astype(jnp.bfloat16)
    d_wx = row_contract(un, d_xb)
    d_wy = row_contract(un, d_yb)
    d_un = back_product(d_xb, wx) + back_product(d_yb, wy)
    norm_one_back = jax.vjp(rms_apply, xf, gain1)[1]
    d_x_norm, d_gain1 = norm_one_back(d_un)
    d_input = (d_resid + d_x_norm).astype(jnp.bfloat16)
    block_grads = (
        lax.psum_scatter(d_gain1, ("fsdp", "seq"), scatter_dimension=0, tiled=True),
        lax.psum_scatter(d_wx, ("fsdp", "seq"), scatter_dimension=0, tiled=True),
        lax.psum_scatter(d_wy, ("fsdp", "seq"), scatter_dimension=0, tiled=True),
        lax.psum_scatter(d_cw, ("fsdp", "seq"), scatter_dimension=0, tiled=True),
        lax.psum_scatter(d_cb, ("fsdp", "seq"), scatter_dimension=0, tiled=True),
        lax.psum_scatter(d_wr, ("fsdp", "seq"), scatter_dimension=0, tiled=True),
        lax.psum_scatter(d_br, ("fsdp", "seq"), scatter_dimension=0, tiled=True),
        lax.psum_scatter(d_wi, ("fsdp", "seq"), scatter_dimension=0, tiled=True),
        lax.psum_scatter(d_bi, ("fsdp", "seq"), scatter_dimension=0, tiled=True),
        lax.psum_scatter(d_lam, ("fsdp", "seq"), scatter_dimension=0, tiled=True),
        lax.psum_scatter(d_wo, ("fsdp", "seq"), scatter_dimension=0, tiled=True),
    )
    return (
        output,
        d_input,
        block_grads[0],
        block_grads[1],
        block_grads[2],
        block_grads[3],
        block_grads[4],
        block_grads[5],
        block_grads[6],
        block_grads[7],
        block_grads[8],
        block_grads[9],
        block_grads[10],
        mlp_grads[0],
        mlp_grads[1],
        mlp_grads[2],
        mlp_grads[3],
    )


NAMES = ("zh", "zl", "y", "x", "c")
F32 = jnp.float32
BF16 = jnp.bfloat16
GELU_C = 0.7978845608
GELU_K = 0.044715


def after(v, *first):
    return lax.optimization_barrier((v,) + first)[0]


def swap(v, name):
    return lax.ppermute(v, name, [(0, 1), (1, 0)])


def add16(one, two):
    return (one.astype(F32) + two.astype(F32)).astype(BF16)


def act_gather(v, a, b, second=(), third=(), during=None):
    h = v.shape[0] // 2
    near, from_a, from_b = swap(v, "c"), swap(v, a), swap(v, b)
    from_a, from_b, near = lax.optimization_barrier((from_a, from_b, near) + tuple(second))[:3]
    far0, far1 = swap(from_a[:h], b), swap(from_b[h:], a)
    near_a, near_b = swap(from_a, "c"), swap(from_b, "c")
    if during is not None:
        third = tuple(third) + tuple(during(from_a))
    far0, far1, near_a, near_b = lax.optimization_barrier((far0, far1, near_a, near_b) + tuple(third))[:4]
    far = jnp.concatenate([far0, far1], axis=0)
    return [v, near, from_a, near_a, from_b, near_b, far, swap(far, "c")]


def act_scatter(blocks, a, b, second=(), third=(), during=None, last=None):
    far, to_a, to_b = [add16(blocks[k], swap(blocks[k + 1], "c")) for k in (6, 2, 4)]
    far = after(far, *second)
    own = blocks[0].astype(F32) + swap(blocks[1], "c").astype(F32)
    h = far.shape[0] // 2
    in_b, in_a = swap(far[:h], b), swap(far[h:], a)
    if during is not None:
        third = tuple(third) + tuple(during(far))
    to_a = jnp.concatenate([add16(to_a[:h], in_b), to_a[h:]], axis=0)
    to_b = jnp.concatenate([to_b[:h], add16(to_b[h:], in_a)], axis=0)
    to_a, to_b = lax.optimization_barrier((to_a, to_b) + tuple(third))[:2]
    from_a, from_b = swap(to_a, a), swap(to_b, b)
    if last is not None:
        from_a, from_b = lax.optimization_barrier((from_a, from_b) + tuple(last(to_a)))[:2]
    return own + from_a.astype(F32) + from_b.astype(F32)


def w_parts(v, w1, w2, second=()):
    from_1, from_2 = lax.optimization_barrier((swap(v, w1), swap(v, w2)) + tuple(second))[:2]
    return [v, from_1, from_2, swap(from_1, w2)]


def w_place(parts, w1, w2):
    i1, i2 = lax.axis_index(w1), lax.axis_index(w2)
    out = jnp.zeros((2, 2) + parts[0].shape, parts[0].dtype)
    tail = (0,) * parts[0].ndim
    for part, j1, j2 in zip(parts, (i1, 1 - i1, i1, 1 - i1), (i2, i2, 1 - i2, 1 - i2)):
        out = lax.dynamic_update_slice(out, part[None, None], (j1, j2) + tail)
    return out


def w_scatter(v, w1, w2, hold=()):
    i1, i2 = lax.axis_index(w1), lax.axis_index(w2)

    def get(j1, j2):
        return lax.dynamic_slice(v, (j1, j2) + (0,) * (v.ndim - 2), (1, 1) + v.shape[2:])[0, 0]

    to_other, to_own = swap(get(1 - i1, 1 - i2), w2), swap(get(i1, 1 - i2), w2)
    to_other, to_own = lax.optimization_barrier((to_other, to_own) + tuple(hold))[:2]
    other = (get(1 - i1, i2).astype(F32) + to_other.astype(F32)).astype(v.dtype)
    own = get(i1, i2).astype(F32) + to_own.astype(F32)
    received = swap(other, w1)
    return lambda *late: own + after(received, *late).astype(F32), other


def pack_kernel(plan, a_ref, b_ref, gain_ref, out_ref):
    half = out_ref.shape[2] // 2
    for first, ref in ((0, a_ref), (half, b_ref)):
        scaled = (ref[...].astype(F32) * gain_ref[...]).astype(BF16)
        for dest, pieces in enumerate(plan):
            at = first
            for source, size in pieces:
                out_ref[dest, :, at : at + size] = scaled[:, source : source + size]
                at += size
            if at < first + half:
                out_ref[dest, :, at : first + half] = jnp.zeros((scaled.shape[0], first + half - at), BF16)


def unpack_kernel(plan, ga_ref, gb_ref, a_ref, b_ref, gain_ref, da_ref, db_ref, dgain_ref):
    total = jnp.zeros(dgain_ref.shape, F32)
    for grad_ref, ref, out in ((ga_ref, a_ref, da_ref), (gb_ref, b_ref, db_ref)):
        for dest, pieces in enumerate(plan):
            at = 0
            for source, size in pieces:
                piece = grad_ref[dest, :, at : at + size].astype(F32)
                out[:, source : source + size] = piece * gain_ref[...]
                weight = ref[:, source : source + size].astype(F32)
                total = total + jnp.sum(piece * weight, axis=1, keepdims=True)
                at += size
    dgain_ref[...] = total


def pack_columns(plan, half, one, two, gain):
    return pl.pallas_call(
        functools.partial(pack_kernel, plan),
        out_shape=jax.ShapeDtypeStruct((8, one.shape[0], 2 * half), BF16),
        compiler_params=pltpu.CompilerParams(vmem_limit_bytes=24 << 20),
        cost_estimate=pl.CostEstimate(flops=4 * one.size, transcendentals=0, bytes_accessed=8 * one.size),
        name="pack_columns",
    )(one, two, gain)


def unpack_columns(plan, grad_one, grad_two, one, two, gain):
    half = grad_one.shape[2] if grad_two is not None else grad_one.shape[2] // 2
    rows, cols = one.shape
    whole = lambda *shape: pl.BlockSpec(shape, lambda i: (0,) * len(shape))
    grads = [
        pl.BlockSpec((8, rows, half), lambda i: (0, 0, 0)),
        pl.BlockSpec((8, rows, half), lambda i: (0, 0, 0 if grad_two is not None else 1)),
    ]
    shape = jax.ShapeDtypeStruct(one.shape, F32)
    return pl.pallas_call(
        functools.partial(unpack_kernel, plan),
        grid=(1,),
        in_specs=grads + [whole(rows, cols), whole(rows, cols), whole(rows, 1)],
        out_specs=[whole(rows, cols), whole(rows, cols), whole(rows, 1)],
        out_shape=[shape, shape, jax.ShapeDtypeStruct((rows, 1), F32)],
        compiler_params=pltpu.CompilerParams(vmem_limit_bytes=32 << 20),
        cost_estimate=pl.CostEstimate(flops=8 * one.size, transcendentals=0, bytes_accessed=16 * one.size),
        name="unpack_columns",
    )(grad_one, grad_one if grad_two is None else grad_two, one, two, gain)


def exchange(v, tp):
    return lax.all_to_all(v, tp, split_axis=0, concat_axis=0, tiled=True)


def neg_expm1(v):
    series = 1.0 + v * (1.0 / 10.0)
    for n in range(9, 1, -1):
        series = 1.0 + v * (1.0 / n) * series
    return jnp.where(v > -0.5, -v * series, 1.0 - jnp.exp(v))


def gate_terms(pa, px, rate, start):
    sr = jax.nn.sigmoid(pa)
    si = jax.nn.sigmoid(px)
    la = -DECAY_C * sr * rate
    decay = jnp.where(start, 0.0, jnp.exp(la))
    e2 = neg_expm1(2.0 * la)
    floor = 0.2 * DECAY_C * rate
    scale = jnp.where(start, 1.0, jnp.sqrt(jnp.maximum(e2, floor)))
    return sr, si, decay, e2, floor, scale


def gelu(v):
    return 0.5 * v * (1.0 + jnp.tanh(GELU_C * (v + GELU_K * v * v * v)))


def gelu_both(v):
    t = jnp.tanh(GELU_C * (v + GELU_K * v * v * v))
    half = 0.5 * (1.0 + t)
    return v * half, half + 0.5 * v * (1.0 - t * t) * GELU_C * (1.0 + 3.0 * GELU_K * v * v)


def scan_tile(decay, drive, into):
    row = lax.broadcasted_iota(jnp.int32, decay.shape, 0)
    for by in (1, 2, 4):
        keep = row >= by
        drive = jnp.where(keep, decay * pltpu.roll(drive, by, 0) + drive, drive)
        decay = jnp.where(keep, decay * pltpu.roll(decay, by, 0), decay)
    return decay * into + drive


def scan_tile_back(decay, drive, into):
    row = lax.broadcasted_iota(jnp.int32, decay.shape, 0)
    for by in (1, 2, 4):
        keep = row < 8 - by
        drive = jnp.where(keep, decay * pltpu.roll(drive, 8 - by, 0) + drive, drive)
        decay = jnp.where(keep, decay * pltpu.roll(decay, 8 - by, 0), decay)
    return decay * into + drive


STEP = 16


def since_start(meta_ref, place, width):
    at = place + lax.broadcasted_iota(jnp.int32, (STEP, 128), 0)
    since, start = at, 0
    for n in range(1, meta_ref.shape[0] - 1):
        start = start + meta_ref[n]
        since = jnp.where(at >= start, at - start, since)
    return jnp.concatenate([since] * (width // 128), axis=1)


def rec_fwd_kernel(meta_ref, xb_ref, yb_ref, vec_ref, w_ref, xc_ref, pa_ref, px_ref, sp_ref, mixed_ref, ext, carry):
    rows, width = xb_ref.shape
    base = pl.program_id(0) * rows

    @pl.when(pl.program_id(0) == 0)
    def _():
        ext[0:8, :] = jnp.zeros((8, width), F32)
        carry[...] = jnp.zeros_like(carry)

    ext[8 : 8 + rows, :] = xb_ref[...].astype(BF16).astype(F32)

    def conv_step(r, _):
        at = pl.multiple_of(r * STEP, STEP)
        window = ext[pl.ds(at, STEP + 8), :]
        since = since_start(meta_ref, base + at, width)
        total = vec_ref[4:5, :] + vec_ref[0:1, :] * window[8:, :]
        for k in range(1, 4):
            moved = jnp.where(since >= k, window[8 - k : 8 - k + STEP, :], 0.0)
            total = total + vec_ref[k : k + 1, :] * moved
        xc_ref[pl.ds(at, STEP), :] = total.astype(BF16)
        return 0

    lax.fori_loop(0, rows // STEP, conv_step, 0, unroll=2)
    ext[0:8, :] = ext[rows : rows + 8, :]
    xc = xc_ref[...]
    pa_ref[...] = jnp.dot(xc, w_ref[:, :width], preferred_element_type=F32) + vec_ref[6:7, :]
    px_ref[...] = jnp.dot(xc, w_ref[:, width:], preferred_element_type=F32) + vec_ref[7:8, :]
    top = lax.broadcasted_iota(jnp.int32, (8, width), 0) == 0

    def scan_step(r, held):
        here = pl.ds(pl.multiple_of(r * STEP, STEP), STEP)
        start = since_start(meta_ref, base + r * STEP, width) == 0
        _, si, decay, _, _, scale = gate_terms(pa_ref[here, :], px_ref[here, :], vec_ref[5:6, :], start)
        drive = scale * si * xc_ref[here, :].astype(F32)
        states, before = [], []
        for part in range(0, STEP, 8):
            now = scan_tile(decay[part : part + 8], drive[part : part + 8], held)
            states.append(now)
            before.append(jnp.where(top, held, pltpu.roll(now, 1, 0)))
            held = jnp.broadcast_to(now[7:8, :], (8, width))
        sp_ref[here, :] = jnp.concatenate(before, axis=0)
        mixed_ref[here, :] = (jnp.concatenate(states, axis=0) * gelu(yb_ref[here, :])).astype(BF16)
        return held

    carry[...] = lax.fori_loop(0, rows // STEP, scan_step, carry[...], unroll=2)


def rec_bwd_kernel(
    meta_ref, dm_ref, yb_ref, sp_ref, pa_ref, px_ref, xc_ref, xb_ref, vec_ref, wt_ref,
    dxy_ref, dw_ref, sum_ref, ext, dp, carry,
):
    rows, width = xb_ref.shape
    base = (pl.num_programs(0) - 1 - pl.program_id(0)) * rows

    @pl.when(pl.program_id(0) == 0)
    def _():
        ext[rows : rows + 8, :] = jnp.zeros((8, width), F32)
        carry[...] = jnp.zeros_like(carry)
        dw_ref[...] = jnp.zeros_like(dw_ref)
        sum_ref[...] = jnp.zeros_like(sum_ref)

    row = lax.broadcasted_iota(jnp.int32, (8, width), 0)
    steps = rows // STEP

    def fold(v):
        return v[0:8, :] + v[8:16, :]

    def scan_step(i, state):
        held, s_rate, s_r, s_i = state
        at = pl.multiple_of((steps - 1 - i) * STEP, STEP)
        here = pl.ds(at, STEP)
        start = since_start(meta_ref, base + at, width) == 0
        rate = vec_ref[5:6, :]
        sr, si, decay, e2, floor, scale = gate_terms(pa_ref[here, :], px_ref[here, :], rate, start)
        xc = xc_ref[here, :].astype(F32)
        before = sp_ref[here, :]
        gate = si * xc
        now = decay * before + scale * gate
        dm = dm_ref[here, :]
        act, slope = gelu_both(yb_ref[here, :])
        dxy_ref[here, width:] = (dm * now * slope).astype(BF16)
        dstate = dm * act
        parts = []
        for part in range(STEP - 8, -1, -8):
            here_decay = decay[part : part + 8]
            coef = jnp.where(row == 7, 1.0, pltpu.roll(here_decay, 7, 0))
            adj = scan_tile_back(coef, dstate[part : part + 8], held)
            held = jnp.broadcast_to((here_decay * adj)[0:1, :], (8, width))
            parts.append(adj)
        adj = jnp.concatenate(parts[::-1], axis=0)
        d_scale = adj * gate
        d_half = jnp.where(start, 0.0, d_scale * 0.5 / scale)
        share = jnp.where(e2 > floor, 1.0, jnp.where(e2 == floor, 0.5, 0.0))
        kept = adj * scale
        d_la = decay * (adj * before - 2.0 * decay * d_half * share)
        d_rate = -DECAY_C * sr * d_la + (0.2 * DECAY_C) * d_half * (1.0 - share)
        d_pa = (-DECAY_C * rate * d_la * sr * (1.0 - sr)).astype(BF16)
        d_px = (kept * xc * si * (1.0 - si)).astype(BF16)
        dp[here, :width] = d_pa
        dp[here, width:] = d_px
        ext[here, :] = kept * si
        return held, s_rate + fold(d_rate), s_r + fold(d_pa.astype(F32)), s_i + fold(d_px.astype(F32))

    held, s_rate, s_r, s_i = lax.fori_loop(
        0, steps, scan_step, (carry[...], sum_ref[40:48, :], sum_ref[48:56, :], sum_ref[56:64, :]), unroll=2
    )
    carry[...] = held
    sum_ref[40:48, :] = s_rate
    sum_ref[48:56, :] = s_r
    sum_ref[56:64, :] = s_i
    ext[0:rows, :] += jnp.dot(dp[...], wt_ref[...], preferred_element_type=F32)
    dw_ref[...] += row_contract(xc_ref[...], dp[...])

    def conv_step(r, sums):
        at = pl.multiple_of(r * STEP, STEP)
        window = ext[pl.ds(at, STEP + 8), :]
        xb = xb_ref[pl.ds(at, STEP), :].astype(BF16).astype(F32)
        total = jnp.zeros((STEP, width), F32)
        new = []
        for k in range(4):
            moved = window[k : k + STEP, :]
            if k:
                moved = jnp.where(since_start(meta_ref, base + at + k, width) >= k, moved, 0.0)
            total = total + vec_ref[k : k + 1, :] * moved
            new.append(sums[k] + fold(moved * xb))
        new.append(sums[4] + fold(window[:STEP, :]))
        dxy_ref[pl.ds(at, STEP), :width] = total.astype(BF16)
        return tuple(new)

    sums = lax.fori_loop(0, steps, conv_step, tuple(sum_ref[8 * q : 8 * q + 8, :] for q in range(5)), unroll=2)
    for q in range(5):
        sum_ref[8 * q : 8 * q + 8, :] = sums[q]
    ext[rows : rows + 8, :] = ext[0:8, :]


def place_kernel(width, taps, meta_ref, *refs):
    parts, (wo_ref, gates_ref, vec_ref, cols) = refs[:4], refs[4:]
    part, model = parts[0].shape[0], wo_ref.shape[1]
    padded = wo_ref.shape[0]
    zl, core = meta_ref[0], meta_ref[1]
    lanes = cols.shape[1]
    wo_ref[4 * part :, :] = jnp.zeros((padded - 4 * part, model), BF16)
    gates_ref[...] = jnp.zeros_like(gates_ref)
    cols[4 * part :, :] = jnp.zeros((padded - 4 * part, lanes), F32)
    for n in range(4):
        here_zl = zl if n % 2 == 0 else 1 - zl
        half = core if n < 2 else 1 - core
        at = pl.multiple_of((here_zl * 2 + half) * part, STEP)
        wo_ref[pl.ds(at, part), :] = parts[n][:, :model]
        rest = parts[n][:, model:]
        cols[pl.ds(at, part), :] = rest[:, :lanes].astype(F32)
        for block in range(2):

            @pl.when(here_zl == block)
            def _(rest=rest, at=at, block=block):
                for g in range(2):
                    source = taps + 4 + g * width
                    target = g * padded + block * width
                    gates_ref[pl.ds(at, part), target : target + width] = rest[:, source : source + width]

    vec_ref[...] = cols[...].T[:8, :]


def place_channels(meta, parts, model, width, taps):
    part = parts[0].shape[0]
    padded = -(-4 * part // 128) * 128
    shape = jax.ShapeDtypeStruct
    return pl.pallas_call(
        functools.partial(place_kernel, width, taps),
        grid_spec=pltpu.PrefetchScalarGridSpec(
            num_scalar_prefetch=1,
            grid=(1,),
            in_specs=[pl.BlockSpec(v.shape, lambda i, m: (0, 0)) for v in parts],
            out_specs=[
                pl.BlockSpec((padded, model), lambda i, m: (0, 0)),
                pl.BlockSpec((padded, 2 * padded), lambda i, m: (0, 0)),
                pl.BlockSpec((8, padded), lambda i, m: (0, 0)),
            ],
            scratch_shapes=[pltpu.VMEM((padded, 128), F32)],
        ),
        out_shape=[shape((padded, model), BF16), shape((padded, 2 * padded), BF16), shape((8, padded), F32)],
        compiler_params=pltpu.CompilerParams(vmem_limit_bytes=24 << 20),
        cost_estimate=pl.CostEstimate(flops=padded * model, transcendentals=0, bytes_accessed=8 * padded * model),
        name="place_channels",
    )(meta, *parts)


def rec_forward(meta, xy, vec, w, tile):
    total, width = xy.shape[0], xy.shape[1] // 2
    block = pl.BlockSpec((tile, width), lambda i, m: (i ^ m[0], 0))
    right = pl.BlockSpec((tile, width), lambda i, m: (i ^ m[0], 1))
    whole = lambda v: pl.BlockSpec(v.shape, lambda i, m: (0, 0))
    return pl.pallas_call(
        rec_fwd_kernel,
        grid_spec=pltpu.PrefetchScalarGridSpec(
            num_scalar_prefetch=1,
            grid=(total // tile,),
            in_specs=[block, right, whole(vec), whole(w)],
            out_specs=[block] * 5,
            scratch_shapes=[pltpu.VMEM((tile + 8, width), F32), pltpu.VMEM((8, width), F32)],
        ),
        out_shape=[jax.ShapeDtypeStruct((total, width), t) for t in (BF16, F32, F32, F32, BF16)],
        compiler_params=pltpu.CompilerParams(vmem_limit_bytes=32 << 20),
        cost_estimate=pl.CostEstimate(
            flops=100 * total * width + 4 * total * width * width,
            transcendentals=6 * total * width,
            bytes_accessed=24 * total * width,
        ),
        name="recurrence_forward",
    )(meta, xy, xy, vec, w)


def rec_backward(meta, dm, xy, sp, pa, px, xc, vec, wt, tile):
    total, width = dm.shape
    steps = total // tile
    block = pl.BlockSpec((tile, width), lambda i, m: ((steps - 1 - i) ^ m[0], 0))
    right = pl.BlockSpec((tile, width), lambda i, m: ((steps - 1 - i) ^ m[0], 1))
    whole = lambda v: pl.BlockSpec(v.shape, lambda i, m: (0, 0))
    return pl.pallas_call(
        rec_bwd_kernel,
        grid_spec=pltpu.PrefetchScalarGridSpec(
            num_scalar_prefetch=1,
            grid=(steps,),
            in_specs=[block, right, block, block, block, block, block, whole(vec), whole(wt)],
            out_specs=[
                pl.BlockSpec((tile, 2 * width), lambda i, m: ((steps - 1 - i) ^ m[0], 0)),
                pl.BlockSpec((width, 2 * width), lambda i, m: (0, 0)),
                pl.BlockSpec((64, width), lambda i, m: (0, 0)),
            ],
            scratch_shapes=[
                pltpu.VMEM((tile + 8, width), F32),
                pltpu.VMEM((tile, 2 * width), BF16),
                pltpu.VMEM((8, width), F32),
            ],
        ),
        out_shape=[
            jax.ShapeDtypeStruct((total, 2 * width), BF16),
            jax.ShapeDtypeStruct((width, 2 * width), F32),
            jax.ShapeDtypeStruct((64, width), F32),
        ],
        compiler_params=pltpu.CompilerParams(vmem_limit_bytes=32 << 20),
        cost_estimate=pl.CostEstimate(
            flops=180 * total * width + 8 * total * width * width,
            transcendentals=6 * total * width,
            bytes_accessed=30 * total * width,
        ),
        name="recurrence_backward",
    )(meta, dm, xy, sp, pa, px, xc, xy, vec, wt)


def dot32(one, two):
    return jnp.dot(one, two, preferred_element_type=F32)


def columns_of(width, most):
    return next(n for n in range(min(width, most), 0, -128) if width % n == 0)


def store_blocks(step, value_ref, outs, rows):
    per = value_ref.shape[0] // rows
    for n, out in enumerate(outs):

        @pl.when(step == n // per)
        def _(n=n, out=out):
            out[...] = value_ref[(n % per) * rows : (n % per + 1) * rows, :]


def blocks_kernel(flip, a_ref, w_ref, *rest):
    outs, value = rest[:-1], rest[-1]
    model = outs[0].shape[1]
    wide = columns_of(model, 512)
    a = a_ref[...]
    for at in range(0, model, wide):
        if flip:
            part = back_product(a, w_ref[at : at + wide, :])
        else:
            part = dot32(a, w_ref[:, at : at + wide])
        value[:, at : at + wide] = part.astype(BF16)
    store_blocks(pl.program_id(0), value, outs, outs[0].shape[0])


def product_blocks(a, w, flip):
    total, deep = a.shape
    model = w.shape[0] if flip else w.shape[1]
    tile, rows = total // 4, total // 8
    return pl.pallas_call(
        functools.partial(blocks_kernel, flip),
        grid=(4,),
        in_specs=[pl.BlockSpec((tile, deep), lambda i: (i, 0)), pl.BlockSpec(w.shape, lambda i: (0, 0))],
        out_specs=[pl.BlockSpec((rows, model), lambda i: (0, 0))] * 8,
        out_shape=[jax.ShapeDtypeStruct((rows, model), BF16)] * 8,
        scratch_shapes=[pltpu.VMEM((tile, model), BF16)],
        compiler_params=pltpu.CompilerParams(vmem_limit_bytes=44 << 20),
        cost_estimate=pl.CostEstimate(
            flops=2 * total * deep * model,
            transcendentals=0,
            bytes_accessed=2 * (total * deep + w.size + total * model),
        ),
        name="product_blocks",
    )(a, w)


def join_pieces(step, pieces, all_ref):
    rows = pieces[0].shape[0]
    per = all_ref.shape[0] // rows
    for n, piece in enumerate(pieces):

        @pl.when(step == n // per)
        def _(n=n, piece=piece):
            all_ref[(n % per) * rows : (n % per + 1) * rows, :] = piece[...]


def pieces_kernel(flip, *refs):
    pieces, (w_ref, all_ref, out_ref) = refs[:8], refs[8:]
    join_pieces(pl.program_id(0), pieces, all_ref)
    a = all_ref[...]
    wide = columns_of(out_ref.shape[1], 384)
    for at in range(0, out_ref.shape[1], wide):
        if flip:
            out_ref[:, at : at + wide] = back_product(a, w_ref[at : at + wide, :])
        else:
            out_ref[:, at : at + wide] = dot32(a, w_ref[:, at : at + wide])


def pieces_product(pieces, w, flip):
    rows, deep = pieces[0].shape
    total, tile = 8 * rows, 2 * rows
    cols = w.shape[0] if flip else w.shape[1]
    once = lambda v: pl.BlockSpec(v.shape, lambda i: (0, 0), pipeline_mode=pl.Buffered(1))
    return pl.pallas_call(
        functools.partial(pieces_kernel, flip),
        grid=(4,),
        in_specs=[once(v) for v in pieces] + [once(w)],
        out_specs=[pl.BlockSpec((tile, deep), lambda i: (i, 0)), pl.BlockSpec((tile, cols), lambda i: (i, 0))],
        out_shape=[jax.ShapeDtypeStruct((total, deep), BF16), jax.ShapeDtypeStruct((total, cols), F32)],
        compiler_params=pltpu.CompilerParams(vmem_limit_bytes=44 << 20),
        cost_estimate=pl.CostEstimate(
            flops=2 * total * deep * cols, transcendentals=0, bytes_accessed=4 * total * (deep + cols) + 2 * w.size
        ),
        name="pieces_product",
    )(*pieces, w)


def ff_kernel(*refs):
    pieces, (cot_ref, wg_ref, wu_ref, wd_ref, x_ref, hidden_ref, dgt_ref, dup_ref), rest = refs[:8], refs[8:16], refs[16:]
    outs, value = rest[:-1], rest[-1]
    half, model = wd_ref.shape
    narrow, wide = columns_of(half, 256), columns_of(model, 512)
    join_pieces(pl.program_id(0), pieces, x_ref)
    x, cot = x_ref[...], cot_ref[...]
    for at in range(0, half, narrow):
        gt = dot32(x, wg_ref[:, at : at + narrow])
        up = dot32(x, wu_ref[:, at : at + narrow])
        dh = back_product(cot, wd_ref[at : at + narrow, :])
        act, slope = gelu_both(gt)
        hidden_ref[:, at : at + narrow] = (act * up).astype(BF16)
        dgt_ref[:, at : at + narrow] = (dh * up * slope).astype(BF16)
        dup_ref[:, at : at + narrow] = (dh * act).astype(BF16)
    d_gt, d_up = dgt_ref[...], dup_ref[...]
    for at in range(0, model, wide):
        part = back_product(d_gt, wg_ref[at : at + wide, :]) + back_product(d_up, wu_ref[at : at + wide, :])
        value[:, at : at + wide] = part.astype(BF16)
    store_blocks(pl.program_id(0), value, outs, outs[0].shape[0])


def feed_forward(pieces, cot, wgu, wd):
    rows, model = pieces[0].shape
    half = wd.shape[0]
    total, tile = 8 * rows, 2 * rows
    at = lambda cols: pl.BlockSpec((tile, cols), lambda i: (i, 0))
    once = lambda v: pl.BlockSpec(v.shape, lambda i: (0, 0), pipeline_mode=pl.Buffered(1))
    side = lambda n: pl.BlockSpec((model, half), lambda i: (0, n), pipeline_mode=pl.Buffered(1))
    widths = (model, half, half, half)
    return pl.pallas_call(
        ff_kernel,
        grid=(4,),
        in_specs=[once(v) for v in pieces] + [at(model), side(0), side(1), once(wd)],
        out_specs=[at(n) for n in widths] + [pl.BlockSpec((rows, model), lambda i: (0, 0))] * 8,
        out_shape=[jax.ShapeDtypeStruct((total, n), BF16) for n in widths] + [jax.ShapeDtypeStruct((rows, model), BF16)] * 8,
        scratch_shapes=[pltpu.VMEM((tile, model), BF16)],
        compiler_params=pltpu.CompilerParams(vmem_limit_bytes=56 << 20),
        cost_estimate=pl.CostEstimate(
            flops=10 * total * model * half,
            transcendentals=total * half,
            bytes_accessed=2 * (4 * total * model + 3 * half * model + 3 * total * half),
        ),
        name="feed_forward",
    )(*pieces, cot, wgu, wgu, wd)


def norm_back(dv, v, scale):
    return scale * dv - scale * scale * scale * v * jnp.mean(dv * v, axis=-1, keepdims=True)


PLANE = ("y", "x", "c")
STACK = ("zh", "zl")


def tensor_parallel(
    layer_input, lengths, norm1_gain, w_x, w_y, conv_w, conv_b, w_rgate, b_rgate, w_igate, b_igate, lam,
    w_out, norm2_gain, w_gate, w_up, w_down, cot,
):
    rows, model = layer_input.shape
    taps = conv_w.shape[1]
    width = w_rgate.shape[1]
    part = w_out.shape[0]
    channels = 4 * part
    padded = -(-channels // 128) * 128
    extra = padded - channels
    blocks = channels // width
    units = w_down.shape[0]
    core = lax.axis_index("c")
    me = (lax.axis_index("y") * 2 + lax.axis_index("x")) * 2 + core
    meta = jnp.concatenate([me.astype(jnp.int32)[None], lengths[0].astype(jnp.int32)])

    gain1 = norm1_gain.astype(F32)[:, None]
    gain2 = norm2_gain.astype(F32)[:, None]
    rec_plan = tuple(
        tuple((((2 * (t % 2) + z) * 4 + t // 2) * width, width) for z in range(2)) for t in range(8)
    )
    ff_plan = tuple(tuple(((f * 8 + t) * units, units) for f in range(4)) for t in range(8))

    packed_xy = pack_columns(rec_plan, padded, w_x, w_y, gain1)
    wxy = exchange(packed_xy, PLANE)
    conv_w, conv_b, b_rgate, b_igate, lam, w_rgate, w_igate, w_out = lax.optimization_barrier(
        (conv_w, conv_b, b_rgate, b_igate, lam, w_rgate, w_igate, w_out, packed_xy)
    )[:8]
    small = [w_out, conv_w, conv_b[:, None], b_rgate[:, None], b_igate[:, None], lam[:, None], w_rgate, w_igate]
    small_width = sum(v.shape[1] for v in small)
    small = jnp.pad(jnp.concatenate(small, axis=1), ((0, 0), (0, -small_width % 128)))

    stacked = w_parts(small, *STACK)
    xf = layer_input.astype(F32)
    scale1 = lax.rsqrt(jnp.mean(xf * xf, axis=-1, keepdims=True) + NORM_EPS)
    packed_gu = []

    def exchange_units(from_a):
        packed = pack_columns(ff_plan, 4 * units, w_gate, w_up, gain2)
        packed_gu.append(exchange(after(packed, from_a), PLANE).reshape(-1, 8 * units))
        return packed_gu

    xs_pieces = act_gather(after((xf * scale1).astype(BF16), wxy), "x", "y", (), (), exchange_units)
    packed_gu = packed_gu[0]
    wxy_parts = w_parts(wxy.reshape(-1, 2 * padded), *STACK, (stacked[1], xs_pieces[2], xs_pieces[4]))
    upper = lax.axis_index("zh") == core
    keep = [jnp.where(upper, stacked[n], stacked[n + 1]) for n in (0, 2)]
    give = [swap(jnp.where(upper, stacked[n + 1], stacked[n]), "c") for n in (0, 2)]
    place = jnp.stack([lax.axis_index("zl"), core]).astype(jnp.int32)
    wo, gates, vec = place_channels(place, keep + give, model, width, taps)
    lam_all = vec[taps + 3]
    vec = jnp.concatenate([vec[: taps + 1], jax.nn.softplus(-lam_all)[None], vec[taps + 1 : taps + 3]], axis=0)

    wd = lax.all_gather(after(w_down, wxy_parts[3]), STACK, axis=0, tiled=True)
    wxy_parts = wxy_parts[:3] + [after(wxy_parts[3], wo, gates)]
    wxy = w_place(wxy_parts, *STACK).reshape(model, -1)
    wgu = lax.all_gather(packed_gu, STACK, axis=0, tiled=True)
    xs_all, xy = pieces_product(xs_pieces, wxy, False)
    xc, pa, px, before, mixed = rec_forward(meta, xy, vec, gates, rows)
    cot_pieces = act_gather(after(cot, mixed), "x", "y")
    blocks_r = product_blocks(mixed, wo, False)
    cot_all = jnp.concatenate(cot_pieces, axis=0)
    resid = xf + act_scatter(blocks_r, "x", "y", (wd,))
    scale2 = lax.rsqrt(jnp.mean(resid * resid, axis=-1, keepdims=True) + NORM_EPS)
    xs2_pieces = act_gather((resid * scale2).astype(BF16), "x", "y", (cot_all,))
    xs2_all, hidden, d_gt, d_up, *blocks_2 = feed_forward(xs2_pieces, cot_all, wgu, wd)
    d_wd = []

    def down_product(far):
        d_wd.append(row_contract(after(hidden, far), cot_all).astype(BF16))
        return d_wd

    d_un2 = act_scatter(blocks_2, "x", "y", (), (), down_product)
    d_wd = d_wd[0]
    d_resid = cot.astype(F32) + norm_back(d_un2, resid, scale2)
    d_mix = d_resid.astype(BF16)
    d_wd = lax.psum_scatter(d_wd, STACK, scatter_dimension=0, tiled=True)
    d_wg = row_contract(xs2_all, after(d_gt, d_mix)).astype(BF16)
    d_wu = row_contract(xs2_all, after(d_up, d_mix)).astype(BF16)
    d_mix_pieces = act_gather(d_mix, "x", "y", (d_wg,), (d_wu, d_wd))
    d_wg = lax.psum_scatter(d_wg, STACK, scatter_dimension=0, tiled=True)
    d_wu = lax.psum_scatter(d_wu, STACK, scatter_dimension=0, tiled=True)

    d_mix_all, dm = pieces_product(d_mix_pieces, wo, True)
    dxy, d_gates, sums = rec_backward(meta, dm, xy, before, pa, px, xc, vec, gates.T, rows)
    blocks_1 = product_blocks(dxy, wxy, True)
    d_wg = exchange(after(d_wg, blocks_1[0]).reshape(8, -1, 4 * units), PLANE)
    d_wxy = row_contract(xs_all, after(dxy, blocks_1[0])).astype(BF16)
    blocks_o, released = [], []

    def output_blocks(marker):
        released.append(marker)
        released.extend(w_scatter(d_wxy.reshape(2, 2, model // 4, -1), *STACK, (marker,)))
        blocks_o.extend(product_blocks(after(hidden, marker), wd, False))
        return released[2], blocks_o[0]

    d_un = act_scatter(blocks_1, "x", "y", (d_wxy, d_wg), (), None, output_blocks)
    d_input = (d_resid + norm_back(after(d_un, d_wu), xf, scale1)).astype(BF16)
    d_wxy = released[1]().astype(BF16)
    def channels_out(v, kind):
        v = v.astype(kind).reshape(2, 2, part, -1)
        size = (2, 1) + v.shape[2:]
        keep = lax.dynamic_slice(v, (0, core, 0, 0), size)[:, 0]
        send = lax.dynamic_slice(v, (0, 1 - core, 0, 0), size)[:, 0]
        out = jnp.zeros((2,) + keep.shape, kind)
        out = lax.dynamic_update_slice(out, keep[None], (core, 0, 0, 0))
        return lax.dynamic_update_slice(out, swap(send, "c")[None], (1 - core, 0, 0, 0))

    d_wo = channels_out(row_contract(after(mixed, released[0]), d_mix_all)[:channels], BF16)
    sums = jnp.sum(sums.reshape(8, 8, padded), axis=1)
    d_lam_part = -jax.nn.sigmoid(-lam_all) * sums[5]
    d_cols = jnp.concatenate([sums[:5], sums[6:8], d_lam_part[None]], axis=0).T
    row_block = jnp.arange(channels)[:, None] // width
    d_blocks = []
    for g in range(2):
        block = d_gates[:channels, g * padded : g * padded + width]
        for n in range(1, blocks):
            at = g * padded + n * width
            block = jnp.where(row_block == n, d_gates[:channels, at : at + width], block)
        d_blocks.append(block)
    d_small = jnp.concatenate([d_cols[:channels]] + d_blocks, axis=1)
    d_small = channels_out(after(d_small, released[0]), F32)
    ends = []

    def start_channels(far):
        ends.extend(w_scatter(v, *STACK, (far,))[0] for v in (d_wo, d_small))
        return ()

    def end_channels(marker):
        ends.extend(end(marker) for end in ends[:2])
        return ()

    output = act_scatter(blocks_o, "x", "y", (d_input,), (d_wxy,), start_channels, end_channels)
    output = (resid + output).astype(BF16)
    d_wo, d_small = ends[2:]
    d_wxy = exchange(d_wxy.reshape(8, -1, 2 * padded), PLANE)
    d_wx, d_wy, d_gain1 = unpack_columns(rec_plan, d_wxy, None, w_x, w_y, gain1)
    d_wu = exchange(after(d_wu, released[0]).reshape(8, -1, 4 * units), PLANE)
    d_wg, d_wu, d_gain2 = unpack_columns(ff_plan, d_wg, d_wu, w_gate, w_up, gain2)

    d_cw, d_cb, d_br, d_bi, d_lam = d_small[:, :4], d_small[:, 4], d_small[:, 5], d_small[:, 6], d_small[:, 7]
    d_wr, d_wi = d_small[:, 8 : 8 + width], d_small[:, 8 + width : 8 + 2 * width]
    return (
        output, d_input, d_gain1[:, 0], d_wx, d_wy, d_cw, d_cb, d_wr, d_br, d_wi, d_bi, d_lam, d_wo,
        d_gain2[:, 0], d_wg, d_wu, d_wd.astype(F32),
    )


def factored(mesh):
    if tuple(mesh.axis_names) != ("fsdp", "seq") or (mesh.shape["fsdp"], mesh.shape["seq"]) != (4, 8):
        return None
    return Mesh(np.asarray(mesh.devices).reshape((2,) * 5), NAMES)


def solution(mesh):
    small = factored(mesh)
    if small is not None:
        whole, groups = P(NAMES), P(("zh", "zl"))
        return jax.shard_map(
            tensor_parallel,
            mesh=small,
            in_specs=(whole, groups) + (whole,) * 16,
            out_specs=(whole,) * 17,
            check_vma=False,
        )
    in_specs = (
        P(("fsdp", "seq"), None),
        P("fsdp", None),
        P(("fsdp", "seq")),
        P(("fsdp", "seq"), None),
        P(("fsdp", "seq"), None),
        P(("fsdp", "seq"), None),
        P(("fsdp", "seq")),
        P(("fsdp", "seq"), None),
        P(("fsdp", "seq")),
        P(("fsdp", "seq"), None),
        P(("fsdp", "seq")),
        P(("fsdp", "seq")),
        P(("fsdp", "seq"), None),
        P(("fsdp", "seq")),
        P(("fsdp", "seq"), None),
        P(("fsdp", "seq"), None),
        P(("fsdp", "seq"), None),
        P(("fsdp", "seq"), None),
    )
    out_specs = (
        P(("fsdp", "seq"), None),
        P(("fsdp", "seq"), None),
        P(("fsdp", "seq")),
        P(("fsdp", "seq"), None),
        P(("fsdp", "seq"), None),
        P(("fsdp", "seq"), None),
        P(("fsdp", "seq")),
        P(("fsdp", "seq"), None),
        P(("fsdp", "seq")),
        P(("fsdp", "seq"), None),
        P(("fsdp", "seq")),
        P(("fsdp", "seq")),
        P(("fsdp", "seq"), None),
        P(("fsdp", "seq")),
        P(("fsdp", "seq"), None),
        P(("fsdp", "seq"), None),
        P(("fsdp", "seq"), None),
    )
    return jax.shard_map(
        on_device, mesh=mesh, in_specs=in_specs, out_specs=out_specs, check_vma=False
    )
```

```python
import functools

import jax
import jax.numpy as jnp
import numpy as np
from jax import lax
from jax.experimental import pallas as pl
from jax.experimental.pallas import tpu as pltpu
from jax.sharding import Mesh
from jax.sharding import PartitionSpec as P

DECAY_C = 8.0
NORM_EPS = 1e-06


def from_behind(x, axis, by):
    size = lax.axis_size(axis)
    pairs = [(i, i + by) for i in range(size) if 0 <= i + by < size]
    return lax.ppermute(x, axis, pairs)


def carried_in(value, axis, join, neutral, backward):
    count, mine = (lax.axis_size(axis), lax.axis_index(axis))
    pieces = jax.tree.map(lambda part: lax.all_gather(part, axis), value)
    if backward:
        pieces = jax.tree.map(lambda part: part[::-1], pieces)
        mine = count - 1 - mine
    subtotal = jax.tree.map(
        lambda part, zero: jnp.full_like(part, 0) + jnp.asarray(zero, part.dtype), value, neutral
    )

    def step(position, subtotal):
        longer = join(subtotal, jax.tree.map(lambda part: part[position], pieces))
        return jax.tree.map(lambda new, old: jnp.where(position < mine, new, old), longer, subtotal)

    return lax.fori_loop(0, count - 1, step, subtotal)


def rms_apply(value, gain):
    scale = lax.rsqrt(jnp.mean(value * value, axis=-1, keepdims=True) + NORM_EPS)
    return value * scale * gain


def combine(earlier, later):
    return (earlier[0] * later[0], later[0] * earlier[1] + later[1])


def lru_terms(pre_r, pre_i, lam_vec, conv_out, start):
    rate = jax.nn.softplus(-lam_vec)
    log_a = -DECAY_C * jax.nn.sigmoid(pre_r) * rate
    decay = jnp.where(start[:, None], 0.0, jnp.exp(log_a))
    scale = jnp.sqrt(jnp.maximum(-jnp.expm1(2.0 * log_a), 0.2 * DECAY_C * rate))
    scale = jnp.where(start[:, None], 1.0, scale)
    return (decay, scale * jax.nn.sigmoid(pre_i) * conv_out)


def row_contract(left, right):
    return lax.dot_general(
        left, right, (((0,), (0,)), ((), ())), preferred_element_type=jnp.float32
    )


def back_product(grad, weight):
    return lax.dot_general(
        grad, weight, (((1,), (1,)), ((), ())), preferred_element_type=jnp.float32
    )


def split_blocks(value, width):
    return value.reshape(value.shape[0], value.shape[1] // width, width)


def block_product(value, weight):
    width = weight.shape[1]
    mats = weight.reshape(weight.shape[0] // width, width, width)
    result = jnp.einsum(
        "nhi,hij->nhj", split_blocks(value, width), mats, preferred_element_type=jnp.float32
    )
    return result.reshape(value.shape[0], -1)


def block_back(grad, weight):
    width = weight.shape[1]
    mats = weight.reshape(weight.shape[0] // width, width, width)
    result = jnp.einsum(
        "nhj,hij->nhi", split_blocks(grad, width), mats, preferred_element_type=jnp.float32
    )
    return result.reshape(grad.shape[0], -1)


def gate_grad(value, grad, width):
    result = jnp.einsum(
        "nhi,nhj->hij",
        split_blocks(value, width),
        split_blocks(grad, width),
        preferred_element_type=jnp.float32,
    )
    return result.reshape(value.shape[1], width)


def seq_starts(lens_row):
    count = lens_row.shape[0]
    before = jnp.arange(count)[None, :] < jnp.arange(count)[:, None]
    return jnp.sum(jnp.where(before, lens_row[None, :], 0), axis=1)


def seq_masks(lens_row, first, rows, taps):
    starts = seq_starts(lens_row)
    place = first + jnp.arange(rows, dtype=jnp.int32)

    def segment(p):
        return jnp.sum((p[:, None] >= starts[None, :]).astype(jnp.int32), axis=1)

    seg_now = segment(place)
    start = jnp.any(place[:, None] == starts[None, :], axis=1)
    same = jnp.stack(
        [
            ((segment(place - k) == seg_now) & (place - k >= 0)).astype(jnp.float32)
            for k in range(taps)
        ],
        0,
    )
    return (start, same)


def on_device(
    layer_input,
    lengths,
    norm1_gain,
    w_x,
    w_y,
    conv_w,
    conv_b,
    w_rgate,
    b_rgate,
    w_igate,
    b_igate,
    lam,
    w_out,
    norm2_gain,
    w_gate,
    w_up,
    w_down,
    cot,
):
    rows = layer_input.shape[0]
    taps = conv_w.shape[1]
    width = w_rgate.shape[1]
    rim = taps - 1
    index = lax.axis_index("seq")
    start, same = seq_masks(lengths[0], index * rows, rows, taps)
    gain_one, wx, wy, cw, cb, wr, br, wi, bi, lam_all, wo = (
        lax.all_gather(norm1_gain, ("fsdp", "seq"), axis=0, tiled=True),
        lax.all_gather(w_x, ("fsdp", "seq"), axis=0, tiled=True),
        lax.all_gather(w_y, ("fsdp", "seq"), axis=0, tiled=True),
        lax.all_gather(conv_w, ("fsdp", "seq"), axis=0, tiled=True),
        lax.all_gather(conv_b, ("fsdp", "seq"), axis=0, tiled=True),
        lax.all_gather(w_rgate, ("fsdp", "seq"), axis=0, tiled=True),
        lax.all_gather(b_rgate, ("fsdp", "seq"), axis=0, tiled=True),
        lax.all_gather(w_igate, ("fsdp", "seq"), axis=0, tiled=True),
        lax.all_gather(b_igate, ("fsdp", "seq"), axis=0, tiled=True),
        lax.all_gather(lam, ("fsdp", "seq"), axis=0, tiled=True),
        lax.all_gather(w_out, ("fsdp", "seq"), axis=0, tiled=True),
    )
    xf = layer_input.astype(jnp.float32)
    gain1 = gain_one.astype(jnp.float32)
    un = rms_apply(xf, gain1).astype(jnp.bfloat16)
    xb = jnp.dot(un, wx, preferred_element_type=jnp.float32).astype(jnp.bfloat16)
    yb = jnp.dot(un, wy, preferred_element_type=jnp.float32)
    gy = jax.nn.gelu(yb)
    rim_in = from_behind(xb[rows - rim :], "seq", 1)
    extended = jnp.concatenate([rim_in, xb], axis=0).astype(jnp.float32)
    cwf = cw.astype(jnp.float32)
    conv = jnp.broadcast_to(cb.astype(jnp.float32)[None, :], (rows, cwf.shape[0]))
    for k in range(taps):
        conv = conv + cwf[:, k][None, :] * extended[rim - k : rim - k + rows] * same[k][:, None]
    xc = conv.astype(jnp.bfloat16)
    xcf = xc.astype(jnp.float32)
    pre_r = block_product(xc, wr) + br.astype(jnp.float32)[None, :]
    pre_i = block_product(xc, wi) + bi.astype(jnp.float32)[None, :]
    lamf = lam_all.astype(jnp.float32)
    decay, drive = lru_terms(pre_r, pre_i, lamf, xcf, start)
    decay_cum, state_loc = lax.associative_scan(combine, (decay, drive), axis=0)
    zero_vec = jnp.zeros((decay.shape[1],), jnp.float32)
    one_vec = jnp.ones((decay.shape[1],), jnp.float32)
    state_in = carried_in(
        (decay_cum[-1], state_loc[-1]), "seq", combine, (one_vec, zero_vec), False
    )[1]
    state = state_loc + decay_cum * state_in[None, :]
    state_prev = jnp.concatenate([state_in[None, :], state[:-1]], axis=0)
    mixed = (state * gy).astype(jnp.bfloat16)
    resid = xf + jnp.dot(mixed, wo, preferred_element_type=jnp.float32)
    gain_two, wg, wu, wd = (
        lax.all_gather(norm2_gain, ("fsdp", "seq"), axis=0, tiled=True),
        lax.all_gather(w_gate, ("fsdp", "seq"), axis=0, tiled=True),
        lax.all_gather(w_up, ("fsdp", "seq"), axis=0, tiled=True),
        lax.all_gather(w_down, ("fsdp", "seq"), axis=0, tiled=True),
    )
    gain2 = gain_two.astype(jnp.float32)
    un2 = rms_apply(resid, gain2).astype(jnp.bfloat16)
    gate_pre = jnp.dot(un2, wg, preferred_element_type=jnp.float32)
    up_pre = jnp.dot(un2, wu, preferred_element_type=jnp.float32)
    gate_act, gelu_back = jax.vjp(jax.nn.gelu, gate_pre)
    hidden = (gate_act * up_pre).astype(jnp.bfloat16)
    output = (resid + jnp.dot(hidden, wd, preferred_element_type=jnp.float32)).astype(jnp.bfloat16)
    grad = cot.astype(jnp.float32)
    gain_two, wg, wu, wd = (
        lax.all_gather(norm2_gain, ("fsdp", "seq"), axis=0, tiled=True),
        lax.all_gather(w_gate, ("fsdp", "seq"), axis=0, tiled=True),
        lax.all_gather(w_up, ("fsdp", "seq"), axis=0, tiled=True),
        lax.all_gather(w_down, ("fsdp", "seq"), axis=0, tiled=True),
    )
    gain2 = gain_two.astype(jnp.float32)
    d_wd = row_contract(hidden, cot)
    d_hidden = back_product(cot, wd)
    d_gate = gelu_back(d_hidden * up_pre)[0].astype(jnp.bfloat16)
    d_up = (d_hidden * gate_act).astype(jnp.bfloat16)
    d_wg = row_contract(un2, d_gate)
    d_wu = row_contract(un2, d_up)
    d_un2 = back_product(d_gate, wg) + back_product(d_up, wu)
    norm_two_back = jax.vjp(rms_apply, resid, gain2)[1]
    d_resid_norm, d_gain2 = norm_two_back(d_un2)
    mlp_grads = (
        lax.psum_scatter(d_gain2, ("fsdp", "seq"), scatter_dimension=0, tiled=True),
        lax.psum_scatter(d_wg, ("fsdp", "seq"), scatter_dimension=0, tiled=True),
        lax.psum_scatter(d_wu, ("fsdp", "seq"), scatter_dimension=0, tiled=True),
        lax.psum_scatter(d_wd, ("fsdp", "seq"), scatter_dimension=0, tiled=True),
    )
    d_resid = grad + d_resid_norm
    gain_one, wx, wy, cw, cb, wr, br, wi, bi, lam_all, wo = (
        lax.all_gather(norm1_gain, ("fsdp", "seq"), axis=0, tiled=True),
        lax.all_gather(w_x, ("fsdp", "seq"), axis=0, tiled=True),
        lax.all_gather(w_y, ("fsdp", "seq"), axis=0, tiled=True),
        lax.all_gather(conv_w, ("fsdp", "seq"), axis=0, tiled=True),
        lax.all_gather(conv_b, ("fsdp", "seq"), axis=0, tiled=True),
        lax.all_gather(w_rgate, ("fsdp", "seq"), axis=0, tiled=True),
        lax.all_gather(b_rgate, ("fsdp", "seq"), axis=0, tiled=True),
        lax.all_gather(w_igate, ("fsdp", "seq"), axis=0, tiled=True),
        lax.all_gather(b_igate, ("fsdp", "seq"), axis=0, tiled=True),
        lax.all_gather(lam, ("fsdp", "seq"), axis=0, tiled=True),
        lax.all_gather(w_out, ("fsdp", "seq"), axis=0, tiled=True),
    )
    gain1 = gain_one.astype(jnp.float32)
    cwf = cw.astype(jnp.float32)
    lamf = lam_all.astype(jnp.float32)
    d_mix = d_resid.astype(jnp.bfloat16)
    d_wo = row_contract(mixed, d_mix)
    d_mixed = back_product(d_mix, wo)
    d_state = d_mixed * gy
    gelu_y_back = jax.vjp(jax.nn.gelu, yb)[1]
    d_yb = gelu_y_back(d_mixed * state)[0].astype(jnp.bfloat16)
    next_decay = jnp.concatenate([decay[1:], one_vec[None, :]], axis=0)
    decay_after, adjoint_loc = lax.associative_scan(
        combine, (next_decay, d_state), reverse=True, axis=0
    )
    send_decay = decay[0] * decay_after[0]
    send_adjoint = decay[0] * adjoint_loc[0]
    adjoint_in = carried_in((send_decay, send_adjoint), "seq", combine, (one_vec, zero_vec), True)[
        1
    ]
    adjoint = adjoint_loc + decay_after * adjoint_in[None, :]

    def local_lru(pr, pi, lv, cv):
        return lru_terms(pr, pi, lv, cv, start)

    lru_back = jax.vjp(local_lru, pre_r, pre_i, lamf, xcf)[1]
    d_pre_r, d_pre_i, d_lam, d_xc_local = lru_back((adjoint * state_prev, adjoint))
    d_pr = d_pre_r.astype(jnp.bfloat16)
    d_pi = d_pre_i.astype(jnp.bfloat16)
    d_wr = gate_grad(xc, d_pr, width)
    d_wi = gate_grad(xc, d_pi, width)
    d_br = jnp.sum(d_pr.astype(jnp.float32), axis=0)
    d_bi = jnp.sum(d_pi.astype(jnp.float32), axis=0)
    d_xc = d_xc_local + block_back(d_pr, wr) + block_back(d_pi, wi)
    d_cb = jnp.sum(d_xc, axis=0)
    d_cw = jnp.stack(
        [
            jnp.sum(d_xc * extended[rim - k : rim - k + rows] * same[k][:, None], axis=0)
            for k in range(taps)
        ],
        axis=1,
    )
    d_extended = jnp.zeros((rows + rim, d_xc.shape[1]), jnp.float32)
    for k in range(taps):
        d_extended = d_extended + jnp.pad(
            d_xc * cwf[:, k][None, :] * same[k][:, None], ((rim - k, k), (0, 0))
        )
    rim_back = from_behind(d_extended[:rim], "seq", -1)
    d_xb = (d_extended[rim:] + jnp.pad(rim_back, ((rows - rim, 0), (0, 0)))).astype(jnp.bfloat16)
    d_wx = row_contract(un, d_xb)
    d_wy = row_contract(un, d_yb)
    d_un = back_product(d_xb, wx) + back_product(d_yb, wy)
    norm_one_back = jax.vjp(rms_apply, xf, gain1)[1]
    d_x_norm, d_gain1 = norm_one_back(d_un)
    d_input = (d_resid + d_x_norm).astype(jnp.bfloat16)
    block_grads = (
        lax.psum_scatter(d_gain1, ("fsdp", "seq"), scatter_dimension=0, tiled=True),
        lax.psum_scatter(d_wx, ("fsdp", "seq"), scatter_dimension=0, tiled=True),
        lax.psum_scatter(d_wy, ("fsdp", "seq"), scatter_dimension=0, tiled=True),
        lax.psum_scatter(d_cw, ("fsdp", "seq"), scatter_dimension=0, tiled=True),
        lax.psum_scatter(d_cb, ("fsdp", "seq"), scatter_dimension=0, tiled=True),
        lax.psum_scatter(d_wr, ("fsdp", "seq"), scatter_dimension=0, tiled=True),
        lax.psum_scatter(d_br, ("fsdp", "seq"), scatter_dimension=0, tiled=True),
        lax.psum_scatter(d_wi, ("fsdp", "seq"), scatter_dimension=0, tiled=True),
        lax.psum_scatter(d_bi, ("fsdp", "seq"), scatter_dimension=0, tiled=True),
        lax.psum_scatter(d_lam, ("fsdp", "seq"), scatter_dimension=0, tiled=True),
        lax.psum_scatter(d_wo, ("fsdp", "seq"), scatter_dimension=0, tiled=True),
    )
    return (
        output,
        d_input,
        block_grads[0],
        block_grads[1],
        block_grads[2],
        block_grads[3],
        block_grads[4],
        block_grads[5],
        block_grads[6],
        block_grads[7],
        block_grads[8],
        block_grads[9],
        block_grads[10],
        mlp_grads[0],
        mlp_grads[1],
        mlp_grads[2],
        mlp_grads[3],
    )


NAMES = ("zh", "zl", "y", "x", "c")
F32 = jnp.float32
BF16 = jnp.bfloat16
GELU_C = 0.7978845608
GELU_K = 0.044715


def after(v, *first):
    return lax.optimization_barrier((v,) + first)[0]


def swap(v, name):
    return lax.ppermute(v, name, [(0, 1), (1, 0)])


def add16(one, two):
    return (one.astype(F32) + two.astype(F32)).astype(BF16)


def act_gather(v, a, b, second=(), third=(), during=None):
    h = v.shape[0] // 2
    near, from_a, from_b = swap(v, "c"), swap(v, a), swap(v, b)
    from_a, from_b, near = lax.optimization_barrier((from_a, from_b, near) + tuple(second))[:3]
    far0, far1 = swap(from_a[:h], b), swap(from_b[h:], a)
    near_a, near_b = swap(from_a, "c"), swap(from_b, "c")
    if during is not None:
        third = tuple(third) + tuple(during(from_a))
    far0, far1, near_a, near_b = lax.optimization_barrier((far0, far1, near_a, near_b) + tuple(third))[:4]
    far = jnp.concatenate([far0, far1], axis=0)
    return [v, near, from_a, near_a, from_b, near_b, far, swap(far, "c")]


def act_scatter(blocks, a, b, second=(), third=(), during=None, last=None):
    far, to_a, to_b = [add16(blocks[k], swap(blocks[k + 1], "c")) for k in (6, 2, 4)]
    far = after(far, *second)
    own = blocks[0].astype(F32) + swap(blocks[1], "c").astype(F32)
    h = far.shape[0] // 2
    in_b, in_a = swap(far[:h], b), swap(far[h:], a)
    if during is not None:
        third = tuple(third) + tuple(during(far))
    to_a = jnp.concatenate([add16(to_a[:h], in_b), to_a[h:]], axis=0)
    to_b = jnp.concatenate([to_b[:h], add16(to_b[h:], in_a)], axis=0)
    to_a, to_b = lax.optimization_barrier((to_a, to_b) + tuple(third))[:2]
    from_a, from_b = swap(to_a, a), swap(to_b, b)
    if last is not None:
        from_a, from_b = lax.optimization_barrier((from_a, from_b) + tuple(last(to_a)))[:2]
    return own + from_a.astype(F32) + from_b.astype(F32)


def w_parts(v, w1, w2, second=()):
    from_1, from_2 = lax.optimization_barrier((swap(v, w1), swap(v, w2)) + tuple(second))[:2]
    return [v, from_1, from_2, swap(from_1, w2)]


def w_place(parts, w1, w2):
    i1, i2 = lax.axis_index(w1), lax.axis_index(w2)
    out = jnp.zeros((2, 2) + parts[0].shape, parts[0].dtype)
    tail = (0,) * parts[0].ndim
    for part, j1, j2 in zip(parts, (i1, 1 - i1, i1, 1 - i1), (i2, i2, 1 - i2, 1 - i2)):
        out = lax.dynamic_update_slice(out, part[None, None], (j1, j2) + tail)
    return out


def w_scatter(v, w1, w2, hold=()):
    i1, i2 = lax.axis_index(w1), lax.axis_index(w2)

    def get(j1, j2):
        return lax.dynamic_slice(v, (j1, j2) + (0,) * (v.ndim - 2), (1, 1) + v.shape[2:])[0, 0]

    to_other, to_own = swap(get(1 - i1, 1 - i2), w2), swap(get(i1, 1 - i2), w2)
    to_other, to_own = lax.optimization_barrier((to_other, to_own) + tuple(hold))[:2]
    other = (get(1 - i1, i2).astype(F32) + to_other.astype(F32)).astype(v.dtype)
    own = get(i1, i2).astype(F32) + to_own.astype(F32)
    received = swap(other, w1)
    return lambda *late: own + after(received, *late).astype(F32), other


def pack_kernel(plan, a_ref, b_ref, gain_ref, out_ref):
    half = out_ref.shape[2] // 2
    for first, ref in ((0, a_ref), (half, b_ref)):
        scaled = (ref[...].astype(F32) * gain_ref[...]).astype(BF16)
        for dest, pieces in enumerate(plan):
            at = first
            for source, size in pieces:
                out_ref[dest, :, at : at + size] = scaled[:, source : source + size]
                at += size
            if at < first + half:
                out_ref[dest, :, at : first + half] = jnp.zeros((scaled.shape[0], first + half - at), BF16)


def unpack_kernel(plan, ga_ref, gb_ref, a_ref, b_ref, gain_ref, da_ref, db_ref, dgain_ref):
    total = jnp.zeros(dgain_ref.shape, F32)
    for grad_ref, ref, out in ((ga_ref, a_ref, da_ref), (gb_ref, b_ref, db_ref)):
        for dest, pieces in enumerate(plan):
            at = 0
            for source, size in pieces:
                piece = grad_ref[dest, :, at : at + size].astype(F32)
                out[:, source : source + size] = piece * gain_ref[...]
                weight = ref[:, source : source + size].astype(F32)
                total = total + jnp.sum(piece * weight, axis=1, keepdims=True)
                at += size
    dgain_ref[...] = total


def pack_columns(plan, half, one, two, gain):
    return pl.pallas_call(
        functools.partial(pack_kernel, plan),
        out_shape=jax.ShapeDtypeStruct((8, one.shape[0], 2 * half), BF16),
        compiler_params=pltpu.CompilerParams(vmem_limit_bytes=24 << 20),
        cost_estimate=pl.CostEstimate(flops=4 * one.size, transcendentals=0, bytes_accessed=8 * one.size),
        name="pack_columns",
    )(one, two, gain)


def unpack_columns(plan, grad_one, grad_two, one, two, gain):
    half = grad_one.shape[2] if grad_two is not None else grad_one.shape[2] // 2
    rows, cols = one.shape
    whole = lambda *shape: pl.BlockSpec(shape, lambda i: (0,) * len(shape))
    grads = [
        pl.BlockSpec((8, rows, half), lambda i: (0, 0, 0)),
        pl.BlockSpec((8, rows, half), lambda i: (0, 0, 0 if grad_two is not None else 1)),
    ]
    shape = jax.ShapeDtypeStruct(one.shape, F32)
    return pl.pallas_call(
        functools.partial(unpack_kernel, plan),
        grid=(1,),
        in_specs=grads + [whole(rows, cols), whole(rows, cols), whole(rows, 1)],
        out_specs=[whole(rows, cols), whole(rows, cols), whole(rows, 1)],
        out_shape=[shape, shape, jax.ShapeDtypeStruct((rows, 1), F32)],
        compiler_params=pltpu.CompilerParams(vmem_limit_bytes=32 << 20),
        cost_estimate=pl.CostEstimate(flops=8 * one.size, transcendentals=0, bytes_accessed=16 * one.size),
        name="unpack_columns",
    )(grad_one, grad_one if grad_two is None else grad_two, one, two, gain)


def exchange(v, tp):
    return lax.all_to_all(v, tp, split_axis=0, concat_axis=0, tiled=True)


def neg_expm1(v):
    series = 1.0 + v * (1.0 / 10.0)
    for n in range(9, 1, -1):
        series = 1.0 + v * (1.0 / n) * series
    return jnp.where(v > -0.5, -v * series, 1.0 - jnp.exp(v))


def gate_terms(pa, px, rate, start):
    sr = jax.nn.sigmoid(pa)
    si = jax.nn.sigmoid(px)
    la = -DECAY_C * sr * rate
    decay = jnp.where(start, 0.0, jnp.exp(la))
    e2 = neg_expm1(2.0 * la)
    floor = 0.2 * DECAY_C * rate
    scale = jnp.where(start, 1.0, jnp.sqrt(jnp.maximum(e2, floor)))
    return sr, si, decay, e2, floor, scale


def gelu(v):
    return 0.5 * v * (1.0 + jnp.tanh(GELU_C * (v + GELU_K * v * v * v)))


def gelu_both(v):
    t = jnp.tanh(GELU_C * (v + GELU_K * v * v * v))
    half = 0.5 * (1.0 + t)
    return v * half, half + 0.5 * v * (1.0 - t * t) * GELU_C * (1.0 + 3.0 * GELU_K * v * v)


def scan_tile(decay, drive, into):
    row = lax.broadcasted_iota(jnp.int32, decay.shape, 0)
    for by in (1, 2, 4):
        keep = row >= by
        drive = jnp.where(keep, decay * pltpu.roll(drive, by, 0) + drive, drive)
        decay = jnp.where(keep, decay * pltpu.roll(decay, by, 0), decay)
    return decay * into + drive


def scan_tile_back(decay, drive, into):
    row = lax.broadcasted_iota(jnp.int32, decay.shape, 0)
    for by in (1, 2, 4):
        keep = row < 8 - by
        drive = jnp.where(keep, decay * pltpu.roll(drive, 8 - by, 0) + drive, drive)
        decay = jnp.where(keep, decay * pltpu.roll(decay, 8 - by, 0), decay)
    return decay * into + drive


STEP = 16


def since_start(meta_ref, place, width):
    at = place + lax.broadcasted_iota(jnp.int32, (STEP, 128), 0)
    since, start = at, 0
    for n in range(1, meta_ref.shape[0] - 1):
        start = start + meta_ref[n]
        since = jnp.where(at >= start, at - start, since)
    return jnp.concatenate([since] * (width // 128), axis=1)


def rec_fwd_kernel(meta_ref, xb_ref, yb_ref, vec_ref, w_ref, xc_ref, pa_ref, px_ref, sp_ref, mixed_ref, ext, carry):
    rows, width = xb_ref.shape
    base = pl.program_id(0) * rows

    @pl.when(pl.program_id(0) == 0)
    def _():
        ext[0:8, :] = jnp.zeros((8, width), F32)
        carry[...] = jnp.zeros_like(carry)

    ext[8 : 8 + rows, :] = xb_ref[...].astype(BF16).astype(F32)

    def conv_step(r, _):
        at = pl.multiple_of(r * STEP, STEP)
        window = ext[pl.ds(at, STEP + 8), :]
        since = since_start(meta_ref, base + at, width)
        total = vec_ref[4:5, :] + vec_ref[0:1, :] * window[8:, :]
        for k in range(1, 4):
            moved = jnp.where(since >= k, window[8 - k : 8 - k + STEP, :], 0.0)
            total = total + vec_ref[k : k + 1, :] * moved
        xc_ref[pl.ds(at, STEP), :] = total.astype(BF16)
        return 0

    lax.fori_loop(0, rows // STEP, conv_step, 0, unroll=2)
    ext[0:8, :] = ext[rows : rows + 8, :]
    xc = xc_ref[...]
    pa_ref[...] = jnp.dot(xc, w_ref[:, :width], preferred_element_type=F32) + vec_ref[6:7, :]
    px_ref[...] = jnp.dot(xc, w_ref[:, width:], preferred_element_type=F32) + vec_ref[7:8, :]
    top = lax.broadcasted_iota(jnp.int32, (8, width), 0) == 0

    def scan_step(r, held):
        here = pl.ds(pl.multiple_of(r * STEP, STEP), STEP)
        start = since_start(meta_ref, base + r * STEP, width) == 0
        _, si, decay, _, _, scale = gate_terms(pa_ref[here, :], px_ref[here, :], vec_ref[5:6, :], start)
        drive = scale * si * xc_ref[here, :].astype(F32)
        states, before = [], []
        for part in range(0, STEP, 8):
            now = scan_tile(decay[part : part + 8], drive[part : part + 8], held)
            states.append(now)
            before.append(jnp.where(top, held, pltpu.roll(now, 1, 0)))
            held = jnp.broadcast_to(now[7:8, :], (8, width))
        sp_ref[here, :] = jnp.concatenate(before, axis=0)
        mixed_ref[here, :] = (jnp.concatenate(states, axis=0) * gelu(yb_ref[here, :])).astype(BF16)
        return held

    carry[...] = lax.fori_loop(0, rows // STEP, scan_step, carry[...], unroll=2)


def rec_bwd_kernel(
    meta_ref, dm_ref, yb_ref, sp_ref, pa_ref, px_ref, xc_ref, xb_ref, vec_ref, wt_ref,
    dxy_ref, dw_ref, sum_ref, ext, dp, carry,
):
    rows, width = xb_ref.shape
    base = (pl.num_programs(0) - 1 - pl.program_id(0)) * rows

    @pl.when(pl.program_id(0) == 0)
    def _():
        ext[rows : rows + 8, :] = jnp.zeros((8, width), F32)
        carry[...] = jnp.zeros_like(carry)
        dw_ref[...] = jnp.zeros_like(dw_ref)
        sum_ref[...] = jnp.zeros_like(sum_ref)

    row = lax.broadcasted_iota(jnp.int32, (8, width), 0)
    steps = rows // STEP

    def fold(v):
        return v[0:8, :] + v[8:16, :]

    def scan_step(i, state):
        held, s_rate, s_r, s_i = state
        at = pl.multiple_of((steps - 1 - i) * STEP, STEP)
        here = pl.ds(at, STEP)
        start = since_start(meta_ref, base + at, width) == 0
        rate = vec_ref[5:6, :]
        sr, si, decay, e2, floor, scale = gate_terms(pa_ref[here, :], px_ref[here, :], rate, start)
        xc = xc_ref[here, :].astype(F32)
        before = sp_ref[here, :]
        gate = si * xc
        now = decay * before + scale * gate
        dm = dm_ref[here, :]
        act, slope = gelu_both(yb_ref[here, :])
        dxy_ref[here, width:] = (dm * now * slope).astype(BF16)
        dstate = dm * act
        parts = []
        for part in range(STEP - 8, -1, -8):
            here_decay = decay[part : part + 8]
            coef = jnp.where(row == 7, 1.0, pltpu.roll(here_decay, 7, 0))
            adj = scan_tile_back(coef, dstate[part : part + 8], held)
            held = jnp.broadcast_to((here_decay * adj)[0:1, :], (8, width))
            parts.append(adj)
        adj = jnp.concatenate(parts[::-1], axis=0)
        d_scale = adj * gate
        d_half = jnp.where(start, 0.0, d_scale * 0.5 / scale)
        share = jnp.where(e2 > floor, 1.0, jnp.where(e2 == floor, 0.5, 0.0))
        kept = adj * scale
        d_la = decay * (adj * before - 2.0 * decay * d_half * share)
        d_rate = -DECAY_C * sr * d_la + (0.2 * DECAY_C) * d_half * (1.0 - share)
        d_pa = (-DECAY_C * rate * d_la * sr * (1.0 - sr)).astype(BF16)
        d_px = (kept * xc * si * (1.0 - si)).astype(BF16)
        dp[here, :width] = d_pa
        dp[here, width:] = d_px
        ext[here, :] = kept * si
        return held, s_rate + fold(d_rate), s_r + fold(d_pa.astype(F32)), s_i + fold(d_px.astype(F32))

    held, s_rate, s_r, s_i = lax.fori_loop(
        0, steps, scan_step, (carry[...], sum_ref[40:48, :], sum_ref[48:56, :], sum_ref[56:64, :]), unroll=2
    )
    carry[...] = held
    sum_ref[40:48, :] = s_rate
    sum_ref[48:56, :] = s_r
    sum_ref[56:64, :] = s_i
    ext[0:rows, :] += jnp.dot(dp[...], wt_ref[...], preferred_element_type=F32)
    dw_ref[...] += row_contract(xc_ref[...], dp[...])

    def conv_step(r, sums):
        at = pl.multiple_of(r * STEP, STEP)
        window = ext[pl.ds(at, STEP + 8), :]
        xb = xb_ref[pl.ds(at, STEP), :].astype(BF16).astype(F32)
        total = jnp.zeros((STEP, width), F32)
        new = []
        for k in range(4):
            moved = window[k : k + STEP, :]
            if k:
                moved = jnp.where(since_start(meta_ref, base + at + k, width) >= k, moved, 0.0)
            total = total + vec_ref[k : k + 1, :] * moved
            new.append(sums[k] + fold(moved * xb))
        new.append(sums[4] + fold(window[:STEP, :]))
        dxy_ref[pl.ds(at, STEP), :width] = total.astype(BF16)
        return tuple(new)

    sums = lax.fori_loop(0, steps, conv_step, tuple(sum_ref[8 * q : 8 * q + 8, :] for q in range(5)), unroll=2)
    for q in range(5):
        sum_ref[8 * q : 8 * q + 8, :] = sums[q]
    ext[rows : rows + 8, :] = ext[0:8, :]


def place_kernel(width, taps, meta_ref, *refs):
    parts, (wo_ref, gates_ref, vec_ref, cols) = refs[:4], refs[4:]
    part, model = parts[0].shape[0], wo_ref.shape[1]
    padded = wo_ref.shape[0]
    zl, core = meta_ref[0], meta_ref[1]
    lanes = cols.shape[1]
    wo_ref[4 * part :, :] = jnp.zeros((padded - 4 * part, model), BF16)
    gates_ref[...] = jnp.zeros_like(gates_ref)
    cols[4 * part :, :] = jnp.zeros((padded - 4 * part, lanes), F32)
    for n in range(4):
        here_zl = zl if n % 2 == 0 else 1 - zl
        half = core if n < 2 else 1 - core
        at = pl.multiple_of((here_zl * 2 + half) * part, STEP)
        wo_ref[pl.ds(at, part), :] = parts[n][:, :model]
        rest = parts[n][:, model:]
        cols[pl.ds(at, part), :] = rest[:, :lanes].astype(F32)
        for block in range(2):

            @pl.when(here_zl == block)
            def _(rest=rest, at=at, block=block):
                for g in range(2):
                    source = taps + 4 + g * width
                    target = g * padded + block * width
                    gates_ref[pl.ds(at, part), target : target + width] = rest[:, source : source + width]

    vec_ref[...] = cols[...].T[:8, :]


def place_channels(meta, parts, model, width, taps):
    part = parts[0].shape[0]
    padded = -(-4 * part // 128) * 128
    shape = jax.ShapeDtypeStruct
    return pl.pallas_call(
        functools.partial(place_kernel, width, taps),
        grid_spec=pltpu.PrefetchScalarGridSpec(
            num_scalar_prefetch=1,
            grid=(1,),
            in_specs=[pl.BlockSpec(v.shape, lambda i, m: (0, 0)) for v in parts],
            out_specs=[
                pl.BlockSpec((padded, model), lambda i, m: (0, 0)),
                pl.BlockSpec((padded, 2 * padded), lambda i, m: (0, 0)),
                pl.BlockSpec((8, padded), lambda i, m: (0, 0)),
            ],
            scratch_shapes=[pltpu.VMEM((padded, 128), F32)],
        ),
        out_shape=[shape((padded, model), BF16), shape((padded, 2 * padded), BF16), shape((8, padded), F32)],
        compiler_params=pltpu.CompilerParams(vmem_limit_bytes=24 << 20),
        cost_estimate=pl.CostEstimate(flops=padded * model, transcendentals=0, bytes_accessed=8 * padded * model),
        name="place_channels",
    )(meta, *parts)


def rec_forward(meta, xy, vec, w, tile):
    total, width = xy.shape[0], xy.shape[1] // 2
    block = pl.BlockSpec((tile, width), lambda i, m: (i ^ m[0], 0))
    right = pl.BlockSpec((tile, width), lambda i, m: (i ^ m[0], 1))
    whole = lambda v: pl.BlockSpec(v.shape, lambda i, m: (0, 0))
    return pl.pallas_call(
        rec_fwd_kernel,
        grid_spec=pltpu.PrefetchScalarGridSpec(
            num_scalar_prefetch=1,
            grid=(total // tile,),
            in_specs=[block, right, whole(vec), whole(w)],
            out_specs=[block] * 5,
            scratch_shapes=[pltpu.VMEM((tile + 8, width), F32), pltpu.VMEM((8, width), F32)],
        ),
        out_shape=[jax.ShapeDtypeStruct((total, width), t) for t in (BF16, F32, F32, F32, BF16)],
        compiler_params=pltpu.CompilerParams(vmem_limit_bytes=32 << 20),
        cost_estimate=pl.CostEstimate(
            flops=100 * total * width + 4 * total * width * width,
            transcendentals=6 * total * width,
            bytes_accessed=24 * total * width,
        ),
        name="recurrence_forward",
    )(meta, xy, xy, vec, w)


def rec_backward(meta, dm, xy, sp, pa, px, xc, vec, wt, tile):
    total, width = dm.shape
    steps = total // tile
    block = pl.BlockSpec((tile, width), lambda i, m: ((steps - 1 - i) ^ m[0], 0))
    right = pl.BlockSpec((tile, width), lambda i, m: ((steps - 1 - i) ^ m[0], 1))
    whole = lambda v: pl.BlockSpec(v.shape, lambda i, m: (0, 0))
    return pl.pallas_call(
        rec_bwd_kernel,
        grid_spec=pltpu.PrefetchScalarGridSpec(
            num_scalar_prefetch=1,
            grid=(steps,),
            in_specs=[block, right, block, block, block, block, block, whole(vec), whole(wt)],
            out_specs=[
                pl.BlockSpec((tile, 2 * width), lambda i, m: ((steps - 1 - i) ^ m[0], 0)),
                pl.BlockSpec((width, 2 * width), lambda i, m: (0, 0)),
                pl.BlockSpec((64, width), lambda i, m: (0, 0)),
            ],
            scratch_shapes=[
                pltpu.VMEM((tile + 8, width), F32),
                pltpu.VMEM((tile, 2 * width), BF16),
                pltpu.VMEM((8, width), F32),
            ],
        ),
        out_shape=[
            jax.ShapeDtypeStruct((total, 2 * width), BF16),
            jax.ShapeDtypeStruct((width, 2 * width), F32),
            jax.ShapeDtypeStruct((64, width), F32),
        ],
        compiler_params=pltpu.CompilerParams(vmem_limit_bytes=32 << 20),
        cost_estimate=pl.CostEstimate(
            flops=180 * total * width + 8 * total * width * width,
            transcendentals=6 * total * width,
            bytes_accessed=30 * total * width,
        ),
        name="recurrence_backward",
    )(meta, dm, xy, sp, pa, px, xc, xy, vec, wt)


def dot32(one, two):
    return jnp.dot(one, two, preferred_element_type=F32)


def columns_of(width, most):
    return next(n for n in range(min(width, most), 0, -128) if width % n == 0)


def store_blocks(step, value_ref, outs, rows):
    per = value_ref.shape[0] // rows
    for n, out in enumerate(outs):

        @pl.when(step == n // per)
        def _(n=n, out=out):
            out[...] = value_ref[(n % per) * rows : (n % per + 1) * rows, :]


def blocks_kernel(flip, a_ref, w_ref, *rest):
    outs, value = rest[:-1], rest[-1]
    model = outs[0].shape[1]
    wide = columns_of(model, 512)
    a = a_ref[...]
    for at in range(0, model, wide):
        if flip:
            part = back_product(a, w_ref[at : at + wide, :])
        else:
            part = dot32(a, w_ref[:, at : at + wide])
        value[:, at : at + wide] = part.astype(BF16)
    store_blocks(pl.program_id(0), value, outs, outs[0].shape[0])


def product_blocks(a, w, flip):
    total, deep = a.shape
    model = w.shape[0] if flip else w.shape[1]
    tile, rows = total // 4, total // 8
    return pl.pallas_call(
        functools.partial(blocks_kernel, flip),
        grid=(4,),
        in_specs=[pl.BlockSpec((tile, deep), lambda i: (i, 0)), pl.BlockSpec(w.shape, lambda i: (0, 0))],
        out_specs=[pl.BlockSpec((rows, model), lambda i: (0, 0))] * 8,
        out_shape=[jax.ShapeDtypeStruct((rows, model), BF16)] * 8,
        scratch_shapes=[pltpu.VMEM((tile, model), BF16)],
        compiler_params=pltpu.CompilerParams(vmem_limit_bytes=44 << 20),
        cost_estimate=pl.CostEstimate(
            flops=2 * total * deep * model,
            transcendentals=0,
            bytes_accessed=2 * (total * deep + w.size + total * model),
        ),
        name="product_blocks",
    )(a, w)


def join_pieces(step, pieces, all_ref):
    rows = pieces[0].shape[0]
    per = all_ref.shape[0] // rows
    for n, piece in enumerate(pieces):

        @pl.when(step == n // per)
        def _(n=n, piece=piece):
            all_ref[(n % per) * rows : (n % per + 1) * rows, :] = piece[...]


def pieces_kernel(flip, *refs):
    pieces, (w_ref, all_ref, out_ref) = refs[:8], refs[8:]
    join_pieces(pl.program_id(0), pieces, all_ref)
    a = all_ref[...]
    wide = columns_of(out_ref.shape[1], 384)
    for at in range(0, out_ref.shape[1], wide):
        if flip:
            out_ref[:, at : at + wide] = back_product(a, w_ref[at : at + wide, :])
        else:
            out_ref[:, at : at + wide] = dot32(a, w_ref[:, at : at + wide])


def pieces_product(pieces, w, flip):
    rows, deep = pieces[0].shape
    total, tile = 8 * rows, 2 * rows
    cols = w.shape[0] if flip else w.shape[1]
    once = lambda v: pl.BlockSpec(v.shape, lambda i: (0, 0), pipeline_mode=pl.Buffered(1))
    return pl.pallas_call(
        functools.partial(pieces_kernel, flip),
        grid=(4,),
        in_specs=[once(v) for v in pieces] + [once(w)],
        out_specs=[pl.BlockSpec((tile, deep), lambda i: (i, 0)), pl.BlockSpec((tile, cols), lambda i: (i, 0))],
        out_shape=[jax.ShapeDtypeStruct((total, deep), BF16), jax.ShapeDtypeStruct((total, cols), F32)],
        compiler_params=pltpu.CompilerParams(vmem_limit_bytes=44 << 20),
        cost_estimate=pl.CostEstimate(
            flops=2 * total * deep * cols, transcendentals=0, bytes_accessed=4 * total * (deep + cols) + 2 * w.size
        ),
        name="pieces_product",
    )(*pieces, w)


def ff_kernel(*refs):
    pieces, (cot_ref, wg_ref, wu_ref, wd_ref, x_ref, hidden_ref, dgt_ref, dup_ref), rest = refs[:8], refs[8:16], refs[16:]
    outs, value = rest[:-1], rest[-1]
    half, model = wd_ref.shape
    narrow, wide = columns_of(half, 256), columns_of(model, 512)
    join_pieces(pl.program_id(0), pieces, x_ref)
    x, cot = x_ref[...], cot_ref[...]
    for at in range(0, half, narrow):
        gt = dot32(x, wg_ref[:, at : at + narrow])
        up = dot32(x, wu_ref[:, at : at + narrow])
        dh = back_product(cot, wd_ref[at : at + narrow, :])
        act, slope = gelu_both(gt)
        hidden_ref[:, at : at + narrow] = (act * up).astype(BF16)
        dgt_ref[:, at : at + narrow] = (dh * up * slope).astype(BF16)
        dup_ref[:, at : at + narrow] = (dh * act).astype(BF16)
    d_gt, d_up = dgt_ref[...], dup_ref[...]
    for at in range(0, model, wide):
        part = back_product(d_gt, wg_ref[at : at + wide, :]) + back_product(d_up, wu_ref[at : at + wide, :])
        value[:, at : at + wide] = part.astype(BF16)
    store_blocks(pl.program_id(0), value, outs, outs[0].shape[0])


def feed_forward(pieces, cot, wgu, wd):
    rows, model = pieces[0].shape
    half = wd.shape[0]
    total, tile = 8 * rows, 2 * rows
    at = lambda cols: pl.BlockSpec((tile, cols), lambda i: (i, 0))
    once = lambda v: pl.BlockSpec(v.shape, lambda i: (0, 0), pipeline_mode=pl.Buffered(1))
    side = lambda n: pl.BlockSpec((model, half), lambda i: (0, n), pipeline_mode=pl.Buffered(1))
    widths = (model, half, half, half)
    return pl.pallas_call(
        ff_kernel,
        grid=(4,),
        in_specs=[once(v) for v in pieces] + [at(model), side(0), side(1), once(wd)],
        out_specs=[at(n) for n in widths] + [pl.BlockSpec((rows, model), lambda i: (0, 0))] * 8,
        out_shape=[jax.ShapeDtypeStruct((total, n), BF16) for n in widths] + [jax.ShapeDtypeStruct((rows, model), BF16)] * 8,
        scratch_shapes=[pltpu.VMEM((tile, model), BF16)],
        compiler_params=pltpu.CompilerParams(vmem_limit_bytes=56 << 20),
        cost_estimate=pl.CostEstimate(
            flops=10 * total * model * half,
            transcendentals=total * half,
            bytes_accessed=2 * (4 * total * model + 3 * half * model + 3 * total * half),
        ),
        name="feed_forward",
    )(*pieces, cot, wgu, wgu, wd)


def norm_back(dv, v, scale):
    return scale * dv - scale * scale * scale * v * jnp.mean(dv * v, axis=-1, keepdims=True)


PLANE = ("y", "x", "c")
STACK = ("zh", "zl")


def tensor_parallel(
    layer_input, lengths, norm1_gain, w_x, w_y, conv_w, conv_b, w_rgate, b_rgate, w_igate, b_igate, lam,
    w_out, norm2_gain, w_gate, w_up, w_down, cot,
):
    rows, model = layer_input.shape
    taps = conv_w.shape[1]
    width = w_rgate.shape[1]
    part = w_out.shape[0]
    channels = 4 * part
    padded = -(-channels // 128) * 128
    extra = padded - channels
    blocks = channels // width
    units = w_down.shape[0]
    core = lax.axis_index("c")
    me = (lax.axis_index("y") * 2 + lax.axis_index("x")) * 2 + core
    meta = jnp.concatenate([me.astype(jnp.int32)[None], lengths[0].astype(jnp.int32)])

    gain1 = norm1_gain.astype(F32)[:, None]
    gain2 = norm2_gain.astype(F32)[:, None]
    rec_plan = tuple(
        tuple((((2 * (t % 2) + z) * 4 + t // 2) * width, width) for z in range(2)) for t in range(8)
    )
    ff_plan = tuple(tuple(((f * 8 + t) * units, units) for f in range(4)) for t in range(8))

    packed_xy = pack_columns(rec_plan, padded, w_x, w_y, gain1)
    wxy = exchange(packed_xy, PLANE)
    conv_w, conv_b, b_rgate, b_igate, lam, w_rgate, w_igate, w_out = lax.optimization_barrier(
        (conv_w, conv_b, b_rgate, b_igate, lam, w_rgate, w_igate, w_out, packed_xy)
    )[:8]
    small = [w_out, conv_w, conv_b[:, None], b_rgate[:, None], b_igate[:, None], lam[:, None], w_rgate, w_igate]
    small_width = sum(v.shape[1] for v in small)
    small = jnp.pad(jnp.concatenate(small, axis=1), ((0, 0), (0, -small_width % 128)))

    stacked = w_parts(small, *STACK)
    xf = layer_input.astype(F32)
    scale1 = lax.rsqrt(jnp.mean(xf * xf, axis=-1, keepdims=True) + NORM_EPS)
    packed_gu = []

    def exchange_units(from_a):
        packed = pack_columns(ff_plan, 4 * units, w_gate, w_up, gain2)
        packed_gu.append(exchange(after(packed, from_a), PLANE).reshape(-1, 8 * units))
        return packed_gu

    xs_pieces = act_gather(after((xf * scale1).astype(BF16), wxy), "x", "y", (), (), exchange_units)
    packed_gu = packed_gu[0]
    wxy_parts = w_parts(wxy.reshape(-1, 2 * padded), *STACK, (stacked[1], xs_pieces[2], xs_pieces[4]))
    upper = lax.axis_index("zh") == core
    keep = [jnp.where(upper, stacked[n], stacked[n + 1]) for n in (0, 2)]
    give = [swap(jnp.where(upper, stacked[n + 1], stacked[n]), "c") for n in (0, 2)]
    place = jnp.stack([lax.axis_index("zl"), core]).astype(jnp.int32)
    wo, gates, vec = place_channels(place, keep + give, model, width, taps)
    lam_all = vec[taps + 3]
    vec = jnp.concatenate([vec[: taps + 1], jax.nn.softplus(-lam_all)[None], vec[taps + 1 : taps + 3]], axis=0)

    wd = lax.all_gather(after(w_down, wxy_parts[3]), STACK, axis=0, tiled=True)
    wxy_parts = wxy_parts[:3] + [after(wxy_parts[3], wo, gates)]
    wxy = w_place(wxy_parts, *STACK).reshape(model, -1)
    wgu = lax.all_gather(packed_gu, STACK, axis=0, tiled=True)
    xs_all, xy = pieces_product(xs_pieces, wxy, False)
    xc, pa, px, before, mixed = rec_forward(meta, xy, vec, gates, rows)
    cot_pieces = act_gather(after(cot, mixed), "x", "y")
    blocks_r = product_blocks(mixed, wo, False)
    cot_all = jnp.concatenate(cot_pieces, axis=0)
    resid = xf + act_scatter(blocks_r, "x", "y", (wd,))
    scale2 = lax.rsqrt(jnp.mean(resid * resid, axis=-1, keepdims=True) + NORM_EPS)
    xs2_pieces = act_gather((resid * scale2).astype(BF16), "x", "y", (cot_all,))
    xs2_all, hidden, d_gt, d_up, *blocks_2 = feed_forward(xs2_pieces, cot_all, wgu, wd)
    d_wd = []

    def down_product(far):
        d_wd.append(row_contract(after(hidden, far), cot_all).astype(BF16))
        return d_wd

    d_un2 = act_scatter(blocks_2, "x", "y", (), (), down_product)
    d_wd = d_wd[0]
    d_resid = cot.astype(F32) + norm_back(d_un2, resid, scale2)
    d_mix = d_resid.astype(BF16)
    d_wd = lax.psum_scatter(d_wd, STACK, scatter_dimension=0, tiled=True)
    d_wg = row_contract(xs2_all, after(d_gt, d_mix)).astype(BF16)
    d_wu = row_contract(xs2_all, after(d_up, d_mix)).astype(BF16)
    d_mix_pieces = act_gather(d_mix, "x", "y", (d_wg,), (d_wu, d_wd))
    d_wg = lax.psum_scatter(d_wg, STACK, scatter_dimension=0, tiled=True)
    d_wu = lax.psum_scatter(d_wu, STACK, scatter_dimension=0, tiled=True)

    d_mix_all, dm = pieces_product(d_mix_pieces, wo, True)
    dxy, d_gates, sums = rec_backward(meta, dm, xy, before, pa, px, xc, vec, gates.T, rows)
    blocks_1 = product_blocks(dxy, wxy, True)
    d_wg = exchange(after(d_wg, blocks_1[0]).reshape(8, -1, 4 * units), PLANE)
    d_wxy = row_contract(xs_all, after(dxy, blocks_1[0])).astype(BF16)
    blocks_o, released = [], []

    def output_blocks(marker):
        released.append(marker)
        released.extend(w_scatter(d_wxy.reshape(2, 2, model // 4, -1), *STACK, (marker,)))
        blocks_o.extend(product_blocks(after(hidden, marker), wd, False))
        return released[2], blocks_o[0]

    d_un = act_scatter(blocks_1, "x", "y", (d_wxy, d_wg), (), None, output_blocks)
    d_input = (d_resid + norm_back(after(d_un, d_wu), xf, scale1)).astype(BF16)
    def channels_out(v, kind):
        v = v.astype(kind).reshape(2, 2, part, -1)
        size = (2, 1) + v.shape[2:]
        keep = lax.dynamic_slice(v, (0, core, 0, 0), size)[:, 0]
        send = lax.dynamic_slice(v, (0, 1 - core, 0, 0), size)[:, 0]
        out = jnp.zeros((2,) + keep.shape, kind)
        out = lax.dynamic_update_slice(out, keep[None], (core, 0, 0, 0))
        return lax.dynamic_update_slice(out, swap(send, "c")[None], (1 - core, 0, 0, 0))

    sums = jnp.sum(sums.reshape(8, 8, padded), axis=1)
    d_lam_part = -jax.nn.sigmoid(-lam_all) * sums[5]
    d_cols = jnp.concatenate([sums[:5], sums[6:8], d_lam_part[None]], axis=0).T
    row_block = jnp.arange(channels)[:, None] // width
    d_blocks = []
    for g in range(2):
        block = d_gates[:channels, g * padded : g * padded + width]
        for n in range(1, blocks):
            at = g * padded + n * width
            block = jnp.where(row_block == n, d_gates[:channels, at : at + width], block)
        d_blocks.append(block)
    d_small = jnp.concatenate([d_cols[:channels]] + d_blocks, axis=1)
    d_wu = exchange(after(d_wu, released[0]).reshape(8, -1, 4 * units), PLANE)
    sent, ends = [], []

    def start_channels(far):
        sent.append(channels_out(row_contract(after(mixed, far), d_mix_all)[:channels], BF16))
        sent.append(channels_out(after(d_small, far), F32))
        return ()

    def end_channels(marker):
        ends.append(released[1](marker).astype(BF16))
        ends.extend(w_scatter(v, *STACK, (marker,))[0]() for v in sent)
        ends.append(after(d_wu, marker))
        return ()

    output = act_scatter(blocks_o, "x", "y", (d_input,), (), start_channels, end_channels)
    output = (resid + output).astype(BF16)
    d_wxy, d_wo, d_small, d_wu = ends
    d_wxy = exchange(d_wxy.reshape(8, -1, 2 * padded), PLANE)
    d_wx, d_wy, d_gain1 = unpack_columns(rec_plan, d_wxy, None, w_x, w_y, gain1)
    d_wg, d_wu, d_gain2 = unpack_columns(ff_plan, d_wg, d_wu, w_gate, w_up, gain2)

    d_cw, d_cb, d_br, d_bi, d_lam = d_small[:, :4], d_small[:, 4], d_small[:, 5], d_small[:, 6], d_small[:, 7]
    d_wr, d_wi = d_small[:, 8 : 8 + width], d_small[:, 8 + width : 8 + 2 * width]
    return (
        output, d_input, d_gain1[:, 0], d_wx, d_wy, d_cw, d_cb, d_wr, d_br, d_wi, d_bi, d_lam, d_wo,
        d_gain2[:, 0], d_wg, d_wu, d_wd.astype(F32),
    )


def factored(mesh):
    if tuple(mesh.axis_names) != ("fsdp", "seq") or (mesh.shape["fsdp"], mesh.shape["seq"]) != (4, 8):
        return None
    return Mesh(np.asarray(mesh.devices).reshape((2,) * 5), NAMES)


def solution(mesh):
    small = factored(mesh)
    if small is not None:
        whole, groups = P(NAMES), P(("zh", "zl"))
        return jax.shard_map(
            tensor_parallel,
            mesh=small,
            in_specs=(whole, groups) + (whole,) * 16,
            out_specs=(whole,) * 17,
            check_vma=False,
        )
    in_specs = (
        P(("fsdp", "seq"), None),
        P("fsdp", None),
        P(("fsdp", "seq")),
        P(("fsdp", "seq"), None),
        P(("fsdp", "seq"), None),
        P(("fsdp", "seq"), None),
        P(("fsdp", "seq")),
        P(("fsdp", "seq"), None),
        P(("fsdp", "seq")),
        P(("fsdp", "seq"), None),
        P(("fsdp", "seq")),
        P(("fsdp", "seq")),
        P(("fsdp", "seq"), None),
        P(("fsdp", "seq")),
        P(("fsdp", "seq"), None),
        P(("fsdp", "seq"), None),
        P(("fsdp", "seq"), None),
        P(("fsdp", "seq"), None),
    )
    out_specs = (
        P(("fsdp", "seq"), None),
        P(("fsdp", "seq"), None),
        P(("fsdp", "seq")),
        P(("fsdp", "seq"), None),
        P(("fsdp", "seq"), None),
        P(("fsdp", "seq"), None),
        P(("fsdp", "seq")),
        P(("fsdp", "seq"), None),
        P(("fsdp", "seq")),
        P(("fsdp", "seq"), None),
        P(("fsdp", "seq")),
        P(("fsdp", "seq")),
        P(("fsdp", "seq"), None),
        P(("fsdp", "seq")),
        P(("fsdp", "seq"), None),
        P(("fsdp", "seq"), None),
        P(("fsdp", "seq"), None),
    )
    return jax.shard_map(
        on_device, mesh=mesh, in_specs=in_specs, out_specs=out_specs, check_vma=False
    )
```
